128 devices in a mesh: tm: 16 (over x, y), batch: 8 (over z, core).
Axes of the slice: x: 4, y: 4, z: 4, core: 2. Of those that a mesh axis runs over, the one named last changes fastest.
Arguments:
- rgb_maps: bfloat16 [32, 64, 16, 16, 128], P('batch', 'tm'), may hold values from -6 to 6
- flow_maps: bfloat16 [32, 64, 16, 16, 128], P('batch', 'tm'), may hold values from -6 to 6
- in_weights: bfloat16 [2, 1152, 128], replicated, may hold values from -0.1875 to 0.1875
- out_weights: bfloat16 [2, 1152, 128], replicated, may hold values from -0.1875 to 0.1875
- decay: float32 [2, 64, 128], P(None, 'tm'), may hold values from 0 to 1, as said below
- skip: float32 [2, 128], replicated, may hold values from 0.5 to 1.5
- proj_in: float32 [128, 2048], replicated, may hold values from -0.5 to 0.5
- proj_gain: float32 [2048], replicated, may hold values from 0.1 to 1.9
- proj_out: bfloat16 [2048, 2048], replicated, may hold values from -0.125 to 0.125
Outputs:
- grad_in: float32 [2, 1152, 128], replicated
- grad_out: float32 [2, 1152, 128], replicated
The draws below stay inside these ranges and needn't reach their ends.
Inputs may be any that keep to these rules, and one draw needn't show every extreme that they name: Every entry of decay is a retention factor between 0 and 1.
All inputs are finite; a program needn't handle non-finite values.
Results may differ from the reference program's by a relative error of at most 0.015.
The reference program's roundings to bfloat16 on the way count: a program that leaves them out, or rounds other values in their place, can miss the bound.
Values may be sent and summed in bfloat16 or wider, within the bound.
No kernel may reach another device: no remote copies, remote signals or barrier semaphores. Data moves between devices by JAX's collectives and lax.ppermute only.
A program may use at most 192 MiB of HBM per device.

```python
import jax
import jax.numpy as jnp
from jax import lax

LAYER_CHANNELS = 128
PROJ = 2048
MAP = 16
CLIP_FRAMES = 64
CLIPS = 32


def draw_decay(key, part):
    random_keys = jax.random.split(jax.random.fold_in(key, 7), 6)
    fast_share = 0.45
    fast_pick = jax.random.uniform(random_keys[0], (2, LAYER_CHANNELS)) < fast_share
    slow_rate = jnp.exp(jax.random.uniform(random_keys[1], (2, LAYER_CHANNELS), minval=jnp.log(0.02), maxval=jnp.log(0.4))) / CLIP_FRAMES
    fast_rate = jnp.exp(jax.random.uniform(random_keys[2], (2, LAYER_CHANNELS), minval=jnp.log(0.06), maxval=jnp.log(0.12)))
    rate_base = jnp.where(fast_pick, fast_rate, slow_rate)
    jitter = jax.random.uniform(random_keys[3], (2, CLIP_FRAMES, LAYER_CHANNELS), minval=0.5, maxval=1.5)
    spike_positions = jax.random.randint(random_keys[4], (2, 4, LAYER_CHANNELS), 0, CLIP_FRAMES)
    frame_numbers = jnp.arange(CLIP_FRAMES)
    spike_mask = jnp.any(frame_numbers[None, :, None, None] == spike_positions[:, None, :, :], axis=2)
    spike_multiplier = jax.random.uniform(random_keys[5], (2, CLIP_FRAMES, LAYER_CHANNELS), minval=0.5, maxval=0.8)
    memory_keep = jnp.exp(-rate_base[:, None, :] * jitter)
    memory_keep = memory_keep * jnp.where(spike_mask, spike_multiplier, 1.0)
    return memory_keep.astype(jnp.float32)


def block_scale(stream_key, shape, cuts, smallest, top_value):
    def one(position, shards_of):
        heights = jax.random.uniform(jax.random.fold_in(jax.random.fold_in(stream_key, 6), position), (shards_of,), jnp.float32, smallest / len(cuts), top_value / len(cuts))
        return jnp.repeat(jnp.exp(heights), shape[position] // shards_of).reshape((-1,) + (1,) * (len(shape) - position - 1))

    level = one(*cuts[0])
    for cut in cuts[1:]:
        level = level * one(*cut)
    return level


def centred(stream_key, dims, deviation, reach, cuts=(), dtype=jnp.bfloat16):
    drawn = jax.random.normal(stream_key, dims, jnp.float32) * deviation
    if len(cuts) > 0:
        drawn = block_scale(stream_key, dims, cuts, -0.22, 0.18) * drawn
    return jnp.clip(drawn, min=-reach, max=reach).astype(dtype)


def setup_inputs(seed: int = 0) -> dict:
    key_list = jax.random.split(jax.random.key(seed), 10)
    rgb_maps = centred(key_list[0], (CLIPS, CLIP_FRAMES, MAP, MAP, LAYER_CHANNELS), 1.0, 6.0, ((0, 8), (1, 16)))
    flow_maps = centred(key_list[1], (CLIPS, CLIP_FRAMES, MAP, MAP, LAYER_CHANNELS), 1.0, 6.0, ((0, 8), (1, 16)))
    in_weights = centred(key_list[2], (2, 9 * LAYER_CHANNELS, LAYER_CHANNELS), (9 * LAYER_CHANNELS) ** -0.5, 0.1875)
    out_weights = centred(key_list[3], (2, 9 * LAYER_CHANNELS, LAYER_CHANNELS), (9 * LAYER_CHANNELS) ** -0.5, 0.1875)
    decay = draw_decay(jax.random.fold_in(key_list[9], 71), 0)
    skip = jnp.clip(jax.random.uniform(key_list[5], (2, LAYER_CHANNELS), jnp.float32, 0.5, 1.5), 0.5, 1.5)
    proj_in = centred(key_list[6], (LAYER_CHANNELS, PROJ), LAYER_CHANNELS ** -0.5, 0.5, (), jnp.float32)
    proj_gain = jnp.clip(1.0 + 0.18 * jax.random.normal(key_list[7], (PROJ,), jnp.float32), 0.1, 1.9)
    proj_out = centred(key_list[8], (PROJ, PROJ), PROJ ** -0.5, 0.125)
    return dict(rgb_maps=rgb_maps, flow_maps=flow_maps, in_weights=in_weights, out_weights=out_weights, decay=decay, skip=skip, proj_in=proj_in, proj_gain=proj_gain, proj_out=proj_out)


LAMBDA_OFF = 0.0051
EPSILON = 1e-05
HIGHEST = lax.Precision.HIGHEST

def patches(feature_maps, flip_sign):
    map_side = feature_maps.shape[-2]
    padding = [(0, 0)] * (feature_maps.ndim - 3) + [(1, 1), (1, 1), (0, 0)]
    padded = jnp.pad(feature_maps, padding)
    pieces = []
    for row_off in range(3):
        for col_off in range(3):
            top_row = 1 + flip_sign * (row_off - 1)
            left_col = 1 + flip_sign * (col_off - 1)
            pieces.append(padded[..., top_row:top_row + map_side, left_col:left_col + map_side, :])
    return jnp.concatenate(pieces, axis=-1)

def convolve(feature_maps, weights, flip_sign):
    stacked = patches(feature_maps, flip_sign)
    flat = stacked.reshape(-1, stacked.shape[-1])
    result = jnp.dot(flat, weights, preferred_element_type=jnp.float32)
    return result.reshape(feature_maps.shape[:-1] + (weights.shape[1],))

def flipped(weights):
    channels = weights.shape[1]
    return weights.reshape(9, channels, channels).transpose(0, 2, 1).reshape(9 * channels, channels)

def weight_product(feature_maps, grads):
    stacked = patches(feature_maps, 1)
    flat = stacked.reshape(-1, stacked.shape[-1])
    return lax.dot_general(flat, grads.reshape(-1, grads.shape[-1]), (((0,), (0,)), ((), ())), preferred_element_type=jnp.float32)

def silu_grad(values):
    sigma = jax.nn.sigmoid(values)
    return sigma * (1.0 + values * (1.0 - sigma))

def view_forward(clip_maps, in_w, out_w, decays, skip_v):
    inputs = convolve(clip_maps, in_w, 1).astype(jnp.bfloat16)

    def advance(carried, pair_in):
        decay_now, input_now = pair_in
        carried = decay_now * carried + input_now.astype(jnp.float32)
        return (carried, carried)
    start_state = jnp.zeros(clip_maps.shape[1:], jnp.float32)
    _, states = lax.scan(advance, start_state, (decays, inputs))
    states_b = states.astype(jnp.bfloat16)
    mixed_out = convolve(states_b, out_w, 1) + skip_v * inputs.astype(jnp.float32)
    return (inputs, states_b, mixed_out)

def batch_norm(values):
    center = lax.optimization_barrier(jnp.mean(values, axis=0))
    centered = values - center
    scale = lax.rsqrt(lax.optimization_barrier(jnp.mean(centered * centered, axis=0)) + EPSILON)
    return (centered * scale, scale)

def reference(rgb_maps, flow_maps, in_weights, out_weights, decay, skip, proj_in, proj_gain, proj_out):
    views = (rgb_maps, flow_maps)
    cell_count = rgb_maps.shape[1] * rgb_maps.shape[2] * rgb_maps.shape[3]
    clip_total = rgb_maps.shape[0]
    pooled_all = []
    for view_idx in range(2):

        def pool_clip(clip_maps, view_idx=view_idx):
            _, _, mixed_out = view_forward(clip_maps, in_weights[view_idx], out_weights[view_idx], decay[view_idx], skip[view_idx])
            return lax.optimization_barrier(jnp.sum(jax.nn.silu(mixed_out), axis=(0, 1, 2))) / cell_count
        pooled_all.append(lax.map(pool_clip, views[view_idx]))
    hidden_x, hidden_s, hidden_n, z_x, z_s, z_n = ([], [], [], [], [], [])
    for view_idx in range(2):
        hidden = jnp.dot(pooled_all[view_idx], proj_in, precision=HIGHEST, preferred_element_type=jnp.float32)
        normed, scale = batch_norm(hidden)
        gained = normed * proj_gain
        relu_b = jnp.maximum(gained, 0.0).astype(jnp.bfloat16)
        z_full = jnp.dot(relu_b, proj_out, preferred_element_type=jnp.float32)
        z_normed, z_scale = batch_norm(z_full)
        hidden_x.append(normed)
        hidden_s.append(scale)
        hidden_n.append(gained)
        z_x.append(z_normed)
        z_s.append(z_scale)
        z_n.append(z_normed.astype(jnp.bfloat16))
    corr = jnp.dot(z_n[0].T, z_n[1], preferred_element_type=jnp.float32) / clip_total
    eye_mask = jnp.arange(corr.shape[0])[:, None] == jnp.arange(corr.shape[1])[None, :]
    dcorr = jnp.where(eye_mask, -2.0 * (1.0 - corr), 2.0 * LAMBDA_OFF * corr)
    zn_rgb = z_n[0].astype(jnp.float32)
    zn_flow = z_n[1].astype(jnp.float32)
    dzn = [jnp.dot(zn_flow, dcorr.T, precision=HIGHEST) / clip_total, jnp.dot(zn_rgb, dcorr, precision=HIGHEST) / clip_total]
    dpooled = []
    for view_idx in range(2):
        grad_zn = dzn[view_idx]
        dz_b = ((grad_zn - lax.optimization_barrier(jnp.mean(grad_zn, axis=0)) - z_x[view_idx] * lax.optimization_barrier(jnp.mean(grad_zn * z_x[view_idx], axis=0))) * z_s[view_idx]).astype(jnp.bfloat16)
        drelu = jnp.dot(dz_b, proj_out.T, preferred_element_type=jnp.float32)
        dxh = jnp.where(hidden_n[view_idx] > 0, drelu, 0.0) * proj_gain
        xh_now = hidden_x[view_idx]
        dhidden = (dxh - lax.optimization_barrier(jnp.mean(dxh, axis=0)) - xh_now * lax.optimization_barrier(jnp.mean(dxh * xh_now, axis=0))) * hidden_s[view_idx]
        dpooled.append(jnp.dot(dhidden, proj_in.T, precision=HIGHEST))
    grads_in, grads_out = ([], [])
    for view_idx in range(2):
        in_w = in_weights[view_idx]
        out_w = out_weights[view_idx]
        decays = decay[view_idx]
        skip_v = skip[view_idx]
        decay_next = jnp.concatenate([decays[1:], jnp.zeros((1, decays.shape[1]), jnp.float32)], axis=0)

        def clip_grads(totals, pair_in, in_w=in_w, out_w=out_w, decays=decays, skip_v=skip_v, decay_next=decay_next):
            clip_maps, dpool = pair_in
            inputs, states_b, mixed_out = view_forward(clip_maps, in_w, out_w, decays, skip_v)
            dmix = dpool / cell_count * silu_grad(mixed_out)
            dmix_b = dmix.astype(jnp.bfloat16)
            out_grad = weight_product(states_b, dmix_b)
            from_out = convolve(dmix_b, flipped(out_w), -1)

            def retreat(carried, pair_back):
                decay_after, source = pair_back
                carried = source + decay_after * carried
                return (carried, carried)
            _, adjoint = lax.scan(retreat, jnp.zeros(clip_maps.shape[1:], jnp.float32), (decay_next, from_out), reverse=True)
            dinput = (adjoint + skip_v * dmix).astype(jnp.bfloat16)
            in_grad = weight_product(clip_maps, dinput)
            return ((totals[0] + in_grad, totals[1] + out_grad), None)
        zero_grad = jnp.zeros(in_w.shape, jnp.float32)
        (in_total, out_total), _ = lax.scan(clip_grads, (zero_grad, zero_grad), (views[view_idx], dpooled[view_idx]))
        grads_in.append(in_total)
        grads_out.append(out_total)
    return (jnp.stack(grads_in), jnp.stack(grads_out))
```

```python
import jax
import jax.numpy as jnp
from jax import lax
from jax.sharding import Mesh
from jax.sharding import PartitionSpec as P

TIME = ("xl", "y")
PLANE = ("xh", "xl")


LAMBDA_OFF = 0.0051
EPSILON = 1e-05
HIGHEST = lax.Precision.HIGHEST


def patches(feature_maps, flip_sign):
    map_side = feature_maps.shape[-2]
    padding = [(0, 0)] * (feature_maps.ndim - 3) + [(1, 1), (1, 1), (0, 0)]
    padded = jnp.pad(feature_maps, padding)
    pieces = []
    for row_off in range(3):
        for col_off in range(3):
            top_row = 1 + flip_sign * (row_off - 1)
            left_col = 1 + flip_sign * (col_off - 1)
            pieces.append(
                padded[..., top_row : top_row + map_side, left_col : left_col + map_side, :]
            )
    return jnp.concatenate(pieces, axis=-1)


def convolve(feature_maps, weights, flip_sign):
    stacked = patches(feature_maps, flip_sign)
    flat = stacked.reshape(-1, stacked.shape[-1])
    result = jnp.dot(flat, weights, preferred_element_type=jnp.float32)
    return result.reshape(feature_maps.shape[:-1] + (weights.shape[1],))


def flipped(weights):
    channels = weights.shape[1]
    return weights.reshape(9, channels, channels).transpose(0, 2, 1).reshape(9 * channels, channels)


def weight_product(feature_maps, grads):
    stacked = patches(feature_maps, 1)
    flat = stacked.reshape(-1, stacked.shape[-1])
    return lax.dot_general(
        flat,
        grads.reshape(-1, grads.shape[-1]),
        (((0,), (0,)), ((), ())),
        preferred_element_type=jnp.float32,
    )


def silu_grad(values):
    sigma = jax.nn.sigmoid(values)
    return sigma * (1.0 + values * (1.0 - sigma))


def swapped(x):
    return lax.ppermute(x, "core", [(0, 1), (1, 0)])


def from_cores(x):
    here, there = x, swapped(x)
    first = lax.axis_index("core") == 0
    return jnp.stack([jnp.where(first, here, there), jnp.where(first, there, here)])


def from_all(x, axes):
    peers = lax.axis_size(axes)
    return lax.all_to_all(jnp.broadcast_to(x[None], (peers, *x.shape)), axes, 0, 0, tiled=True)


def in_parts(x):
    high = lax.reduce_precision(x, 8, 7)
    middle = lax.reduce_precision(x - high, 8, 7)
    low = x - high - middle
    return jnp.concatenate([high, middle, low], axis=-2).astype(jnp.bfloat16)


def clips_to_devices(rgb_maps, flow_maps, decay, half):
    clips, frames, side, _, channels = rgb_maps.shape
    straight = half == 0
    first = jnp.where(straight, rgb_maps, flow_maps)
    second = jnp.where(straight, flow_maps, rgb_maps)
    pieces = jnp.stack([first, second]).reshape(2, clips, frames * side * side, channels)
    parts = in_parts(jnp.where(straight, decay, decay[::-1]))
    parts = jnp.pad(parts, ((0, 0), (0, 16 - 3 * frames), (0, 0)))
    parts = jnp.broadcast_to(parts[:, None], (2, clips, 16, channels))
    sent = jnp.concatenate([pieces, parts], axis=2).reshape(2 * clips, -1, channels)
    got = lax.all_to_all(sent, TIME, 0, 0, tiled=True)
    peers = got.shape[0]
    maps = got[:, : frames * side * side].reshape(peers * frames, side, side, channels)
    parts = got[:, frames * side * side :].astype(jnp.float32)
    parts = parts[:, : 3 * frames].reshape(peers, 3, frames, channels)
    decays = (parts[:, 0] + parts[:, 1] + parts[:, 2]).reshape(peers * frames, channels)
    return maps, decays


def batch_norm(values):
    center = jnp.mean(values, axis=1, keepdims=True)
    centered = values - center
    scale = lax.rsqrt(jnp.mean(centered * centered, axis=1, keepdims=True) + EPSILON)
    return centered * scale, scale


def norm_back(grad, normed, scale):
    mean = jnp.mean(grad, axis=0, keepdims=True)
    along = jnp.mean(grad * normed, axis=0, keepdims=True)
    return (grad - mean - normed * along) * scale


def projector_back(pooled, proj_in, proj_gain, proj_out, view):
    _, clips, channels = pooled.shape
    width = proj_in.shape[1]
    hidden = jnp.dot(
        pooled.reshape(2 * clips, channels), proj_in, precision=HIGHEST, preferred_element_type=jnp.float32
    )
    hidden_x, hidden_s = batch_norm(hidden.reshape(2, clips, width))
    hidden_n = hidden_x * proj_gain
    relu_b = jnp.maximum(hidden_n, 0.0).astype(jnp.bfloat16)
    z = jnp.dot(relu_b.reshape(2 * clips, width), proj_out, preferred_element_type=jnp.float32)
    z_x, z_s = batch_norm(z.reshape(2, clips, width))
    zn = z_x.astype(jnp.bfloat16)
    first = view == 0
    own = jnp.where(first, zn[0], zn[1])
    other = jnp.where(first, zn[1], zn[0])
    own_wide = own.astype(jnp.float32)
    other_wide = other.astype(jnp.float32)
    corr_diag = jnp.sum(own_wide * other_wide, axis=0) / clips
    extra = -2.0 * (1.0 - corr_diag) - 2.0 * LAMBDA_OFF * corr_diag
    gram = lax.dot_general(other, other, (((1,), (1,)), ((), ())), preferred_element_type=jnp.float32)
    spread = jnp.dot(gram, own_wide, precision=HIGHEST, preferred_element_type=jnp.float32)
    dzn = spread * (2.0 * LAMBDA_OFF / (clips * clips)) + other_wide * (extra / clips)
    dz_b = norm_back(
        dzn, jnp.where(first, z_x[0], z_x[1]), jnp.where(first, z_s[0], z_s[1])
    ).astype(jnp.bfloat16)
    drelu = lax.dot_general(dz_b, proj_out, (((1,), (1,)), ((), ())), preferred_element_type=jnp.float32)
    own_x = jnp.where(first, hidden_x[0], hidden_x[1])
    own_s = jnp.where(first, hidden_s[0], hidden_s[1])
    own_n = jnp.where(first, hidden_n[0], hidden_n[1])
    dxh = jnp.where(own_n > 0, drelu, 0.0) * proj_gain
    dhidden = norm_back(dxh, own_x, own_s)
    return dhidden


def summed(grads):
    rows, channels = grads.shape
    core = lax.axis_index("core")
    halves = grads.reshape(2, rows // 2, channels)
    mine = lax.dynamic_index_in_dim(halves, core, 0, False)
    given = lax.dynamic_index_in_dim(halves, 1 - core, 0, False)
    total = mine + swapped(given)
    pieces = total.astype(jnp.bfloat16).reshape(4, rows // 8, channels)
    total = jnp.sum(lax.all_to_all(pieces, "z", 0, 0, tiled=True).astype(jnp.float32), axis=0)
    total = jnp.sum(from_all(total.astype(jnp.bfloat16), "y").astype(jnp.float32), axis=0)
    seen = from_all(total.astype(jnp.bfloat16), PLANE).astype(jnp.float32)
    both = jnp.stack([seen[0] + seen[3], seen[1] + seen[2]]).astype(jnp.bfloat16)
    whole = from_cores(from_all(both, "z"))
    return whole.transpose(2, 0, 1, 3, 4).reshape(2, rows, channels).astype(jnp.float32)


def per_device(
    rgb_maps, flow_maps, in_weights, out_weights, decay, skip, proj_in, proj_gain, proj_out
):
    half = lax.axis_index("xh")
    view = lax.axis_index("xl") ^ half
    clip = lax.axis_index("y")
    batch = lax.axis_index(("z", "core"))
    clips_here = rgb_maps.shape[0]
    maps, decays = clips_to_devices(rgb_maps, flow_maps, decay, half)
    frames, side, _, channels = maps.shape
    cell_count = 2 * frames * side * side
    in_w = lax.dynamic_index_in_dim(in_weights, view, 0, False)
    out_w = lax.dynamic_index_in_dim(out_weights, view, 0, False)
    skip_v = lax.dynamic_index_in_dim(skip, view, 0, False)

    inputs = convolve(maps, in_w, 1).astype(jnp.bfloat16)
    carried = jnp.zeros((side, side, channels), jnp.float32)
    for t in range(frames):
        carried = decays[t] * carried + inputs[t].astype(jnp.float32)
    carried = lax.ppermute(carried, PLANE, [(0, 3), (1, 2)])
    states = []
    for t in range(frames):
        carried = decays[t] * carried + inputs[t].astype(jnp.float32)
        states.append(carried)
    states_b = jnp.stack(states).astype(jnp.bfloat16)
    mixed = convolve(states_b, out_w, 1) + skip_v * inputs.astype(jnp.float32)
    pooled_part = jnp.sum(jax.nn.silu(mixed), axis=(0, 1, 2))

    seen = from_all(from_cores(pooled_part), ("xh", "xl", "y", "z"))
    seen = seen.reshape(2, 2, clips_here, 4, 2, channels)
    views = jnp.stack([seen[0, 0] + seen[1, 1], seen[0, 1] + seen[1, 0]]) / cell_count
    pooled = views.transpose(0, 2, 3, 1, 4).reshape(2, -1, channels)
    dhidden = projector_back(pooled, proj_in, proj_gain, proj_out, view)
    own_row = lax.dynamic_slice_in_dim(dhidden, batch * clips_here + clip, 1, 0)
    dpooled = lax.dot_general(own_row, proj_in, (((1,), (1,)), ((), ())), precision=HIGHEST)

    dmix = dpooled[0] / cell_count * silu_grad(mixed)
    dmix_b = dmix.astype(jnp.bfloat16)
    from_out = convolve(dmix_b, flipped(out_w), -1)
    carried = from_out[frames - 1]
    for t in range(frames - 2, -1, -1):
        carried = from_out[t] + decays[t + 1] * carried
    carried = lax.ppermute(decays[0] * carried, PLANE, [(3, 0), (2, 1)])
    out_grad = weight_product(states_b, dmix_b)
    adjoint = [None] * frames
    for t in range(frames - 1, -1, -1):
        carried = from_out[t] + carried
        adjoint[t] = carried
        carried = decays[t] * carried
    dinput = (jnp.stack(adjoint) + skip_v * dmix).astype(jnp.bfloat16)
    in_grad = weight_product(maps, dinput)
    whole = summed(jnp.concatenate([in_grad, out_grad]))
    rows = in_grad.shape[0]
    return (whole[:, :rows], whole[:, rows:])


def solution(mesh):
    finer = Mesh(mesh.devices.reshape(2, 2, 4, 4, 2), ("xh", "xl", "y", "z", "core"))
    frames = ("xh", "xl", "y")
    return jax.shard_map(
        per_device,
        mesh=finer,
        in_specs=(
            P(("z", "core"), frames, None, None, None),
            P(("z", "core"), frames, None, None, None),
            P(),
            P(),
            P(None, frames, None),
            P(),
            P(),
            P(),
            P(),
        ),
        out_specs=(P(), P()),
        check_vma=False,
    )
```

```python
import jax
import jax.numpy as jnp
from jax import lax
from jax.experimental import pallas as pl
from jax.experimental.pallas import tpu as pltpu
from jax.sharding import Mesh
from jax.sharding import PartitionSpec as P

TIME = ("xl", "y")
PLANE = ("xh", "xl")


LAMBDA_OFF = 0.0051
EPSILON = 1e-05
HIGHEST = lax.Precision.HIGHEST


BF16, F32 = jnp.bfloat16, jnp.float32


def pair_weights(weights):
    empty = jnp.zeros((weights.shape[0] // 3, weights.shape[1]), weights.dtype)
    upper = jnp.concatenate([weights, empty], axis=0)
    lower = jnp.concatenate([empty, weights], axis=0)
    return jnp.concatenate([upper, lower], axis=1)


def flipped(weights):
    channels = weights.shape[1]
    blocks = weights.reshape(9, channels, channels)[::-1]
    return blocks.transpose(0, 2, 1).reshape(9 * channels, channels)


def clear_edges(cols_ref):
    frames, _, _, side, lanes = cols_ref.shape
    cols_ref[:, 0, 0] = jnp.zeros((frames, side, lanes), BF16)
    cols_ref[:, side // 2, 1] = jnp.zeros((frames, side, lanes), BF16)


def spread_columns(maps, cols_ref):
    frames, pairs, _, side, channels = maps.shape
    flat = maps.astype(F32).reshape(frames * side * side, channels)
    column = lax.broadcasted_iota(jnp.int32, flat.shape, 0) & (side - 1)
    left = jnp.where(column == 0, 0.0, pltpu.roll(flat, 1, 0))
    right = jnp.where(column == side - 1, 0.0, pltpu.roll(flat, flat.shape[0] - 1, 0))
    for k, shifted in enumerate((left, flat, right)):
        rows = shifted.astype(BF16).reshape(frames, pairs, 2, side, channels)
        lanes = slice(k * channels, (k + 1) * channels)
        cols_ref[:, 0:pairs, 1, :, lanes] = rows[:, :, 0]
        cols_ref[:, 1 : pairs + 1, 0, :, lanes] = rows[:, :, 1]


def pair_patches(cols_ref):
    frames, ends, _, side, lanes = cols_ref.shape
    pairs = ends - 1
    pieces = [cols_ref[:, a : a + pairs, b].reshape(frames * pairs * side, lanes) for a in (0, 1) for b in (0, 1)]
    return jnp.concatenate(pieces, axis=1)


def pair_convolve(cols_ref, weights_ref):
    frames, ends, _, side, lanes = cols_ref.shape
    channels = lanes // 3
    both = jnp.dot(pair_patches(cols_ref), weights_ref[...], preferred_element_type=F32)
    shape = (frames, ends - 1, side, channels)
    return both[:, :channels].reshape(shape), both[:, channels:].reshape(shape)


def add_weight_product(cols_ref, grads, acc_ref):
    frames, pairs, _, side, channels = grads.shape
    rows = frames * pairs * side
    both = [grads[:, :, k].reshape(rows, channels) for k in range(2)]
    acc_ref[...] += lax.dot_general(
        jnp.concatenate(both, axis=1),
        pair_patches(cols_ref),
        (((0,), (0,)), ((), ())),
        preferred_element_type=F32,
    )


def folded(acc_ref):
    channels = acc_ref.shape[0] // 2
    width = acc_ref.shape[1] // 4
    total = acc_ref[:channels, : 3 * width] + acc_ref[channels:, width:]
    return total.T


def inputs_kernel(got_ref, weights_ref, inputs_ref, decays_ref, end_ref, cols_ref, carry_ref):
    step = pl.program_id(0)
    frames, pairs, _, side, channels = inputs_ref.shape
    cells = frames * side * side

    @pl.when(step == 0)
    def _():
        clear_edges(cols_ref)
        carry_ref[...] = jnp.zeros_like(carry_ref)

    spread_columns(got_ref[0, :cells].reshape(inputs_ref.shape), cols_ref)
    parts = got_ref[0, cells:].astype(F32)
    decays = parts[:frames] + parts[frames : 2 * frames] + parts[2 * frames : 3 * frames]
    decays_ref[0] = decays
    for k, rows in enumerate(pair_convolve(cols_ref, weights_ref)):
        inputs_ref[:, :, k] = rows.astype(BF16)
    carried = carry_ref[...]
    for t in range(frames):
        carried = decays[t : t + 1] * carried + inputs_ref[t].astype(F32)
    carry_ref[...] = carried

    @pl.when(step == pl.num_programs(0) - 1)
    def _():
        end_ref[...] = carried


def mixed_kernel(inputs_ref, decays_ref, income_ref, skip_ref, weights_ref, states_ref, slope_ref, pooled_ref, cols_ref, carry_ref, sum_ref):
    step = pl.program_id(0)
    frames = inputs_ref.shape[0]

    @pl.when(step == 0)
    def _():
        clear_edges(cols_ref)
        carry_ref[...] = income_ref[...]
        sum_ref[...] = jnp.zeros_like(sum_ref)

    carried = carry_ref[...]
    for t in range(frames):
        carried = decays_ref[0, t : t + 1] * carried + inputs_ref[t].astype(F32)
        states_ref[t] = carried.astype(BF16)
    carry_ref[...] = carried
    spread_columns(states_ref[...], cols_ref)
    total = sum_ref[...]
    for k, rows in enumerate(pair_convolve(cols_ref, weights_ref)):
        mixed = rows + skip_ref[...] * inputs_ref[:, :, k].astype(F32)
        sigma = jax.nn.sigmoid(mixed)
        slope_ref[:, :, k] = sigma * (1.0 + mixed * (1.0 - sigma))
        total = total + jnp.sum(mixed * sigma, axis=(0, 1))
    sum_ref[...] = total

    @pl.when(step == pl.num_programs(0) - 1)
    def _():
        pooled_ref[...] = jnp.sum(total, axis=0, keepdims=True)


def from_out_kernel(slope_ref, decays_ref, dpool_ref, weights_ref, dmix_ref, source_ref, end_ref, cols_ref, carry_ref):
    step = pl.program_id(0)
    frames = slope_ref.shape[0]

    @pl.when(step == 0)
    def _():
        clear_edges(cols_ref)
        carry_ref[...] = jnp.zeros_like(carry_ref)

    dmix_ref[...] = (dpool_ref[...] * slope_ref[...]).astype(BF16)
    spread_columns(dmix_ref[...], cols_ref)
    for k, rows in enumerate(pair_convolve(cols_ref, weights_ref)):
        source_ref[:, :, k] = rows
    carried = carry_ref[...]
    for t in reversed(range(frames)):
        carried = decays_ref[0, t : t + 1] * (source_ref[t] + carried)
    carry_ref[...] = carried

    @pl.when(step == pl.num_programs(0) - 1)
    def _():
        end_ref[...] = carried


def out_grad_kernel(states_ref, dmix_ref, grad_ref, cols_ref, acc_ref):
    step = pl.program_id(0)

    @pl.when(step == 0)
    def _():
        clear_edges(cols_ref)
        acc_ref[...] = jnp.zeros_like(acc_ref)

    spread_columns(states_ref[...], cols_ref)
    add_weight_product(cols_ref, dmix_ref[...], acc_ref)

    @pl.when(step == pl.num_programs(0) - 1)
    def _():
        grad_ref[...] = folded(acc_ref)


def in_grad_kernel(got_ref, slope_ref, source_ref, decays_ref, income_ref, dpool_ref, skip_ref, grad_ref, cols_ref, carry_ref, dinput_ref, acc_ref):
    step = pl.program_id(0)
    frames, _, _, side, _ = slope_ref.shape

    @pl.when(step == 0)
    def _():
        clear_edges(cols_ref)
        carry_ref[...] = income_ref[...]
        acc_ref[...] = jnp.zeros_like(acc_ref)

    spread_columns(got_ref[0, : frames * side * side].reshape(slope_ref.shape), cols_ref)
    carried = carry_ref[...]
    for t in reversed(range(frames)):
        carried = source_ref[t] + carried
        dmix = dpool_ref[...] * slope_ref[t]
        dinput_ref[t] = (carried + skip_ref[...] * dmix).astype(BF16)
        carried = decays_ref[0, t : t + 1] * carried
    carry_ref[...] = carried
    add_weight_product(cols_ref, dinput_ref[...], acc_ref)

    @pl.when(step == pl.num_programs(0) - 1)
    def _():
        grad_ref[...] = folded(acc_ref)


class Plan:
    def __init__(self, steps, frames, side, channels):
        self.steps, self.frames, self.side, self.channels = steps, frames, side, channels
        self.map = (side // 2, 2, side, channels)

    def whole(self, shape):
        return pl.BlockSpec(shape, lambda i: (0,) * len(shape))

    def order(self, back):
        return (lambda i: self.steps - 1 - i) if back else (lambda i: i)

    def maps(self, back=False):
        at = self.order(back)
        return pl.BlockSpec((self.frames, *self.map), lambda i: (at(i), 0, 0, 0, 0))

    def got(self, rows, back=False):
        at = self.order(back)
        return pl.BlockSpec((1, rows, self.channels), lambda i: (at(i), 0, 0))

    def decays(self, back=False):
        return self.got(self.frames, back)

    def maps_of(self, dtype):
        return jax.ShapeDtypeStruct((self.steps * self.frames, *self.map), dtype)

    def carry_of(self):
        return jax.ShapeDtypeStruct(self.map, F32)

    def decays_of(self):
        return jax.ShapeDtypeStruct((self.steps, self.frames, self.channels), F32)

    def grad_of(self):
        return jax.ShapeDtypeStruct((9 * self.channels, self.channels), F32)

    def cols(self):
        return pltpu.VMEM((self.frames, self.side // 2 + 1, 2, self.side, 3 * self.channels), BF16)

    def carry(self):
        return pltpu.VMEM(self.map, F32)

    def acc(self):
        return pltpu.VMEM((2 * self.channels, 12 * self.channels), F32)

    def row(self):
        return self.whole((1, self.channels))

    def weights(self):
        return self.whole((12 * self.channels, 2 * self.channels))

    def call(self, kernel, in_specs, out_shape, out_specs, scratch):
        cells = self.steps * self.frames * self.side * self.side
        work = 2 * 9 * cells * self.channels * self.channels
        return pl.pallas_call(
            kernel,
            grid=(self.steps,),
            in_specs=in_specs,
            out_specs=out_specs,
            out_shape=out_shape,
            scratch_shapes=scratch,
            cost_estimate=pl.CostEstimate(flops=2 * work, transcendentals=0, bytes_accessed=4 * cells * self.channels),
            compiler_params=pltpu.CompilerParams(dimension_semantics=("arbitrary",), vmem_limit_bytes=48 << 20),
        )


def swapped(x):
    return lax.ppermute(x, "core", [(0, 1), (1, 0)])


def from_cores(x):
    here, there = x, swapped(x)
    first = lax.axis_index("core") == 0
    return jnp.stack([jnp.where(first, here, there), jnp.where(first, there, here)])


def from_all(x, axes):
    peers = lax.axis_size(axes)
    return lax.all_to_all(jnp.broadcast_to(x[None], (peers, *x.shape)), axes, 0, 0, tiled=True)


def in_parts(x):
    high = lax.reduce_precision(x, 8, 7)
    middle = lax.reduce_precision(x - high, 8, 7)
    low = x - high - middle
    return jnp.concatenate([high, middle, low], axis=-2).astype(jnp.bfloat16)


def clips_to_devices(rgb_maps, flow_maps, decay, half):
    clips, frames, side, _, channels = rgb_maps.shape
    straight = half == 0
    first = jnp.where(straight, rgb_maps, flow_maps)
    second = jnp.where(straight, flow_maps, rgb_maps)
    pieces = jnp.stack([first, second]).reshape(2, clips, frames * side * side, channels)
    parts = in_parts(jnp.where(straight, decay, decay[::-1]))
    parts = jnp.pad(parts, ((0, 0), (0, 16 - 3 * frames), (0, 0)))
    parts = jnp.broadcast_to(parts[:, None], (2, clips, 16, channels))
    sent = jnp.concatenate([pieces, parts], axis=2).reshape(2 * clips, -1, channels)
    return lax.all_to_all(sent, TIME, 0, 0, tiled=True)


def batch_norm(values):
    center = jnp.mean(values, axis=1, keepdims=True)
    centered = values - center
    scale = lax.rsqrt(jnp.mean(centered * centered, axis=1, keepdims=True) + EPSILON)
    return centered * scale, scale


def norm_back(grad, normed, scale):
    mean = jnp.mean(grad, axis=0, keepdims=True)
    along = jnp.mean(grad * normed, axis=0, keepdims=True)
    return (grad - mean - normed * along) * scale


def projector_back(pooled, proj_in, proj_gain, proj_out, view):
    _, clips, channels = pooled.shape
    width = proj_in.shape[1]
    hidden = jnp.dot(
        pooled.reshape(2 * clips, channels), proj_in, precision=HIGHEST, preferred_element_type=jnp.float32
    )
    hidden_x, hidden_s = batch_norm(hidden.reshape(2, clips, width))
    hidden_n = hidden_x * proj_gain
    relu_b = jnp.maximum(hidden_n, 0.0).astype(jnp.bfloat16)
    z = jnp.dot(relu_b.reshape(2 * clips, width), proj_out, preferred_element_type=jnp.float32)
    z_x, z_s = batch_norm(z.reshape(2, clips, width))
    zn = z_x.astype(jnp.bfloat16)
    first = view == 0
    own = jnp.where(first, zn[0], zn[1])
    other = jnp.where(first, zn[1], zn[0])
    own_wide = own.astype(jnp.float32)
    other_wide = other.astype(jnp.float32)
    corr_diag = jnp.sum(own_wide * other_wide, axis=0) / clips
    extra = -2.0 * (1.0 - corr_diag) - 2.0 * LAMBDA_OFF * corr_diag
    gram = lax.dot_general(other, other, (((1,), (1,)), ((), ())), preferred_element_type=jnp.float32)
    spread = jnp.dot(gram, own_wide, precision=HIGHEST, preferred_element_type=jnp.float32)
    dzn = spread * (2.0 * LAMBDA_OFF / (clips * clips)) + other_wide * (extra / clips)
    dz_b = norm_back(
        dzn, jnp.where(first, z_x[0], z_x[1]), jnp.where(first, z_s[0], z_s[1])
    ).astype(jnp.bfloat16)
    drelu = lax.dot_general(dz_b, proj_out, (((1,), (1,)), ((), ())), preferred_element_type=jnp.float32)
    own_x = jnp.where(first, hidden_x[0], hidden_x[1])
    own_s = jnp.where(first, hidden_s[0], hidden_s[1])
    own_n = jnp.where(first, hidden_n[0], hidden_n[1])
    dxh = jnp.where(own_n > 0, drelu, 0.0) * proj_gain
    dhidden = norm_back(dxh, own_x, own_s)
    return dhidden


def summed(grads):
    rows, channels = grads.shape
    core = lax.axis_index("core")
    halves = grads.reshape(2, rows // 2, channels)
    mine = lax.dynamic_index_in_dim(halves, core, 0, False)
    given = lax.dynamic_index_in_dim(halves, 1 - core, 0, False)
    total = mine + swapped(given)
    pieces = total.astype(jnp.bfloat16).reshape(4, rows // 8, channels)
    total = jnp.sum(lax.all_to_all(pieces, "z", 0, 0, tiled=True).astype(jnp.float32), axis=0)
    total = jnp.sum(from_all(total.astype(jnp.bfloat16), "y").astype(jnp.float32), axis=0)
    seen = from_all(total.astype(jnp.bfloat16), PLANE).astype(jnp.float32)
    both = jnp.stack([seen[0] + seen[3], seen[1] + seen[2]]).astype(jnp.bfloat16)
    whole = from_cores(from_all(both, "z"))
    return whole.transpose(2, 0, 1, 3, 4).reshape(2, rows, channels).astype(jnp.float32)


def per_device(
    rgb_maps, flow_maps, in_weights, out_weights, decay, skip, proj_in, proj_gain, proj_out
):
    half = lax.axis_index("xh")
    view = lax.axis_index("xl") ^ half
    clip = lax.axis_index("y")
    batch = lax.axis_index(("z", "core"))
    clips_here = rgb_maps.shape[0]
    _, frames_here, side, _, channels = rgb_maps.shape
    got = clips_to_devices(rgb_maps, flow_maps, decay, half)
    steps, rows, _ = got.shape
    cell_count = 2 * steps * frames_here * side * side
    plan = Plan(steps, frames_here, side, channels)
    in_w = lax.dynamic_index_in_dim(in_weights, view, 0, False)
    out_w = lax.dynamic_index_in_dim(out_weights, view, 0, False)
    skip_v = lax.dynamic_index_in_dim(skip, view, 0, True)
    carry_spec = plan.whole(plan.map)

    inputs, decays, end = plan.call(
        inputs_kernel,
        [plan.got(rows), plan.weights()],
        [plan.maps_of(BF16), plan.decays_of(), plan.carry_of()],
        [plan.maps(), plan.decays(), carry_spec],
        [plan.cols(), plan.carry()],
    )(got, pair_weights(in_w))
    income = lax.ppermute(end, PLANE, [(0, 3), (1, 2)])
    states_b, slope, pooled_part = plan.call(
        mixed_kernel,
        [plan.maps(), plan.decays(), carry_spec, plan.row(), plan.weights()],
        [plan.maps_of(BF16), plan.maps_of(F32), jax.ShapeDtypeStruct((1, channels), F32)],
        [plan.maps(), plan.maps(), plan.row()],
        [plan.cols(), plan.carry(), pltpu.VMEM((side, channels), F32)],
    )(inputs, decays, income, skip_v, pair_weights(out_w))

    seen = from_all(from_cores(pooled_part[0]), ("xh", "xl", "y", "z"))
    seen = seen.reshape(2, 2, clips_here, 4, 2, channels)
    views = jnp.stack([seen[0, 0] + seen[1, 1], seen[0, 1] + seen[1, 0]]) / cell_count
    pooled = views.transpose(0, 2, 3, 1, 4).reshape(2, -1, channels)
    dhidden = projector_back(pooled, proj_in, proj_gain, proj_out, view)
    own_row = lax.dynamic_slice_in_dim(dhidden, batch * clips_here + clip, 1, 0)
    dpooled = lax.dot_general(own_row, proj_in, (((1,), (1,)), ((), ())), precision=HIGHEST)

    dpool = dpooled / cell_count
    dmix_b, source, end = plan.call(
        from_out_kernel,
        [plan.maps(True), plan.decays(True), plan.row(), plan.weights()],
        [plan.maps_of(BF16), plan.maps_of(F32), plan.carry_of()],
        [plan.maps(True), plan.maps(True), carry_spec],
        [plan.cols(), plan.carry()],
    )(slope, decays, dpool, pair_weights(flipped(out_w)))
    income = lax.ppermute(end, PLANE, [(3, 0), (2, 1)])
    out_grad = plan.call(
        out_grad_kernel,
        [plan.maps(), plan.maps()],
        plan.grad_of(),
        plan.whole((9 * channels, channels)),
        [plan.cols(), plan.acc()],
    )(states_b, dmix_b)
    in_grad = plan.call(
        in_grad_kernel,
        [plan.got(rows, True), plan.maps(True), plan.maps(True), plan.decays(True), carry_spec, plan.row(), plan.row()],
        plan.grad_of(),
        plan.whole((9 * channels, channels)),
        [plan.cols(), plan.carry(), pltpu.VMEM((frames_here, *plan.map), BF16), plan.acc()],
    )(got, slope, source, decays, income, dpool, skip_v)
    whole = summed(jnp.concatenate([in_grad, out_grad]))
    taps = in_grad.shape[0]
    return (whole[:, :taps], whole[:, taps:])


def solution(mesh):
    finer = Mesh(mesh.devices.reshape(2, 2, 4, 4, 2), ("xh", "xl", "y", "z", "core"))
    frames = ("xh", "xl", "y")
    return jax.shard_map(
        per_device,
        mesh=finer,
        in_specs=(
            P(("z", "core"), frames, None, None, None),
            P(("z", "core"), frames, None, None, None),
            P(),
            P(),
            P(None, frames, None),
            P(),
            P(),
            P(),
            P(),
        ),
        out_specs=(P(), P()),
        check_vma=False,
    )
```

```python
import jax
import jax.numpy as jnp
from jax import lax
from jax.experimental import pallas as pl
from jax.experimental.pallas import tpu as pltpu
from jax.sharding import Mesh
from jax.sharding import PartitionSpec as P

TIME = ("xl", "y")
PLANE = ("xh", "xl")


LAMBDA_OFF = 0.0051
EPSILON = 1e-05
HIGHEST = lax.Precision.HIGHEST


BF16, F32 = jnp.bfloat16, jnp.float32


def pair_weights(weights_ref, both_ref):
    taps, channels = weights_ref.shape[1:]
    third = taps // 3
    both_ref[:taps, :channels] = weights_ref[0]
    both_ref[taps:, :channels] = jnp.zeros((third, channels), BF16)
    both_ref[:third, channels:] = jnp.zeros((third, channels), BF16)
    both_ref[third:, channels:] = weights_ref[0]


def flipped_pair_weights(weights_ref, both_ref):
    taps, channels = weights_ref.shape[1:]
    third = taps // 3
    both_ref[taps:, :channels] = jnp.zeros((third, channels), BF16)
    both_ref[:third, channels:] = jnp.zeros((third, channels), BF16)
    for k in range(taps // channels):
        block = weights_ref[0, taps - (k + 1) * channels : taps - k * channels].astype(F32).T.astype(BF16)
        both_ref[k * channels : (k + 1) * channels, :channels] = block
        both_ref[third + k * channels : third + (k + 1) * channels, channels:] = block


def take_carry(carry_ref, income_ref, has_income):
    @pl.when(has_income)
    def _():
        carry_ref[...] = income_ref[...]

    @pl.when(jnp.logical_not(has_income))
    def _():
        carry_ref[...] = jnp.zeros_like(carry_ref)


def clear_edges(cols_ref):
    frames, _, _, side, lanes = cols_ref.shape
    cols_ref[:, 0, 0] = jnp.zeros((frames, side, lanes), BF16)
    cols_ref[:, side // 2, 1] = jnp.zeros((frames, side, lanes), BF16)


def spread_columns(maps, cols_ref):
    frames, pairs, _, side, channels = maps.shape
    flat = maps.astype(F32).reshape(frames * side * side, channels)
    column = lax.broadcasted_iota(jnp.int32, flat.shape, 0) & (side - 1)
    left = jnp.where(column == 0, 0.0, pltpu.roll(flat, 1, 0))
    right = jnp.where(column == side - 1, 0.0, pltpu.roll(flat, flat.shape[0] - 1, 0))
    for k, shifted in enumerate((left, flat, right)):
        rows = shifted.astype(BF16).reshape(frames, pairs, 2, side, channels)
        lanes = slice(k * channels, (k + 1) * channels)
        cols_ref[:, 0:pairs, 1, :, lanes] = rows[:, :, 0]
        cols_ref[:, 1 : pairs + 1, 0, :, lanes] = rows[:, :, 1]


def pair_patches(cols_ref):
    frames, ends, _, side, lanes = cols_ref.shape
    pairs = ends - 1
    pieces = [cols_ref[:, a : a + pairs, b].reshape(frames * pairs * side, lanes) for a in (0, 1) for b in (0, 1)]
    return jnp.concatenate(pieces, axis=1)


def pair_convolve(cols_ref, weights_ref):
    frames, ends, _, side, lanes = cols_ref.shape
    channels = lanes // 3
    both = jnp.dot(pair_patches(cols_ref), weights_ref[...], preferred_element_type=F32)
    shape = (frames, ends - 1, side, channels)
    return both[:, :channels].reshape(shape), both[:, channels:].reshape(shape)


def add_weight_product(cols_ref, grads, acc_ref):
    frames, pairs, _, side, channels = grads.shape
    rows = frames * pairs * side
    both = [grads[:, :, k].reshape(rows, channels) for k in range(2)]
    acc_ref[...] += lax.dot_general(
        jnp.concatenate(both, axis=1),
        pair_patches(cols_ref),
        (((0,), (0,)), ((), ())),
        preferred_element_type=F32,
    )


def folded(acc_ref):
    channels = acc_ref.shape[0] // 2
    width = acc_ref.shape[1] // 4
    total = acc_ref[:channels, : 3 * width] + acc_ref[channels:, width:]
    return total.T


def inputs_kernel(place_ref, got_ref, weights_ref, inputs_ref, decays_ref, end_ref, cols_ref, both_ref, carry_ref):
    step = pl.program_id(0)
    frames, pairs, _, side, channels = inputs_ref.shape
    cells = frames * side * side

    @pl.when(step == 0)
    def _():
        clear_edges(cols_ref)
        pair_weights(weights_ref, both_ref)
        carry_ref[...] = jnp.zeros_like(carry_ref)

    spread_columns(got_ref[0, :cells].reshape(inputs_ref.shape), cols_ref)
    parts = got_ref[0, cells:].astype(F32)
    decays = parts[:frames] + parts[frames : 2 * frames] + parts[2 * frames : 3 * frames]
    decays_ref[0] = decays
    for k, rows in enumerate(pair_convolve(cols_ref, both_ref)):
        inputs_ref[:, :, k] = rows.astype(BF16)
    carried = carry_ref[...]
    for t in range(frames):
        carried = decays[t : t + 1] * carried + inputs_ref[t].astype(F32)
    carry_ref[...] = carried

    @pl.when(step == pl.num_programs(0) - 1)
    def _():
        end_ref[...] = carried


def mixed_kernel(place_ref, inputs_ref, decays_ref, income_ref, skip_ref, weights_ref, states_ref, slope_ref, pooled_ref, cols_ref, both_ref, carry_ref, sum_ref):
    step = pl.program_id(0)
    frames = inputs_ref.shape[0]

    @pl.when(step == 0)
    def _():
        clear_edges(cols_ref)
        pair_weights(weights_ref, both_ref)
        take_carry(carry_ref, income_ref, place_ref[0] == 1)
        sum_ref[...] = jnp.zeros_like(sum_ref)

    carried = carry_ref[...]
    for t in range(frames):
        carried = decays_ref[0, t : t + 1] * carried + inputs_ref[t].astype(F32)
        states_ref[t] = carried.astype(BF16)
    carry_ref[...] = carried
    spread_columns(states_ref[...], cols_ref)
    total = sum_ref[...]
    for k, rows in enumerate(pair_convolve(cols_ref, both_ref)):
        mixed = rows + skip_ref[0] * inputs_ref[:, :, k].astype(F32)
        sigma = jax.nn.sigmoid(mixed)
        slope_ref[:, :, k] = sigma * (1.0 + mixed * (1.0 - sigma))
        total = total + jnp.sum(mixed * sigma, axis=(0, 1))
    sum_ref[...] = total

    @pl.when(step == pl.num_programs(0) - 1)
    def _():
        pooled_ref[...] = jnp.sum(total, axis=0, keepdims=True)


def from_out_kernel(place_ref, slope_ref, decays_ref, dpool_ref, weights_ref, dmix_ref, source_ref, end_ref, cols_ref, both_ref, carry_ref):
    step = pl.program_id(0)
    frames = slope_ref.shape[0]

    @pl.when(step == 0)
    def _():
        clear_edges(cols_ref)
        flipped_pair_weights(weights_ref, both_ref)
        carry_ref[...] = jnp.zeros_like(carry_ref)

    dmix_ref[...] = (dpool_ref[...] * slope_ref[...]).astype(BF16)
    spread_columns(dmix_ref[...], cols_ref)
    for k, rows in enumerate(pair_convolve(cols_ref, both_ref)):
        source_ref[:, :, k] = rows
    carried = carry_ref[...]
    for t in reversed(range(frames)):
        carried = decays_ref[0, t : t + 1] * (source_ref[t] + carried)
    carry_ref[...] = carried

    @pl.when(step == pl.num_programs(0) - 1)
    def _():
        end_ref[...] = carried


def out_grad_kernel(place_ref, states_ref, dmix_ref, grad_ref, cols_ref, acc_ref):
    step = pl.program_id(0)

    @pl.when(step == 0)
    def _():
        clear_edges(cols_ref)
        acc_ref[...] = jnp.zeros_like(acc_ref)

    spread_columns(states_ref[...], cols_ref)
    add_weight_product(cols_ref, dmix_ref[...], acc_ref)

    @pl.when(step == pl.num_programs(0) - 1)
    def _():
        grad_ref[...] = folded(acc_ref)


def in_grad_kernel(place_ref, got_ref, slope_ref, source_ref, decays_ref, income_ref, dpool_ref, skip_ref, grad_ref, cols_ref, carry_ref, dinput_ref, acc_ref):
    step = pl.program_id(0)
    frames, _, _, side, _ = slope_ref.shape

    @pl.when(step == 0)
    def _():
        clear_edges(cols_ref)
        take_carry(carry_ref, income_ref, place_ref[0] == 0)
        acc_ref[...] = jnp.zeros_like(acc_ref)

    spread_columns(got_ref[0, : frames * side * side].reshape(slope_ref.shape), cols_ref)
    carried = carry_ref[...]
    for t in reversed(range(frames)):
        carried = source_ref[t] + carried
        dmix = dpool_ref[...] * slope_ref[t]
        dinput_ref[t] = (carried + skip_ref[0] * dmix).astype(BF16)
        carried = decays_ref[0, t : t + 1] * carried
    carry_ref[...] = carried
    add_weight_product(cols_ref, dinput_ref[...], acc_ref)

    @pl.when(step == pl.num_programs(0) - 1)
    def _():
        grad_ref[...] = folded(acc_ref)


class Plan:
    def __init__(self, steps, frames, side, channels):
        self.steps, self.frames, self.side, self.channels = steps, frames, side, channels
        self.map = (side // 2, 2, side, channels)

    def whole(self, shape):
        return pl.BlockSpec(shape, lambda i, place: (0,) * len(shape))

    def order(self, back):
        return (lambda i: self.steps - 1 - i) if back else (lambda i: i)

    def maps(self, back=False):
        at = self.order(back)
        return pl.BlockSpec((self.frames, *self.map), lambda i, place: (at(i), 0, 0, 0, 0))

    def got(self, rows, back=False):
        at = self.order(back)
        return pl.BlockSpec((1, rows, self.channels), lambda i, place: (at(i), 0, 0))

    def decays(self, back=False):
        return self.got(self.frames, back)

    def of_view(self, rows):
        return pl.BlockSpec((1, rows, self.channels), lambda i, place: (place[1], 0, 0))

    def maps_of(self, dtype):
        return jax.ShapeDtypeStruct((self.steps * self.frames, *self.map), dtype)

    def carry_of(self):
        return jax.ShapeDtypeStruct(self.map, F32)

    def decays_of(self):
        return jax.ShapeDtypeStruct((self.steps, self.frames, self.channels), F32)

    def grad_of(self):
        return jax.ShapeDtypeStruct((9 * self.channels, self.channels), F32)

    def cols(self):
        return pltpu.VMEM((self.frames, self.side // 2 + 1, 2, self.side, 3 * self.channels), BF16)

    def carry(self):
        return pltpu.VMEM(self.map, F32)

    def acc(self):
        return pltpu.VMEM((2 * self.channels, 12 * self.channels), F32)

    def row(self):
        return self.whole((1, self.channels))

    def both(self):
        return pltpu.VMEM((12 * self.channels, 2 * self.channels), BF16)

    def call(self, kernel, in_specs, out_shape, out_specs, scratch):
        cells = self.steps * self.frames * self.side * self.side
        work = 2 * 9 * cells * self.channels * self.channels
        return pl.pallas_call(
            kernel,
            out_shape=out_shape,
            grid_spec=pltpu.PrefetchScalarGridSpec(
                num_scalar_prefetch=1,
                grid=(self.steps,),
                in_specs=in_specs,
                out_specs=out_specs,
                scratch_shapes=scratch,
            ),
            cost_estimate=pl.CostEstimate(flops=2 * work, transcendentals=0, bytes_accessed=4 * cells * self.channels),
            compiler_params=pltpu.CompilerParams(dimension_semantics=("arbitrary",), vmem_limit_bytes=16 << 20),
        )


def swapped(x):
    return lax.ppermute(x, "core", [(0, 1), (1, 0)])


def from_cores(x):
    here, there = x, swapped(x)
    first = lax.axis_index("core") == 0
    return jnp.stack([jnp.where(first, here, there), jnp.where(first, there, here)])


def from_all(x, axes):
    peers = lax.axis_size(axes)
    return lax.all_to_all(jnp.broadcast_to(x[None], (peers, *x.shape)), axes, 0, 0, tiled=True)


def in_parts(x):
    high = lax.reduce_precision(x, 8, 7)
    middle = lax.reduce_precision(x - high, 8, 7)
    low = x - high - middle
    return jnp.concatenate([high, middle, low], axis=-2).astype(jnp.bfloat16)


def clips_to_devices(rgb_maps, flow_maps, decay, half):
    clips, frames, side, _, channels = rgb_maps.shape
    straight = half == 0
    first = jnp.where(straight, rgb_maps, flow_maps)
    second = jnp.where(straight, flow_maps, rgb_maps)
    pieces = jnp.stack([first, second]).reshape(2, clips, frames * side * side, channels)
    parts = in_parts(jnp.where(straight, decay, decay[::-1]))
    parts = jnp.pad(parts, ((0, 0), (0, 16 - 3 * frames), (0, 0)))
    parts = jnp.broadcast_to(parts[:, None], (2, clips, 16, channels))
    sent = jnp.concatenate([pieces, parts], axis=2).reshape(2 * clips, -1, channels)
    return lax.all_to_all(sent, TIME, 0, 0, tiled=True)


def batch_norm(values):
    center = jnp.mean(values, axis=1, keepdims=True)
    centered = values - center
    scale = lax.rsqrt(jnp.mean(centered * centered, axis=1, keepdims=True) + EPSILON)
    return centered * scale, scale


def norm_back(grad, normed, scale):
    mean = jnp.mean(grad, axis=0, keepdims=True)
    along = jnp.mean(grad * normed, axis=0, keepdims=True)
    return (grad - mean - normed * along) * scale


def projector_back(pooled, proj_in, proj_gain, proj_out, view):
    _, clips, channels = pooled.shape
    width = proj_in.shape[1]
    hidden = jnp.dot(
        pooled.reshape(2 * clips, channels), proj_in, precision=HIGHEST, preferred_element_type=jnp.float32
    )
    hidden_x, hidden_s = batch_norm(hidden.reshape(2, clips, width))
    hidden_n = hidden_x * proj_gain
    relu_b = jnp.maximum(hidden_n, 0.0).astype(jnp.bfloat16)
    z = jnp.dot(relu_b.reshape(2 * clips, width), proj_out, preferred_element_type=jnp.float32)
    z_x, z_s = batch_norm(z.reshape(2, clips, width))
    zn = z_x.astype(jnp.bfloat16)
    first = view == 0
    own = jnp.where(first, zn[0], zn[1])
    other = jnp.where(first, zn[1], zn[0])
    own_wide = own.astype(jnp.float32)
    other_wide = other.astype(jnp.float32)
    corr_diag = jnp.sum(own_wide * other_wide, axis=0) / clips
    extra = -2.0 * (1.0 - corr_diag) - 2.0 * LAMBDA_OFF * corr_diag
    gram = lax.dot_general(other, other, (((1,), (1,)), ((), ())), preferred_element_type=jnp.float32)
    spread = jnp.dot(gram, own_wide, precision=HIGHEST, preferred_element_type=jnp.float32)
    dzn = spread * (2.0 * LAMBDA_OFF / (clips * clips)) + other_wide * (extra / clips)
    dz_b = norm_back(
        dzn, jnp.where(first, z_x[0], z_x[1]), jnp.where(first, z_s[0], z_s[1])
    ).astype(jnp.bfloat16)
    drelu = lax.dot_general(dz_b, proj_out, (((1,), (1,)), ((), ())), preferred_element_type=jnp.float32)
    own_x = jnp.where(first, hidden_x[0], hidden_x[1])
    own_s = jnp.where(first, hidden_s[0], hidden_s[1])
    own_n = jnp.where(first, hidden_n[0], hidden_n[1])
    dxh = jnp.where(own_n > 0, drelu, 0.0) * proj_gain
    dhidden = norm_back(dxh, own_x, own_s)
    return dhidden


def from_other_half(x):
    return lax.ppermute(x, PLANE, [(0, 3), (1, 2), (2, 1), (3, 0)])


def from_peer(x, axes, k):
    return lax.ppermute(x, axes, [(i, i ^ k) for i in range(4)])


def from_ring(x, axes):
    return [x] + [from_peer(x, axes, k) for k in (1, 2, 3)]


def total_of(arrays):
    return sum(a.astype(F32) for a in arrays)


def place_kernel(place_ref, *refs):
    view, core, ring = place_ref[1], place_ref[2], place_ref[3]
    outs = refs[8:]
    for shift, pieces in enumerate((refs[:4], refs[4:8])):
        for k, piece in enumerate(pieces):
            rows = piece.shape[2]
            start = pl.multiple_of((4 * (core ^ shift) + (ring ^ k)) * rows, rows)
            for n, out in enumerate(outs):
                for v in range(2):
                    out[view ^ v, pl.ds(start, rows)] = piece[n, v].astype(F32)


def summed(grads, place):
    taps, channels = grads[0].shape
    core, ring = lax.axis_index("core"), lax.axis_index("z")
    halves = jnp.stack(grads).reshape(len(grads), 2, 4, taps // 8, channels)
    mine = lax.dynamic_index_in_dim(halves, core, 1, False)
    given = lax.dynamic_index_in_dim(halves, 1 - core, 1, False)
    pieces = (mine + swapped(given)).astype(BF16)
    parts = [lax.dynamic_index_in_dim(pieces, ring, 1, False)]
    parts += [from_peer(lax.dynamic_index_in_dim(pieces, ring ^ k, 1, False), "z", k) for k in (1, 2, 3)]
    parts = from_ring(total_of(parts).astype(BF16), "y")
    parts = from_ring(total_of(parts).astype(BF16), PLANE)
    both = jnp.stack([total_of([parts[0], parts[3]]), total_of([parts[1], parts[2]])], axis=1).astype(BF16)
    mine = from_ring(both, "z")
    given = [swapped(a) for a in mine]
    whole = jax.ShapeDtypeStruct((2, taps, channels), F32)
    return tuple(
        pl.pallas_call(
            place_kernel,
            out_shape=[whole] * len(grads),
            in_specs=[pl.BlockSpec(memory_space=pltpu.SMEM)] + [pl.BlockSpec(memory_space=pltpu.VMEM)] * 8,
            compiler_params=pltpu.CompilerParams(vmem_limit_bytes=16 << 20),
        )(place, *mine, *given)
    )


def per_device(
    rgb_maps, flow_maps, in_weights, out_weights, decay, skip, proj_in, proj_gain, proj_out
):
    half = lax.axis_index("xh")
    view = lax.axis_index("xl") ^ half
    clip = lax.axis_index("y")
    batch = lax.axis_index(("z", "core"))
    clips_here = rgb_maps.shape[0]
    _, frames_here, side, _, channels = rgb_maps.shape
    got = clips_to_devices(rgb_maps, flow_maps, decay, half)
    steps, rows, _ = got.shape
    cell_count = 2 * steps * frames_here * side * side
    plan = Plan(steps, frames_here, side, channels)
    taps = in_weights.shape[1]
    weights = plan.of_view(taps)
    skips = skip.reshape(2, 1, channels)
    place = jnp.stack([half, view, lax.axis_index("core"), lax.axis_index("z")]).astype(jnp.int32)
    carry_spec = plan.whole(plan.map)

    inputs, decays, end = plan.call(
        inputs_kernel,
        [plan.got(rows), weights],
        [plan.maps_of(BF16), plan.decays_of(), plan.carry_of()],
        [plan.maps(), plan.decays(), carry_spec],
        [plan.cols(), plan.both(), plan.carry()],
    )(place, got, in_weights)
    income = from_other_half(end)
    states_b, slope, pooled_part = plan.call(
        mixed_kernel,
        [plan.maps(), plan.decays(), carry_spec, plan.of_view(1), weights],
        [plan.maps_of(BF16), plan.maps_of(F32), jax.ShapeDtypeStruct((1, channels), F32)],
        [plan.maps(), plan.maps(), plan.row()],
        [plan.cols(), plan.both(), plan.carry(), pltpu.VMEM((side, channels), F32)],
    )(place, inputs, decays, income, skips, out_weights)

    seen = from_all(from_cores(pooled_part[0]), ("xh", "xl", "y", "z"))
    seen = seen.reshape(2, 2, clips_here, 4, 2, channels)
    views = jnp.stack([seen[0, 0] + seen[1, 1], seen[0, 1] + seen[1, 0]]) / cell_count
    pooled = views.transpose(0, 2, 3, 1, 4).reshape(2, -1, channels)
    dhidden = projector_back(pooled, proj_in, proj_gain, proj_out, view)
    own_row = lax.dynamic_slice_in_dim(dhidden, batch * clips_here + clip, 1, 0)
    dpooled = lax.dot_general(own_row, proj_in, (((1,), (1,)), ((), ())), precision=HIGHEST)

    dpool = dpooled / cell_count
    dmix_b, source, end = plan.call(
        from_out_kernel,
        [plan.maps(True), plan.decays(True), plan.row(), weights],
        [plan.maps_of(BF16), plan.maps_of(F32), plan.carry_of()],
        [plan.maps(True), plan.maps(True), carry_spec],
        [plan.cols(), plan.both(), plan.carry()],
    )(place, slope, decays, dpool, out_weights)
    income = from_other_half(end)
    out_grad = plan.call(
        out_grad_kernel,
        [plan.maps(), plan.maps()],
        plan.grad_of(),
        plan.whole((9 * channels, channels)),
        [plan.cols(), plan.acc()],
    )(place, states_b, dmix_b)
    in_grad = plan.call(
        in_grad_kernel,
        [plan.got(rows, True), plan.maps(True), plan.maps(True), plan.decays(True), carry_spec, plan.row(), plan.of_view(1)],
        plan.grad_of(),
        plan.whole((9 * channels, channels)),
        [plan.cols(), plan.carry(), pltpu.VMEM((frames_here, *plan.map), BF16), plan.acc()],
    )(place, got, slope, source, decays, income, dpool, skips)
    return summed([in_grad, out_grad], place)


def solution(mesh):
    finer = Mesh(mesh.devices.reshape(2, 2, 4, 4, 2), ("xh", "xl", "y", "z", "core"))
    frames = ("xh", "xl", "y")
    return jax.shard_map(
        per_device,
        mesh=finer,
        in_specs=(
            P(("z", "core"), frames, None, None, None),
            P(("z", "core"), frames, None, None, None),
            P(),
            P(),
            P(None, frames, None),
            P(),
            P(),
            P(),
            P(),
        ),
        out_specs=(P(), P()),
        check_vma=False,
    )
```

```python
import functools

import jax
import jax.numpy as jnp
from jax import lax
from jax.experimental import pallas as pl
from jax.experimental.pallas import tpu as pltpu
from jax.sharding import Mesh
from jax.sharding import PartitionSpec as P

TIME = ("xl", "y")
PLANE = ("xh", "xl")


LAMBDA_OFF = 0.0051
EPSILON = 1e-05
HIGHEST = lax.Precision.HIGHEST


BF16, F32 = jnp.bfloat16, jnp.float32


def pair_weights(weights_ref, both_ref):
    taps, channels = weights_ref.shape[1:]
    third = taps // 3
    both_ref[:taps, :channels] = weights_ref[0]
    both_ref[taps:, :channels] = jnp.zeros((third, channels), BF16)
    both_ref[:third, channels:] = jnp.zeros((third, channels), BF16)
    both_ref[third:, channels:] = weights_ref[0]


def flipped_pair_weights(weights_ref, both_ref):
    taps, channels = weights_ref.shape[1:]
    third = taps // 3
    both_ref[taps:, :channels] = jnp.zeros((third, channels), BF16)
    both_ref[:third, channels:] = jnp.zeros((third, channels), BF16)
    for k in range(taps // channels):
        block = weights_ref[0, taps - (k + 1) * channels : taps - k * channels].astype(F32).T.astype(BF16)
        both_ref[k * channels : (k + 1) * channels, :channels] = block
        both_ref[third + k * channels : third + (k + 1) * channels, channels:] = block


def take_carry(carry_ref, income_ref, has_income):
    @pl.when(has_income)
    def _():
        carry_ref[...] = income_ref[...]

    @pl.when(jnp.logical_not(has_income))
    def _():
        carry_ref[...] = jnp.zeros_like(carry_ref)


def clear_edges(cols_ref):
    frames, _, _, side, lanes = cols_ref.shape
    cols_ref[:, 0, 0] = jnp.zeros((frames, side, lanes), BF16)
    cols_ref[:, side // 2, 1] = jnp.zeros((frames, side, lanes), BF16)


def spread_columns(maps, cols_ref):
    frames, pairs, _, side, channels = maps.shape
    flat = maps.astype(F32).reshape(frames * side * side, channels)
    column = lax.broadcasted_iota(jnp.int32, flat.shape, 0) & (side - 1)
    left = jnp.where(column == 0, 0.0, pltpu.roll(flat, 1, 0))
    right = jnp.where(column == side - 1, 0.0, pltpu.roll(flat, flat.shape[0] - 1, 0))
    for k, shifted in enumerate((left, flat, right)):
        rows = shifted.astype(BF16).reshape(frames, pairs, 2, side, channels)
        lanes = slice(k * channels, (k + 1) * channels)
        cols_ref[:, 0:pairs, 1, :, lanes] = rows[:, :, 0]
        cols_ref[:, 1 : pairs + 1, 0, :, lanes] = rows[:, :, 1]


def pair_patches(cols_ref):
    frames, ends, _, side, lanes = cols_ref.shape
    pairs = ends - 1
    pieces = [cols_ref[:, a : a + pairs, b].reshape(frames * pairs * side, lanes) for a in (0, 1) for b in (0, 1)]
    return jnp.concatenate(pieces, axis=1)


def pair_convolve(cols_ref, weights_ref):
    frames, ends, _, side, lanes = cols_ref.shape
    channels = lanes // 3
    both = jnp.dot(pair_patches(cols_ref), weights_ref[...], preferred_element_type=F32)
    shape = (frames, ends - 1, side, channels)
    return both[:, :channels].reshape(shape), both[:, channels:].reshape(shape)


def add_weight_product(cols_ref, grads, acc_ref):
    frames, pairs, _, side, channels = grads.shape
    rows = frames * pairs * side
    both = [grads[:, :, k].reshape(rows, channels) for k in range(2)]
    acc_ref[...] += lax.dot_general(
        jnp.concatenate(both, axis=1),
        pair_patches(cols_ref),
        (((0,), (0,)), ((), ())),
        preferred_element_type=F32,
    )


def folded(acc_ref):
    channels = acc_ref.shape[0] // 2
    width = acc_ref.shape[1] // 4
    total = acc_ref[:channels, : 3 * width] + acc_ref[channels:, width:]
    return total.T


def inputs_kernel(place_ref, got_ref, weights_ref, inputs_ref, decays_ref, end_ref, cols_ref, both_ref, carry_ref):
    step = pl.program_id(0)
    frames, pairs, _, side, channels = inputs_ref.shape
    cells = frames * side * side

    @pl.when(step == 0)
    def _():
        clear_edges(cols_ref)
        pair_weights(weights_ref, both_ref)
        carry_ref[...] = jnp.zeros_like(carry_ref)

    spread_columns(got_ref[0, :cells].reshape(inputs_ref.shape), cols_ref)
    parts = got_ref[0, cells:].astype(F32)
    decays = parts[:frames] + parts[frames : 2 * frames] + parts[2 * frames : 3 * frames]
    decays_ref[0] = decays
    for k, rows in enumerate(pair_convolve(cols_ref, both_ref)):
        inputs_ref[:, :, k] = rows.astype(BF16)
    carried = carry_ref[...]
    for t in range(frames):
        carried = decays[t : t + 1] * carried + inputs_ref[t].astype(F32)
    carry_ref[...] = carried

    @pl.when(step == pl.num_programs(0) - 1)
    def _():
        end_ref[...] = carried


def mixed_kernel(place_ref, inputs_ref, decays_ref, income_ref, skip_ref, weights_ref, states_ref, slope_ref, pooled_ref, cols_ref, both_ref, carry_ref, sum_ref):
    step = pl.program_id(0)
    frames = inputs_ref.shape[0]

    @pl.when(step == 0)
    def _():
        clear_edges(cols_ref)
        pair_weights(weights_ref, both_ref)
        take_carry(carry_ref, income_ref, place_ref[0] == 1)
        sum_ref[...] = jnp.zeros_like(sum_ref)

    carried = carry_ref[...]
    for t in range(frames):
        carried = decays_ref[0, t : t + 1] * carried + inputs_ref[t].astype(F32)
        states_ref[t] = carried.astype(BF16)
    carry_ref[...] = carried
    spread_columns(states_ref[...], cols_ref)
    total = sum_ref[...]
    for k, rows in enumerate(pair_convolve(cols_ref, both_ref)):
        mixed = rows + skip_ref[0] * inputs_ref[:, :, k].astype(F32)
        sigma = jax.nn.sigmoid(mixed)
        slope_ref[:, :, k] = sigma * (1.0 + mixed * (1.0 - sigma))
        total = total + jnp.sum(mixed * sigma, axis=(0, 1))
    sum_ref[...] = total

    @pl.when(step == pl.num_programs(0) - 1)
    def _():
        pooled_ref[...] = jnp.sum(total, axis=0, keepdims=True)


def from_out_kernel(place_ref, slope_ref, decays_ref, dpool_ref, weights_ref, dmix_ref, source_ref, end_ref, cols_ref, both_ref, carry_ref):
    step = pl.program_id(0)
    frames = slope_ref.shape[0]

    @pl.when(step == 0)
    def _():
        clear_edges(cols_ref)
        flipped_pair_weights(weights_ref, both_ref)
        carry_ref[...] = jnp.zeros_like(carry_ref)

    dmix_ref[...] = (dpool_ref[...] * slope_ref[...]).astype(BF16)
    spread_columns(dmix_ref[...], cols_ref)
    for k, rows in enumerate(pair_convolve(cols_ref, both_ref)):
        source_ref[:, :, k] = rows
    carried = carry_ref[...]
    for t in reversed(range(frames)):
        carried = decays_ref[0, t : t + 1] * (source_ref[t] + carried)
    carry_ref[...] = carried

    @pl.when(step == pl.num_programs(0) - 1)
    def _():
        end_ref[...] = carried


def out_grad_kernel(place_ref, states_ref, dmix_ref, grad_ref, cols_ref, acc_ref):
    step = pl.program_id(0)

    @pl.when(step == 0)
    def _():
        clear_edges(cols_ref)
        acc_ref[...] = jnp.zeros_like(acc_ref)

    spread_columns(states_ref[...], cols_ref)
    add_weight_product(cols_ref, dmix_ref[...], acc_ref)

    @pl.when(step == pl.num_programs(0) - 1)
    def _():
        grad_ref[...] = folded(acc_ref)


def in_grad_kernel(place_ref, got_ref, slope_ref, source_ref, decays_ref, income_ref, dpool_ref, skip_ref, grad_ref, cols_ref, carry_ref, dinput_ref, acc_ref):
    step = pl.program_id(0)
    frames, _, _, side, _ = slope_ref.shape

    @pl.when(step == 0)
    def _():
        clear_edges(cols_ref)
        take_carry(carry_ref, income_ref, place_ref[0] == 0)
        acc_ref[...] = jnp.zeros_like(acc_ref)

    spread_columns(got_ref[0, : frames * side * side].reshape(slope_ref.shape), cols_ref)
    carried = carry_ref[...]
    for t in reversed(range(frames)):
        carried = source_ref[t] + carried
        dmix = dpool_ref[...] * slope_ref[t]
        dinput_ref[t] = (carried + skip_ref[0] * dmix).astype(BF16)
        carried = decays_ref[0, t : t + 1] * carried
    carry_ref[...] = carried
    add_weight_product(cols_ref, dinput_ref[...], acc_ref)

    @pl.when(step == pl.num_programs(0) - 1)
    def _():
        grad_ref[...] = folded(acc_ref)


class Plan:
    def __init__(self, steps, frames, side, channels):
        self.steps, self.frames, self.side, self.channels = steps, frames, side, channels
        self.map = (side // 2, 2, side, channels)

    def whole(self, shape):
        return pl.BlockSpec(shape, lambda i, place: (0,) * len(shape))

    def order(self, back):
        return (lambda i: self.steps - 1 - i) if back else (lambda i: i)

    def maps(self, back=False):
        at = self.order(back)
        return pl.BlockSpec((self.frames, *self.map), lambda i, place: (at(i), 0, 0, 0, 0))

    def got(self, rows, back=False):
        at = self.order(back)
        return pl.BlockSpec((1, rows, self.channels), lambda i, place: (at(i), 0, 0))

    def decays(self, back=False):
        return self.got(self.frames, back)

    def of_view(self, rows):
        return pl.BlockSpec((1, rows, self.channels), lambda i, place: (place[1], 0, 0))

    def maps_of(self, dtype):
        return jax.ShapeDtypeStruct((self.steps * self.frames, *self.map), dtype)

    def carry_of(self):
        return jax.ShapeDtypeStruct(self.map, F32)

    def decays_of(self):
        return jax.ShapeDtypeStruct((self.steps, self.frames, self.channels), F32)

    def grad_of(self):
        return jax.ShapeDtypeStruct((9 * self.channels, self.channels), F32)

    def cols(self):
        return pltpu.VMEM((self.frames, self.side // 2 + 1, 2, self.side, 3 * self.channels), BF16)

    def carry(self):
        return pltpu.VMEM(self.map, F32)

    def acc(self):
        return pltpu.VMEM((2 * self.channels, 12 * self.channels), F32)

    def row(self):
        return self.whole((1, self.channels))

    def both(self):
        return pltpu.VMEM((12 * self.channels, 2 * self.channels), BF16)

    def call(self, kernel, in_specs, out_shape, out_specs, scratch):
        cells = self.steps * self.frames * self.side * self.side
        work = 2 * 9 * cells * self.channels * self.channels
        return pl.pallas_call(
            kernel,
            out_shape=out_shape,
            grid_spec=pltpu.PrefetchScalarGridSpec(
                num_scalar_prefetch=1,
                grid=(self.steps,),
                in_specs=in_specs,
                out_specs=out_specs,
                scratch_shapes=scratch,
            ),
            cost_estimate=pl.CostEstimate(flops=2 * work, transcendentals=0, bytes_accessed=4 * cells * self.channels),
            compiler_params=pltpu.CompilerParams(dimension_semantics=("arbitrary",), vmem_limit_bytes=16 << 20),
        )


def swapped(x):
    return lax.ppermute(x, "core", [(0, 1), (1, 0)])


def from_cores(x):
    here, there = x, swapped(x)
    first = lax.axis_index("core") == 0
    return jnp.stack([jnp.where(first, here, there), jnp.where(first, there, here)])


def from_all(x, axes):
    peers = lax.axis_size(axes)
    return lax.all_to_all(jnp.broadcast_to(x[None], (peers, *x.shape)), axes, 0, 0, tiled=True)


def in_parts(x):
    high = lax.reduce_precision(x, 8, 7)
    middle = lax.reduce_precision(x - high, 8, 7)
    low = x - high - middle
    return jnp.concatenate([high, middle, low], axis=-2).astype(jnp.bfloat16)


def clips_to_devices(rgb_maps, flow_maps, decay, half):
    clips, frames, side, _, channels = rgb_maps.shape
    straight = half == 0
    first = jnp.where(straight, rgb_maps, flow_maps)
    second = jnp.where(straight, flow_maps, rgb_maps)
    pieces = jnp.stack([first, second]).reshape(2, clips, frames * side * side, channels)
    parts = in_parts(jnp.where(straight, decay, decay[::-1]))
    parts = jnp.pad(parts, ((0, 0), (0, 16 - 3 * frames), (0, 0)))
    parts = jnp.broadcast_to(parts[:, None], (2, clips, 16, channels))
    sent = jnp.concatenate([pieces, parts], axis=2).reshape(2 * clips, -1, channels)
    return lax.all_to_all(sent, TIME, 0, 0, tiled=True)


def batch_norm(values):
    centered = values - jnp.mean(values, axis=0, keepdims=True)
    scale = lax.rsqrt(jnp.mean(centered * centered, axis=0, keepdims=True) + EPSILON)
    return centered * scale, scale


def norm_back(grad, normed, scale):
    mean = jnp.mean(grad, axis=0, keepdims=True)
    along = jnp.mean(grad * normed, axis=0, keepdims=True)
    return (grad - mean - normed * along) * scale


def across(a, b, **kinds):
    return lax.dot_general(a, b, (((1,), (1,)), ((), ())), preferred_element_type=F32, **kinds)


def projector_kernel(place_ref, seen_ref, in_ref, gain_ref, out_ref, dpool_ref, x_ref, n_ref, z_ref, zn_ref, *, cell_count):
    view, row = place_ref[1], place_ref[4]
    clips = seen_ref.shape[1]
    gain = gain_ref[...]
    pooled = jnp.concatenate([seen_ref[0] + seen_ref[3], seen_ref[1] + seen_ref[2]]) / cell_count
    hidden = jnp.dot(pooled, in_ref[...], precision=HIGHEST, preferred_element_type=F32)
    hidden_s, relus = [], []
    for v in range(2):
        x_ref[v], scale = batch_norm(hidden[v * clips : (v + 1) * clips])
        n_ref[v] = x_ref[v] * gain
        hidden_s.append(scale)
        relus.append(jnp.maximum(n_ref[v], 0.0).astype(BF16))
    z = jnp.dot(jnp.concatenate(relus), out_ref[...], preferred_element_type=F32)
    z_s = []
    for v in range(2):
        z_ref[v], scale = batch_norm(z[v * clips : (v + 1) * clips])
        zn_ref[v] = z_ref[v].astype(BF16)
        z_s.append(scale)
    first = view == 0
    own, other = zn_ref[view].astype(F32), zn_ref[1 - view].astype(F32)
    corr_diag = jnp.sum(own * other, axis=0, keepdims=True) / clips
    extra = -2.0 * (1.0 - corr_diag) - 2.0 * LAMBDA_OFF * corr_diag
    gram = across(zn_ref[1 - view], zn_ref[1 - view])
    spread = jnp.dot(gram, own, precision=HIGHEST, preferred_element_type=F32)
    dzn = spread * (2.0 * LAMBDA_OFF / (clips * clips)) + other * (extra / clips)
    dz_b = norm_back(dzn, z_ref[view], jnp.where(first, z_s[0], z_s[1])).astype(BF16)
    dxh = jnp.where(n_ref[view] > 0, across(dz_b, out_ref[...]), 0.0) * gain
    dhidden = norm_back(dxh, x_ref[view], jnp.where(first, hidden_s[0], hidden_s[1]))
    mine = lax.broadcasted_iota(jnp.int32, dhidden.shape, 0) == row
    own_row = jnp.sum(jnp.where(mine, dhidden, 0.0), axis=0, keepdims=True)
    rows = jnp.broadcast_to(own_row, (8, own_row.shape[1]))
    dpool_ref[...] = across(rows, in_ref[...], precision=HIGHEST)[:1] / cell_count


def projector_back(seen, proj_in, proj_gain, proj_out, place, cell_count):
    _, clips, channels = seen.shape
    width = proj_in.shape[1]
    wide = (2, clips, width)
    return pl.pallas_call(
        functools.partial(projector_kernel, cell_count=cell_count),
        out_shape=jax.ShapeDtypeStruct((1, channels), F32),
        in_specs=[pl.BlockSpec(memory_space=pltpu.SMEM)] + [pl.BlockSpec(memory_space=pltpu.VMEM)] * 4,
        scratch_shapes=[pltpu.VMEM(wide, F32), pltpu.VMEM(wide, F32), pltpu.VMEM(wide, F32), pltpu.VMEM(wide, BF16)],
        cost_estimate=pl.CostEstimate(flops=6 * clips * width * width, transcendentals=0, bytes_accessed=2 * width * width),
        compiler_params=pltpu.CompilerParams(vmem_limit_bytes=26 << 20),
    )(place, seen, proj_in, proj_gain.reshape(1, width), proj_out)


def from_other_half(x):
    return lax.ppermute(x, PLANE, [(0, 3), (1, 2), (2, 1), (3, 0)])


def from_peer(x, axes, k):
    return lax.ppermute(x, axes, [(i, i ^ k) for i in range(4)])


def from_ring(x, axes):
    return [x] + [from_peer(x, axes, k) for k in (1, 2, 3)]


def total_of(arrays):
    return sum(a.astype(F32) for a in arrays)


def place_kernel(place_ref, *refs):
    view, core, ring = place_ref[1], place_ref[2], place_ref[3]
    outs = refs[8:]
    for shift, pieces in enumerate((refs[:4], refs[4:8])):
        for k, piece in enumerate(pieces):
            rows = piece.shape[2]
            start = pl.multiple_of((4 * (core ^ shift) + (ring ^ k)) * rows, rows)
            for n, out in enumerate(outs):
                for v in range(2):
                    out[view ^ v, pl.ds(start, rows)] = piece[n, v].astype(F32)


def summed(grads, place):
    taps, channels = grads[0].shape
    core, ring = lax.axis_index("core"), lax.axis_index("z")
    halves = jnp.stack(grads).reshape(len(grads), 2, 4, taps // 8, channels)
    mine = lax.dynamic_index_in_dim(halves, core, 1, False)
    given = lax.dynamic_index_in_dim(halves, 1 - core, 1, False)
    pieces = (mine + swapped(given)).astype(BF16)
    parts = [lax.dynamic_index_in_dim(pieces, ring, 1, False)]
    parts += [from_peer(lax.dynamic_index_in_dim(pieces, ring ^ k, 1, False), "z", k) for k in (1, 2, 3)]
    parts = from_ring(total_of(parts).astype(BF16), "y")
    parts = from_ring(total_of(parts).astype(BF16), PLANE)
    both = jnp.stack([total_of([parts[0], parts[3]]), total_of([parts[1], parts[2]])], axis=1).astype(BF16)
    mine = from_ring(both, "z")
    given = [swapped(a) for a in mine]
    whole = jax.ShapeDtypeStruct((2, taps, channels), F32)
    return tuple(
        pl.pallas_call(
            place_kernel,
            out_shape=[whole] * len(grads),
            in_specs=[pl.BlockSpec(memory_space=pltpu.SMEM)] + [pl.BlockSpec(memory_space=pltpu.VMEM)] * 8,
            compiler_params=pltpu.CompilerParams(vmem_limit_bytes=16 << 20),
        )(place, *mine, *given)
    )


def per_device(
    rgb_maps, flow_maps, in_weights, out_weights, decay, skip, proj_in, proj_gain, proj_out
):
    half = lax.axis_index("xh")
    view = lax.axis_index("xl") ^ half
    _, frames_here, side, _, channels = rgb_maps.shape
    got = clips_to_devices(rgb_maps, flow_maps, decay, half)
    steps, rows, _ = got.shape
    cell_count = 2 * steps * frames_here * side * side
    plan = Plan(steps, frames_here, side, channels)
    taps = in_weights.shape[1]
    weights = plan.of_view(taps)
    skips = skip.reshape(2, 1, channels)
    place = jnp.stack([half, view, lax.axis_index("core"), lax.axis_index("z"), lax.axis_index(("y", "z", "core"))])
    place = place.astype(jnp.int32)
    carry_spec = plan.whole(plan.map)

    inputs, decays, end = plan.call(
        inputs_kernel,
        [plan.got(rows), weights],
        [plan.maps_of(BF16), plan.decays_of(), plan.carry_of()],
        [plan.maps(), plan.decays(), carry_spec],
        [plan.cols(), plan.both(), plan.carry()],
    )(place, got, in_weights)
    income = from_other_half(end)
    states_b, slope, pooled_part = plan.call(
        mixed_kernel,
        [plan.maps(), plan.decays(), carry_spec, plan.of_view(1), weights],
        [plan.maps_of(BF16), plan.maps_of(F32), jax.ShapeDtypeStruct((1, channels), F32)],
        [plan.maps(), plan.maps(), plan.row()],
        [plan.cols(), plan.both(), plan.carry(), pltpu.VMEM((side, channels), F32)],
    )(place, inputs, decays, income, skips, out_weights)

    seen = from_all(from_cores(pooled_part[0]), ("xh", "xl", "y", "z"))
    dpool = projector_back(seen.reshape(4, -1, channels), proj_in, proj_gain, proj_out, place, cell_count)

    dmix_b, source, end = plan.call(
        from_out_kernel,
        [plan.maps(True), plan.decays(True), plan.row(), weights],
        [plan.maps_of(BF16), plan.maps_of(F32), plan.carry_of()],
        [plan.maps(True), plan.maps(True), carry_spec],
        [plan.cols(), plan.both(), plan.carry()],
    )(place, slope, decays, dpool, out_weights)
    income = from_other_half(end)
    out_grad = plan.call(
        out_grad_kernel,
        [plan.maps(), plan.maps()],
        plan.grad_of(),
        plan.whole((9 * channels, channels)),
        [plan.cols(), plan.acc()],
    )(place, states_b, dmix_b)
    in_grad = plan.call(
        in_grad_kernel,
        [plan.got(rows, True), plan.maps(True), plan.maps(True), plan.decays(True), carry_spec, plan.row(), plan.of_view(1)],
        plan.grad_of(),
        plan.whole((9 * channels, channels)),
        [plan.cols(), plan.carry(), pltpu.VMEM((frames_here, *plan.map), BF16), plan.acc()],
    )(place, got, slope, source, decays, income, dpool, skips)
    return summed([in_grad, out_grad], place)


def solution(mesh):
    finer = Mesh(mesh.devices.reshape(2, 2, 4, 4, 2), ("xh", "xl", "y", "z", "core"))
    frames = ("xh", "xl", "y")
    return jax.shard_map(
        per_device,
        mesh=finer,
        in_specs=(
            P(("z", "core"), frames, None, None, None),
            P(("z", "core"), frames, None, None, None),
            P(),
            P(),
            P(None, frames, None),
            P(),
            P(),
            P(),
            P(),
        ),
        out_specs=(P(), P()),
        check_vma=False,
    )
```

```python
import functools

import jax
import jax.numpy as jnp
from jax import lax
from jax.experimental import pallas as pl
from jax.experimental.pallas import tpu as pltpu
from jax.sharding import Mesh
from jax.sharding import PartitionSpec as P

TIME = ("xl", "y")
PLANE = ("xh", "xl")


LAMBDA_OFF = 0.0051
EPSILON = 1e-05
HIGHEST = lax.Precision.HIGHEST


BF16, F32 = jnp.bfloat16, jnp.float32
CHUNKS = 4


def pair_weights(weights_ref, both_ref):
    taps, channels = weights_ref.shape[1:]
    third = taps // 3
    both_ref[:taps, :channels] = weights_ref[0]
    both_ref[taps:, :channels] = jnp.zeros((third, channels), BF16)
    both_ref[:third, channels:] = jnp.zeros((third, channels), BF16)
    both_ref[third:, channels:] = weights_ref[0]


def flipped_pair_weights(weights_ref, both_ref):
    taps, channels = weights_ref.shape[1:]
    third = taps // 3
    both_ref[taps:, :channels] = jnp.zeros((third, channels), BF16)
    both_ref[:third, channels:] = jnp.zeros((third, channels), BF16)
    for k in range(taps // channels):
        block = weights_ref[0, taps - (k + 1) * channels : taps - k * channels].astype(F32).T.astype(BF16)
        both_ref[k * channels : (k + 1) * channels, :channels] = block
        both_ref[third + k * channels : third + (k + 1) * channels, channels:] = block


def take_carry(carry_ref, income_ref, has_income):
    @pl.when(has_income)
    def _():
        carry_ref[...] = income_ref[...]

    @pl.when(jnp.logical_not(has_income))
    def _():
        carry_ref[...] = jnp.zeros_like(carry_ref)


def clear_edges(cols_ref):
    frames, _, _, side, lanes = cols_ref.shape
    cols_ref[:, 0, 0] = jnp.zeros((frames, side, lanes), BF16)
    cols_ref[:, side // 2, 1] = jnp.zeros((frames, side, lanes), BF16)


def spread_columns(maps, cols_ref):
    frames, pairs, _, side, channels = maps.shape
    flat = maps.astype(F32).reshape(frames * side * side, channels)
    column = lax.broadcasted_iota(jnp.int32, flat.shape, 0) & (side - 1)
    left = jnp.where(column == 0, 0.0, pltpu.roll(flat, 1, 0))
    right = jnp.where(column == side - 1, 0.0, pltpu.roll(flat, flat.shape[0] - 1, 0))
    for k, shifted in enumerate((left, flat, right)):
        rows = shifted.astype(BF16).reshape(frames, pairs, 2, side, channels)
        lanes = slice(k * channels, (k + 1) * channels)
        cols_ref[:, 0:pairs, 1, :, lanes] = rows[:, :, 0]
        cols_ref[:, 1 : pairs + 1, 0, :, lanes] = rows[:, :, 1]


def pair_patches(cols_ref):
    frames, ends, _, side, lanes = cols_ref.shape
    pairs = ends - 1
    pieces = [cols_ref[:, a : a + pairs, b].reshape(frames * pairs * side, lanes) for a in (0, 1) for b in (0, 1)]
    return jnp.concatenate(pieces, axis=1)


def pair_convolve(cols_ref, weights_ref):
    frames, ends, _, side, lanes = cols_ref.shape
    channels = lanes // 3
    both = jnp.dot(pair_patches(cols_ref), weights_ref[...], preferred_element_type=F32)
    shape = (frames, ends - 1, side, channels)
    return both[:, :channels].reshape(shape), both[:, channels:].reshape(shape)


def add_weight_product(cols, grads, acc_ref):
    frames, pairs, _, side, channels = grads.shape
    rows = frames * pairs * side
    both = [grads[:, :, k].reshape(rows, channels) for k in range(2)]
    acc_ref[...] += lax.dot_general(
        jnp.concatenate(both, axis=1),
        jnp.concatenate([pair_patches(cols_ref) for cols_ref in cols]),
        (((0,), (0,)), ((), ())),
        preferred_element_type=F32,
    )


def folded(acc_ref):
    channels = acc_ref.shape[0] // 2
    width = acc_ref.shape[1] // 4
    total = acc_ref[:channels, : 3 * width] + acc_ref[channels:, width:]
    return total.T


def spread_groups(groups, cols):
    for maps, cols_ref in zip(groups, cols):
        spread_columns(maps, cols_ref)


def halves(ref):
    group = ref.shape[0] // 2
    return [ref[:group], ref[group:]]


def got_maps(got_ref, shape):
    cells = shape[0] * shape[1] * shape[2] * shape[3] // 2
    return [got_ref[h, :cells].reshape(shape[0] // 2, *shape[1:]) for h in range(2)]


def decay_of(decays_ref, t):
    group = decays_ref.shape[1]
    return decays_ref[t // group, t % group : t % group + 1]


def inputs_kernel(place_ref, got_ref, weights_ref, inputs_ref, decays_ref, end_ref, cols_a, cols_b, both_ref, carry_ref):
    step = pl.program_id(0)
    cols = (cols_a, cols_b)
    frames, _, _, side, _ = inputs_ref.shape
    group = frames // 2
    cells = group * side * side

    @pl.when(step == 0)
    def _():
        clear_edges(cols_a)
        clear_edges(cols_b)
        pair_weights(weights_ref, both_ref)
        carry_ref[...] = jnp.zeros_like(carry_ref)

    spread_groups(got_maps(got_ref, inputs_ref.shape), cols)
    for h in range(2):
        parts = got_ref[h, cells:].astype(F32)
        decays_ref[h] = parts[:group] + parts[group : 2 * group] + parts[2 * group : 3 * group]
        for k, rows in enumerate(pair_convolve(cols[h], both_ref)):
            inputs_ref[h * group : (h + 1) * group, :, k] = rows.astype(BF16)
    carried = carry_ref[...]
    for t in range(frames):
        carried = decay_of(decays_ref, t) * carried + inputs_ref[t].astype(F32)
    carry_ref[...] = carried

    @pl.when(step == pl.num_programs(0) - 1)
    def _():
        end_ref[...] = carried


def mixed_kernel(place_ref, inputs_ref, decays_ref, income_ref, skip_ref, weights_ref, states_ref, slope_ref, pooled_ref, cols_a, cols_b, both_ref, carry_ref, sum_ref):
    step = pl.program_id(0)
    cols = (cols_a, cols_b)
    frames = inputs_ref.shape[0]
    group = frames // 2

    @pl.when(step == 0)
    def _():
        clear_edges(cols_a)
        clear_edges(cols_b)
        pair_weights(weights_ref, both_ref)
        take_carry(carry_ref, income_ref, place_ref[0] == 1)
        sum_ref[...] = jnp.zeros_like(sum_ref)

    carried = carry_ref[...]
    for t in range(frames):
        carried = decay_of(decays_ref, t) * carried + inputs_ref[t].astype(F32)
        states_ref[t] = carried.astype(BF16)
    carry_ref[...] = carried
    spread_groups(halves(states_ref), cols)
    total = sum_ref[...]
    for h in range(2):
        here = slice(h * group, (h + 1) * group)
        for k, rows in enumerate(pair_convolve(cols[h], both_ref)):
            mixed = rows + skip_ref[0] * inputs_ref[here, :, k].astype(F32)
            sigma = jax.nn.sigmoid(mixed)
            slope_ref[here, :, k] = sigma * (1.0 + mixed * (1.0 - sigma))
            total = total + jnp.sum(mixed * sigma, axis=(0, 1))
    sum_ref[...] = total

    @pl.when(step == pl.num_programs(0) - 1)
    def _():
        pooled_ref[...] = jnp.sum(total, axis=0, keepdims=True)


def from_out_kernel(place_ref, slope_ref, decays_ref, dpool_ref, weights_ref, dmix_ref, source_ref, end_ref, cols_a, cols_b, both_ref, carry_ref):
    step = pl.program_id(0)
    cols = (cols_a, cols_b)
    frames = slope_ref.shape[0]
    group = frames // 2

    @pl.when(step == 0)
    def _():
        clear_edges(cols_a)
        clear_edges(cols_b)
        flipped_pair_weights(weights_ref, both_ref)
        carry_ref[...] = jnp.zeros_like(carry_ref)

    dmix_ref[...] = (dpool_ref[...] * slope_ref[...]).astype(BF16)
    spread_groups(halves(dmix_ref), cols)
    for h in range(2):
        for k, rows in enumerate(pair_convolve(cols[h], both_ref)):
            source_ref[h * group : (h + 1) * group, :, k] = rows
    carried = carry_ref[...]
    for t in reversed(range(frames)):
        carried = decay_of(decays_ref, t) * (source_ref[t] + carried)
    carry_ref[...] = carried

    @pl.when(step == pl.num_programs(0) - 1)
    def _():
        end_ref[...] = carried


def out_grad_kernel(place_ref, states_ref, dmix_ref, grad_ref, cols_a, cols_b, acc_ref):
    step = pl.program_id(0)

    @pl.when(step == 0)
    def _():
        clear_edges(cols_a)
        clear_edges(cols_b)
        acc_ref[...] = jnp.zeros_like(acc_ref)

    spread_groups(halves(states_ref), (cols_a, cols_b))
    add_weight_product((cols_a, cols_b), dmix_ref[...], acc_ref)

    @pl.when(step == pl.num_programs(0) - 1)
    def _():
        grad_ref[...] = folded(acc_ref)


def in_grad_kernel(place_ref, got_ref, slope_ref, source_ref, decays_ref, income_ref, dpool_ref, skip_ref, grad_ref, cols_a, cols_b, carry_ref, dinput_ref, acc_ref):
    step = pl.program_id(0)
    frames = slope_ref.shape[0]

    @pl.when(step == 0)
    def _():
        clear_edges(cols_a)
        clear_edges(cols_b)
        take_carry(carry_ref, income_ref, place_ref[0] == 0)
        acc_ref[...] = jnp.zeros_like(acc_ref)

    spread_groups(got_maps(got_ref, slope_ref.shape), (cols_a, cols_b))
    carried = carry_ref[...]
    for t in reversed(range(frames)):
        carried = source_ref[t] + carried
        dmix = dpool_ref[...] * slope_ref[t]
        dinput_ref[t] = (carried + skip_ref[0] * dmix).astype(BF16)
        carried = decay_of(decays_ref, t) * carried
    carry_ref[...] = carried
    add_weight_product((cols_a, cols_b), dinput_ref[...], acc_ref)

    @pl.when(step == pl.num_programs(0) - 1)
    def _():
        grad_ref[...] = folded(acc_ref)


class Plan:
    def __init__(self, senders, group, side, channels):
        self.steps, self.frames, self.group, self.side, self.channels = senders // 2, 2 * group, group, side, channels
        self.map = (side // 2, 2, side, channels)

    def whole(self, shape):
        return pl.BlockSpec(shape, lambda i, place: (0,) * len(shape))

    def order(self, back):
        return (lambda i: self.steps - 1 - i) if back else (lambda i: i)

    def maps(self, back=False):
        at = self.order(back)
        return pl.BlockSpec((self.frames, *self.map), lambda i, place: (at(i), 0, 0, 0, 0))

    def got(self, rows, back=False):
        at = self.order(back)
        return pl.BlockSpec((2, rows, self.channels), lambda i, place: (at(i), 0, 0))

    def decays(self, back=False):
        return self.got(self.group, back)

    def of_view(self, rows):
        return pl.BlockSpec((1, rows, self.channels), lambda i, place: (place[1], 0, 0))

    def maps_of(self, dtype):
        return jax.ShapeDtypeStruct((self.steps * self.frames, *self.map), dtype)

    def carry_of(self):
        return jax.ShapeDtypeStruct(self.map, F32)

    def decays_of(self):
        return jax.ShapeDtypeStruct((2 * self.steps, self.group, self.channels), F32)

    def grad_of(self):
        return jax.ShapeDtypeStruct((9 * self.channels, self.channels), F32)

    def cols(self):
        return [pltpu.VMEM((self.group, self.side // 2 + 1, 2, self.side, 3 * self.channels), BF16)] * 2

    def carry(self):
        return pltpu.VMEM(self.map, F32)

    def acc(self):
        return pltpu.VMEM((2 * self.channels, 12 * self.channels), F32)

    def row(self):
        return self.whole((1, self.channels))

    def both(self):
        return pltpu.VMEM((12 * self.channels, 2 * self.channels), BF16)

    def call(self, kernel, in_specs, out_shape, out_specs, scratch):
        cells = self.steps * self.frames * self.side * self.side
        work = 2 * 9 * cells * self.channels * self.channels
        return pl.pallas_call(
            kernel,
            out_shape=out_shape,
            grid_spec=pltpu.PrefetchScalarGridSpec(
                num_scalar_prefetch=1,
                grid=(self.steps,),
                in_specs=in_specs,
                out_specs=out_specs,
                scratch_shapes=scratch,
            ),
            cost_estimate=pl.CostEstimate(flops=2 * work, transcendentals=0, bytes_accessed=4 * cells * self.channels),
            compiler_params=pltpu.CompilerParams(dimension_semantics=("arbitrary",), vmem_limit_bytes=24 << 20),
        )


def swapped(x):
    return lax.ppermute(x, "core", [(0, 1), (1, 0)])


def from_cores(x):
    here, there = x, swapped(x)
    first = lax.axis_index("core") == 0
    return jnp.stack([jnp.where(first, here, there), jnp.where(first, there, here)])


def from_all(x, axes):
    peers = lax.axis_size(axes)
    return lax.all_to_all(jnp.broadcast_to(x[None], (peers, *x.shape)), axes, 0, 0, tiled=True)


def in_hbm(x):
    return pltpu.with_memory_space_constraint(x, pltpu.HBM)


def pack_kernel(place_ref, rgb_ref, flow_ref, decay_ref, sent_ref):
    view = pl.program_id(0)
    frames, channels = decay_ref.shape[1:]
    cells = rgb_ref.shape[1] * rgb_ref.shape[2] * rgb_ref.shape[3]

    @pl.when(view == 0)
    def _():
        sent_ref[0, :cells] = rgb_ref[...].reshape(cells, channels)

    @pl.when(view == 1)
    def _():
        sent_ref[0, :cells] = flow_ref[...].reshape(cells, channels)

    decays = decay_ref[view]
    high = decays.astype(BF16).astype(F32)
    middle = (decays - high).astype(BF16).astype(F32)
    low = decays - high - middle
    rows = sent_ref.shape[1] - cells
    parts = [high, middle, low, jnp.zeros((rows - 3 * frames, channels), F32)]
    sent_ref[0, cells:] = jnp.concatenate(parts).astype(BF16)


def clips_to_devices(rgb_maps, flow_maps, decay, place):
    clips, frames, side, _, channels = rgb_maps.shape
    rows = frames * side * side + 16
    block = (1, *rgb_maps.shape[1:])
    sent = pl.pallas_call(
        pack_kernel,
        out_shape=pltpu.HBM((2 * clips, rows, channels), BF16),
        grid_spec=pltpu.PrefetchScalarGridSpec(
            num_scalar_prefetch=1,
            grid=(2, clips),
            in_specs=[
                pl.BlockSpec(block, lambda v, c, place: (jnp.where(v == 0, c, clips - 1), 0, 0, 0, 0)),
                pl.BlockSpec(block, lambda v, c, place: (jnp.where(v == 0, 0, c), 0, 0, 0, 0)),
                pl.BlockSpec(decay.shape, lambda v, c, place: (0, 0, 0)),
            ],
            out_specs=pl.BlockSpec((1, rows, channels), lambda v, c, place: ((v ^ place[0]) * clips + c, 0, 0)),
        ),
        compiler_params=pltpu.CompilerParams(vmem_limit_bytes=16 << 20),
    )(place, in_hbm(rgb_maps), in_hbm(flow_maps), decay)
    return lax.all_to_all(sent, TIME, 0, 0, tiled=True)


def batch_norm(values):
    centered = values - jnp.mean(values, axis=0, keepdims=True)
    scale = lax.rsqrt(jnp.mean(centered * centered, axis=0, keepdims=True) + EPSILON)
    return centered * scale, scale


def norm_back(grad, normed, scale):
    mean = jnp.mean(grad, axis=0, keepdims=True)
    along = jnp.mean(grad * normed, axis=0, keepdims=True)
    return (grad - mean - normed * along) * scale


def across(a, b, **kinds):
    return lax.dot_general(a, b, (((1,), (1,)), ((), ())), preferred_element_type=F32, **kinds)


def projector_kernel(place_ref, seen_ref, in_ref, gain_ref, far_ref, dpool_ref, x_ref, n_ref, z_ref, zn_ref, out_ref, sems, *, cell_count):
    view, row = place_ref[1], place_ref[4]
    clips = seen_ref.shape[1]
    chunk = out_ref.shape[1] // CHUNKS
    columns = [slice(j * chunk, (j + 1) * chunk) for j in range(CHUNKS)]
    copies = [pltpu.make_async_copy(far_ref.at[:, c], out_ref.at[:, c], sems.at[j]) for j, c in enumerate(columns)]
    for copy in copies:
        copy.start()
    gain = gain_ref[...]
    pooled = jnp.concatenate([seen_ref[0] + seen_ref[3], seen_ref[1] + seen_ref[2]]) / cell_count
    hidden = jnp.dot(pooled, in_ref[...], precision=HIGHEST, preferred_element_type=F32)
    hidden_s, relus = [], []
    for v in range(2):
        x_ref[v], scale = batch_norm(hidden[v * clips : (v + 1) * clips])
        n_ref[v] = x_ref[v] * gain
        hidden_s.append(scale)
        relus.append(jnp.maximum(n_ref[v], 0.0).astype(BF16))
    relu_b = jnp.concatenate(relus)
    scales = []
    for copy, c in zip(copies, columns):
        copy.wait()
        z = jnp.dot(relu_b, out_ref[:, c], preferred_element_type=F32)
        for v in range(2):
            z_ref[v, :, c], scale = batch_norm(z[v * clips : (v + 1) * clips])
            zn_ref[v, :, c] = z_ref[v, :, c].astype(BF16)
            scales.append(scale)
    z_s = [jnp.concatenate(scales[v::2], axis=1) for v in range(2)]
    first = view == 0
    own, other = zn_ref[view].astype(F32), zn_ref[1 - view].astype(F32)
    corr_diag = jnp.sum(own * other, axis=0, keepdims=True) / clips
    extra = -2.0 * (1.0 - corr_diag) - 2.0 * LAMBDA_OFF * corr_diag
    gram = across(zn_ref[1 - view], zn_ref[1 - view])
    spread = jnp.dot(gram, own, precision=HIGHEST, preferred_element_type=F32)
    dzn = spread * (2.0 * LAMBDA_OFF / (clips * clips)) + other * (extra / clips)
    dz_b = norm_back(dzn, z_ref[view], jnp.where(first, z_s[0], z_s[1])).astype(BF16)
    dxh = jnp.where(n_ref[view] > 0, across(dz_b, out_ref[...]), 0.0) * gain
    dhidden = norm_back(dxh, x_ref[view], jnp.where(first, hidden_s[0], hidden_s[1]))
    mine = lax.broadcasted_iota(jnp.int32, dhidden.shape, 0) == row
    own_row = jnp.sum(jnp.where(mine, dhidden, 0.0), axis=0, keepdims=True)
    rows = jnp.broadcast_to(own_row, (8, own_row.shape[1]))
    dpool_ref[...] = across(rows, in_ref[...], precision=HIGHEST)[:1] / cell_count


def projector_back(seen, proj_in, proj_gain, proj_out, place, cell_count):
    _, clips, channels = seen.shape
    width = proj_in.shape[1]
    wide = (2, clips, width)
    return pl.pallas_call(
        functools.partial(projector_kernel, cell_count=cell_count),
        out_shape=jax.ShapeDtypeStruct((1, channels), F32),
        in_specs=[pl.BlockSpec(memory_space=pltpu.SMEM)]
        + [pl.BlockSpec(memory_space=pltpu.VMEM)] * 3
        + [pl.BlockSpec(memory_space=pltpu.HBM)],
        scratch_shapes=[
            pltpu.VMEM(wide, F32),
            pltpu.VMEM(wide, F32),
            pltpu.VMEM(wide, F32),
            pltpu.VMEM(wide, BF16),
            pltpu.VMEM(proj_out.shape, BF16),
            pltpu.SemaphoreType.DMA((CHUNKS,)),
        ],
        cost_estimate=pl.CostEstimate(flops=6 * clips * width * width, transcendentals=0, bytes_accessed=2 * width * width),
        compiler_params=pltpu.CompilerParams(vmem_limit_bytes=26 << 20),
    )(place, seen, proj_in, proj_gain.reshape(1, width), in_hbm(proj_out))


def from_other_half(x):
    return lax.ppermute(x, PLANE, [(0, 3), (1, 2), (2, 1), (3, 0)])


def from_peer(x, axes, k):
    return lax.ppermute(x, axes, [(i, i ^ k) for i in range(4)])


def from_ring(x, axes):
    return [x] + [from_peer(x, axes, k) for k in (1, 2, 3)]


def total_of(arrays):
    return sum(a.astype(F32) for a in arrays)


def place_kernel(place_ref, *refs):
    view, core, ring = place_ref[1], place_ref[2], place_ref[3]
    outs = refs[8:]
    for shift, pieces in enumerate((refs[:4], refs[4:8])):
        for k, piece in enumerate(pieces):
            rows = piece.shape[2]
            start = pl.multiple_of((4 * (core ^ shift) + (ring ^ k)) * rows, rows)
            for n, out in enumerate(outs):
                for v in range(2):
                    out[view ^ v, pl.ds(start, rows)] = piece[n, v].astype(F32)


def summed(grads, place):
    taps, channels = grads[0].shape
    core, ring = lax.axis_index("core"), lax.axis_index("z")
    halves = jnp.stack(grads).reshape(len(grads), 2, 4, taps // 8, channels)
    mine = lax.dynamic_index_in_dim(halves, core, 1, False)
    given = lax.dynamic_index_in_dim(halves, 1 - core, 1, False)
    pieces = (mine + swapped(given)).astype(BF16)
    parts = [lax.dynamic_index_in_dim(pieces, ring, 1, False)]
    parts += [from_peer(lax.dynamic_index_in_dim(pieces, ring ^ k, 1, False), "z", k) for k in (1, 2, 3)]
    parts = from_ring(total_of(parts).astype(BF16), "y")
    parts = from_ring(total_of(parts).astype(BF16), PLANE)
    both = jnp.stack([total_of([parts[0], parts[3]]), total_of([parts[1], parts[2]])], axis=1).astype(BF16)
    mine = from_ring(both, "z")
    given = [swapped(a) for a in mine]
    whole = jax.ShapeDtypeStruct((2, taps, channels), F32)
    return tuple(
        pl.pallas_call(
            place_kernel,
            out_shape=[whole] * len(grads),
            in_specs=[pl.BlockSpec(memory_space=pltpu.SMEM)] + [pl.BlockSpec(memory_space=pltpu.VMEM)] * 8,
            compiler_params=pltpu.CompilerParams(vmem_limit_bytes=16 << 20),
        )(place, *mine, *given)
    )


def per_device(
    rgb_maps, flow_maps, in_weights, out_weights, decay, skip, proj_in, proj_gain, proj_out
):
    half = lax.axis_index("xh")
    view = lax.axis_index("xl") ^ half
    _, frames_here, side, _, channels = rgb_maps.shape
    place = jnp.stack([half, view, lax.axis_index("core"), lax.axis_index("z"), lax.axis_index(("y", "z", "core"))])
    place = place.astype(jnp.int32)
    got = clips_to_devices(rgb_maps, flow_maps, decay, place)
    senders, rows, _ = got.shape
    cell_count = 2 * senders * frames_here * side * side
    plan = Plan(senders, frames_here, side, channels)
    taps = in_weights.shape[1]
    weights = plan.of_view(taps)
    skips = skip.reshape(2, 1, channels)
    carry_spec = plan.whole(plan.map)

    inputs, decays, end = plan.call(
        inputs_kernel,
        [plan.got(rows), weights],
        [plan.maps_of(BF16), plan.decays_of(), plan.carry_of()],
        [plan.maps(), plan.decays(), carry_spec],
        [*plan.cols(), plan.both(), plan.carry()],
    )(place, got, in_weights)
    income = from_other_half(end)
    states_b, slope, pooled_part = plan.call(
        mixed_kernel,
        [plan.maps(), plan.decays(), carry_spec, plan.of_view(1), weights],
        [pltpu.HBM(a.shape, a.dtype) for a in (plan.maps_of(BF16), plan.maps_of(F32))] + [jax.ShapeDtypeStruct((1, channels), F32)],
        [plan.maps(), plan.maps(), plan.row()],
        [*plan.cols(), plan.both(), plan.carry(), pltpu.VMEM((side, channels), F32)],
    )(place, inputs, decays, income, skips, out_weights)

    seen = from_all(from_cores(pooled_part[0]), ("xh", "xl", "y", "z"))
    dpool = projector_back(seen.reshape(4, -1, channels), proj_in, proj_gain, proj_out, place, cell_count)

    dmix_b, source, end = plan.call(
        from_out_kernel,
        [plan.maps(True), plan.decays(True), plan.row(), weights],
        [plan.maps_of(BF16), plan.maps_of(F32), plan.carry_of()],
        [plan.maps(True), plan.maps(True), carry_spec],
        [*plan.cols(), plan.both(), plan.carry()],
    )(place, slope, decays, dpool, out_weights)
    income = from_other_half(end)
    out_grad = plan.call(
        out_grad_kernel,
        [plan.maps(), plan.maps()],
        plan.grad_of(),
        plan.whole((9 * channels, channels)),
        [*plan.cols(), plan.acc()],
    )(place, states_b, dmix_b)
    in_grad = plan.call(
        in_grad_kernel,
        [plan.got(rows, True), plan.maps(True), plan.maps(True), plan.decays(True), carry_spec, plan.row(), plan.of_view(1)],
        plan.grad_of(),
        plan.whole((9 * channels, channels)),
        [*plan.cols(), plan.carry(), pltpu.VMEM((plan.frames, *plan.map), BF16), plan.acc()],
    )(place, got, slope, source, decays, income, dpool, skips)
    return summed([in_grad, out_grad], place)


def solution(mesh):
    finer = Mesh(mesh.devices.reshape(2, 2, 4, 4, 2), ("xh", "xl", "y", "z", "core"))
    frames = ("xh", "xl", "y")
    return jax.shard_map(
        per_device,
        mesh=finer,
        in_specs=(
            P(("z", "core"), frames, None, None, None),
            P(("z", "core"), frames, None, None, None),
            P(),
            P(),
            P(None, frames, None),
            P(),
            P(),
            P(),
            P(),
        ),
        out_specs=(P(), P()),
        check_vma=False,
    )
```

```python
import functools

import jax
import jax.numpy as jnp
from jax import lax
from jax.experimental import pallas as pl
from jax.experimental.pallas import tpu as pltpu
from jax.sharding import Mesh
from jax.sharding import PartitionSpec as P

TIME = ("xl", "y")
PLANE = ("xh", "xl")


LAMBDA_OFF = 0.0051
EPSILON = 1e-05
HIGHEST = lax.Precision.HIGHEST


BF16, F32 = jnp.bfloat16, jnp.float32
CHUNKS = 4


def pair_weights(weights_ref, both_ref):
    taps, channels = weights_ref.shape[1:]
    third = taps // 3
    both_ref[:taps, :channels] = weights_ref[0]
    both_ref[taps:, :channels] = jnp.zeros((third, channels), BF16)
    both_ref[:third, channels:] = jnp.zeros((third, channels), BF16)
    both_ref[third:, channels:] = weights_ref[0]


def flipped_pair_weights(weights_ref, both_ref):
    taps, channels = weights_ref.shape[1:]
    third = taps // 3
    both_ref[taps:, :channels] = jnp.zeros((third, channels), BF16)
    both_ref[:third, channels:] = jnp.zeros((third, channels), BF16)
    for k in range(taps // channels):
        block = weights_ref[0, taps - (k + 1) * channels : taps - k * channels].astype(F32).T.astype(BF16)
        both_ref[k * channels : (k + 1) * channels, :channels] = block
        both_ref[third + k * channels : third + (k + 1) * channels, channels:] = block


def take_carry(carry_ref, income_ref, has_income):
    @pl.when(has_income)
    def _():
        carry_ref[...] = income_ref[...]

    @pl.when(jnp.logical_not(has_income))
    def _():
        carry_ref[...] = jnp.zeros_like(carry_ref)


def clear_edges(cols_ref):
    frames, _, _, side, lanes = cols_ref.shape
    cols_ref[:, 0, 0] = jnp.zeros((frames, side, lanes), BF16)
    cols_ref[:, side // 2, 1] = jnp.zeros((frames, side, lanes), BF16)


def spread_columns(maps, cols_ref):
    frames, pairs, _, side, channels = maps.shape
    flat = maps.astype(F32).reshape(frames * side * side, channels)
    column = lax.broadcasted_iota(jnp.int32, flat.shape, 0) & (side - 1)
    left = jnp.where(column == 0, 0.0, pltpu.roll(flat, 1, 0))
    right = jnp.where(column == side - 1, 0.0, pltpu.roll(flat, flat.shape[0] - 1, 0))
    for k, shifted in enumerate((left, flat, right)):
        rows = shifted.astype(BF16).reshape(frames, pairs, 2, side, channels)
        lanes = slice(k * channels, (k + 1) * channels)
        cols_ref[:, 0:pairs, 1, :, lanes] = rows[:, :, 0]
        cols_ref[:, 1 : pairs + 1, 0, :, lanes] = rows[:, :, 1]


def pair_patches(cols_ref):
    frames, ends, _, side, lanes = cols_ref.shape
    pairs = ends - 1
    pieces = [cols_ref[:, a : a + pairs, b].reshape(frames * pairs * side, lanes) for a in (0, 1) for b in (0, 1)]
    return jnp.concatenate(pieces, axis=1)


def pair_convolve(cols_ref, weights_ref):
    frames, ends, _, side, lanes = cols_ref.shape
    channels = lanes // 3
    both = jnp.dot(pair_patches(cols_ref), weights_ref[...], preferred_element_type=F32)
    shape = (frames, ends - 1, side, channels)
    return both[:, :channels].reshape(shape), both[:, channels:].reshape(shape)


def add_weight_product(cols, grads, acc_ref):
    frames, pairs, _, side, channels = grads.shape
    rows = frames * pairs * side
    both = [grads[:, :, k].reshape(rows, channels) for k in range(2)]
    acc_ref[...] += lax.dot_general(
        jnp.concatenate(both, axis=1),
        jnp.concatenate([pair_patches(cols_ref) for cols_ref in cols]),
        (((0,), (0,)), ((), ())),
        preferred_element_type=F32,
    )


def folded(acc_ref):
    channels = acc_ref.shape[0] // 2
    width = acc_ref.shape[1] // 4
    total = acc_ref[:channels, : 3 * width] + acc_ref[channels:, width:]
    return total.T


def spread_groups(groups, cols):
    for maps, cols_ref in zip(groups, cols):
        spread_columns(maps, cols_ref)


def halves(ref):
    group = ref.shape[0] // 2
    return [ref[:group], ref[group:]]


def got_maps(got_ref, shape):
    cells = shape[0] * shape[1] * shape[2] * shape[3] // 2
    return [got_ref[h, :cells].reshape(shape[0] // 2, *shape[1:]) for h in range(2)]


def decay_of(decays_ref, t):
    group = decays_ref.shape[1]
    return decays_ref[t // group, t % group : t % group + 1]


def inputs_step(step, last, place_ref, got_ref, weights_ref, inputs_ref, decays_ref, end_ref, cols_a, cols_b, both_ref, carry_ref):
    cols = (cols_a, cols_b)
    frames, _, _, side, _ = inputs_ref.shape
    group = frames // 2
    cells = group * side * side

    @pl.when(step == 0)
    def _():
        clear_edges(cols_a)
        clear_edges(cols_b)
        pair_weights(weights_ref, both_ref)
        carry_ref[...] = jnp.zeros_like(carry_ref)

    spread_groups(got_maps(got_ref, inputs_ref.shape), cols)
    for h in range(2):
        parts = got_ref[h, cells:].astype(F32)
        decays_ref[h] = parts[:group] + parts[group : 2 * group] + parts[2 * group : 3 * group]
        for k, rows in enumerate(pair_convolve(cols[h], both_ref)):
            inputs_ref[h * group : (h + 1) * group, :, k] = rows.astype(BF16)
    carried = carry_ref[...]
    for t in range(frames):
        carried = decay_of(decays_ref, t) * carried + inputs_ref[t].astype(F32)
    carry_ref[...] = carried

    @pl.when(step == last)
    def _():
        end_ref[...] = carried


def mixed_step(step, last, place_ref, inputs_ref, decays_ref, income_ref, skip_ref, weights_ref, states_ref, slope_ref, pooled_ref, cols_a, cols_b, both_ref, carry_ref, sum_ref):
    cols = (cols_a, cols_b)
    frames = inputs_ref.shape[0]
    group = frames // 2

    @pl.when(step == 0)
    def _():
        clear_edges(cols_a)
        clear_edges(cols_b)
        pair_weights(weights_ref, both_ref)
        take_carry(carry_ref, income_ref, place_ref[0] == 1)
        sum_ref[...] = jnp.zeros_like(sum_ref)

    carried = carry_ref[...]
    for t in range(frames):
        carried = decay_of(decays_ref, t) * carried + inputs_ref[t].astype(F32)
        states_ref[t] = carried.astype(BF16)
    carry_ref[...] = carried
    spread_groups(halves(states_ref), cols)
    total = sum_ref[...]
    for h in range(2):
        here = slice(h * group, (h + 1) * group)
        for k, rows in enumerate(pair_convolve(cols[h], both_ref)):
            mixed = rows + skip_ref[0] * inputs_ref[here, :, k].astype(F32)
            sigma = jax.nn.sigmoid(mixed)
            slope_ref[here, :, k] = sigma * (1.0 + mixed * (1.0 - sigma))
            total = total + jnp.sum(mixed * sigma, axis=(0, 1))
    sum_ref[...] = total

    @pl.when(step == last)
    def _():
        pooled_ref[...] = jnp.sum(total, axis=0, keepdims=True)


def from_out_step(step, last, place_ref, slope_ref, decays_ref, dpool_ref, weights_ref, dmix_ref, source_ref, end_ref, cols_a, cols_b, both_ref, carry_ref):
    cols = (cols_a, cols_b)
    frames = slope_ref.shape[0]
    group = frames // 2

    @pl.when(step == 0)
    def _():
        clear_edges(cols_a)
        clear_edges(cols_b)
        flipped_pair_weights(weights_ref, both_ref)
        carry_ref[...] = jnp.zeros_like(carry_ref)

    dmix_ref[...] = (dpool_ref[...] * slope_ref[...]).astype(BF16)
    spread_groups(halves(dmix_ref), cols)
    for h in range(2):
        for k, rows in enumerate(pair_convolve(cols[h], both_ref)):
            source_ref[h * group : (h + 1) * group, :, k] = rows
    carried = carry_ref[...]
    for t in reversed(range(frames)):
        carried = decay_of(decays_ref, t) * (source_ref[t] + carried)
    carry_ref[...] = carried

    @pl.when(step == last)
    def _():
        end_ref[...] = carried


def out_grad_step(step, last, place_ref, states_ref, dmix_ref, grad_ref, cols_a, cols_b, acc_ref):

    @pl.when(step == 0)
    def _():
        clear_edges(cols_a)
        clear_edges(cols_b)
        acc_ref[...] = jnp.zeros_like(acc_ref)

    spread_groups(halves(states_ref), (cols_a, cols_b))
    add_weight_product((cols_a, cols_b), dmix_ref[...], acc_ref)

    @pl.when(step == last)
    def _():
        grad_ref[...] = folded(acc_ref)


def in_grad_step(step, last, place_ref, got_ref, slope_ref, source_ref, decays_ref, income_ref, dpool_ref, skip_ref, grad_ref, cols_a, cols_b, carry_ref, dinput_ref, acc_ref):
    frames = slope_ref.shape[0]

    @pl.when(step == 0)
    def _():
        clear_edges(cols_a)
        clear_edges(cols_b)
        take_carry(carry_ref, income_ref, place_ref[0] == 0)
        acc_ref[...] = jnp.zeros_like(acc_ref)

    spread_groups(got_maps(got_ref, slope_ref.shape), (cols_a, cols_b))
    carried = carry_ref[...]
    for t in reversed(range(frames)):
        carried = source_ref[t] + carried
        dmix = dpool_ref[...] * slope_ref[t]
        dinput_ref[t] = (carried + skip_ref[0] * dmix).astype(BF16)
        carried = decay_of(decays_ref, t) * carried
    carry_ref[...] = carried
    add_weight_product((cols_a, cols_b), dinput_ref[...], acc_ref)

    @pl.when(step == last)
    def _():
        grad_ref[...] = folded(acc_ref)


class Plan:
    def __init__(self, senders, group, side, channels):
        self.steps, self.frames, self.group, self.side, self.channels = senders // 2, 2 * group, group, side, channels
        self.map = (side // 2, 2, side, channels)

    def maps_of(self, dtype):
        return jax.ShapeDtypeStruct((self.steps * self.frames, *self.map), dtype)

    def carry_of(self):
        return jax.ShapeDtypeStruct(self.map, F32)

    def decays_of(self):
        return jax.ShapeDtypeStruct((2 * self.steps, self.group, self.channels), F32)

    def grad_of(self):
        return jax.ShapeDtypeStruct((9 * self.channels, self.channels), F32)

    def cols(self):
        return [pltpu.VMEM((self.group, self.side // 2 + 1, 2, self.side, 3 * self.channels), BF16)] * 2

    def carry(self):
        return pltpu.VMEM(self.map, F32)

    def acc(self):
        return pltpu.VMEM((2 * self.channels, 12 * self.channels), F32)

    def both(self):
        return pltpu.VMEM((12 * self.channels, 2 * self.channels), BF16)

    def call(self, run, back, takes, out_shape, gives, scratch, kept=()):
        cells = self.steps * self.frames * self.side * self.side
        work = 2 * 9 * cells * self.channels * self.channels
        blocks = [*takes, *gives]
        buffers = [pltpu.VMEM(out_shape[n].shape, out_shape[n].dtype) for n in kept]
        sems = [pltpu.SemaphoreType.DMA((len(kept), self.steps))] if kept else []
        first_out = len(takes)

        def kernel(place_ref, *refs):
            arrays, rest = list(refs[: len(blocks)]), refs[len(blocks) :]
            far = {}
            for k, n in enumerate(kept):
                far[k] = arrays[first_out + n]
                arrays[first_out + n] = rest[k]
            rest = rest[len(kept) :]
            if kept:
                sems_ref, rest = rest[-1], rest[:-1]

            def copy_of(k, i):
                rows = pl.ds(i * gives[kept[k]], gives[kept[k]])
                return pltpu.make_async_copy(arrays[first_out + kept[k]].at[rows], far[k].at[rows], sems_ref.at[k, i])

            def step(i, _):
                at = self.steps - 1 - i if back else i
                views = []
                for ref, block in zip(arrays, blocks):
                    if block == "view":
                        views.append(ref.at[pl.ds(place_ref[1], 1)])
                    else:
                        views.append(ref if block is None else ref.at[pl.ds(at * block, block)])
                run(i, self.steps - 1, place_ref, *views, *rest)
                for k in range(len(kept)):
                    copy_of(k, at).start()
                return 0

            lax.fori_loop(0, self.steps, step, 0)
            for k in range(len(kept)):
                for i in range(self.steps):
                    copy_of(k, i).wait()

        vmem, hbm = pl.BlockSpec(memory_space=pltpu.VMEM), pl.BlockSpec(memory_space=pltpu.HBM)
        return pl.pallas_call(
            kernel,
            out_shape=[pltpu.HBM(o.shape, o.dtype) if n in kept else o for n, o in enumerate(out_shape)],
            in_specs=[pl.BlockSpec(memory_space=pltpu.SMEM)] + [vmem] * len(takes),
            out_specs=[hbm if n in kept else vmem for n in range(len(out_shape))],
            scratch_shapes=[*buffers, *scratch, *sems],
            cost_estimate=pl.CostEstimate(flops=2 * work, transcendentals=0, bytes_accessed=4 * cells * self.channels),
            compiler_params=pltpu.CompilerParams(vmem_limit_bytes=24 << 20),
        )


def swapped(x):
    return lax.ppermute(x, "core", [(0, 1), (1, 0)])


def from_cores(x):
    here, there = x, swapped(x)
    first = lax.axis_index("core") == 0
    return jnp.stack([jnp.where(first, here, there), jnp.where(first, there, here)])


def from_all(x, axes):
    peers = lax.axis_size(axes)
    return lax.all_to_all(jnp.broadcast_to(x[None], (peers, *x.shape)), axes, 0, 0, tiled=True)


def in_hbm(x):
    return pltpu.with_memory_space_constraint(x, pltpu.HBM)


def pack_kernel(place_ref, rgb_ref, flow_ref, decay_ref, sent_ref, parts_ref, map_sems, part_sems):
    half = place_ref[0]
    clips, cells, channels = rgb_ref.shape
    frames = decay_ref.shape[1]
    copies = []
    for v, maps_ref in enumerate((rgb_ref, flow_ref)):
        for c in range(clips):
            to = sent_ref.at[(v ^ half) * clips + c, :cells]
            copies.append(pltpu.make_async_copy(maps_ref.at[c], to, map_sems.at[v, c]))
    for copy in copies:
        copy.start()
    for v in range(2):
        decays = decay_ref[v]
        high = decays.astype(BF16).astype(F32)
        middle = (decays - high).astype(BF16).astype(F32)
        low = decays - high - middle
        parts = [high, middle, low, jnp.zeros((parts_ref.shape[1] - 3 * frames, channels), F32)]
        parts_ref[v] = jnp.concatenate(parts).astype(BF16)
    late = []
    for v in range(2):
        for c in range(clips):
            to = sent_ref.at[(v ^ half) * clips + c, cells:]
            late.append(pltpu.make_async_copy(parts_ref.at[v], to, part_sems.at[v, c]))
    for copy in late:
        copy.start()
    for copy in copies + late:
        copy.wait()


def clips_to_devices(rgb_maps, flow_maps, decay, place):
    clips, frames, side, _, channels = rgb_maps.shape
    cells = frames * side * side
    hbm = pl.BlockSpec(memory_space=pltpu.HBM)
    sent = pl.pallas_call(
        pack_kernel,
        out_shape=pltpu.HBM((2 * clips, cells + 16, channels), BF16),
        in_specs=[pl.BlockSpec(memory_space=pltpu.SMEM), hbm, hbm, pl.BlockSpec(memory_space=pltpu.VMEM)],
        out_specs=hbm,
        scratch_shapes=[
            pltpu.VMEM((2, 16, channels), BF16),
            pltpu.SemaphoreType.DMA((2, clips)),
            pltpu.SemaphoreType.DMA((2, clips)),
        ],
        compiler_params=pltpu.CompilerParams(vmem_limit_bytes=16 << 20),
    )(place, *(in_hbm(maps.reshape(clips, cells, channels)) for maps in (rgb_maps, flow_maps)), decay)
    return lax.all_to_all(sent, TIME, 0, 0, tiled=True)


def batch_norm(values):
    centered = values - jnp.mean(values, axis=0, keepdims=True)
    scale = lax.rsqrt(jnp.mean(centered * centered, axis=0, keepdims=True) + EPSILON)
    return centered * scale, scale


def norm_back(grad, normed, scale):
    mean = jnp.mean(grad, axis=0, keepdims=True)
    along = jnp.mean(grad * normed, axis=0, keepdims=True)
    return (grad - mean - normed * along) * scale


def across(a, b, **kinds):
    return lax.dot_general(a, b, (((1,), (1,)), ((), ())), preferred_element_type=F32, **kinds)


def projector_kernel(place_ref, seen_ref, in_ref, gain_ref, far_ref, dpool_ref, x_ref, n_ref, z_ref, zn_ref, out_ref, sems, *, cell_count):
    view, row = place_ref[1], place_ref[4]
    clips = seen_ref.shape[1]
    chunk = out_ref.shape[1] // CHUNKS
    columns = [slice(j * chunk, (j + 1) * chunk) for j in range(CHUNKS)]
    copies = [pltpu.make_async_copy(far_ref.at[:, c], out_ref.at[:, c], sems.at[j]) for j, c in enumerate(columns)]
    for copy in copies:
        copy.start()
    gain = gain_ref[...]
    pooled = jnp.concatenate([seen_ref[0] + seen_ref[3], seen_ref[1] + seen_ref[2]]) / cell_count
    hidden = jnp.dot(pooled, in_ref[...], precision=HIGHEST, preferred_element_type=F32)
    hidden_s, relus = [], []
    for v in range(2):
        x_ref[v], scale = batch_norm(hidden[v * clips : (v + 1) * clips])
        n_ref[v] = x_ref[v] * gain
        hidden_s.append(scale)
        relus.append(jnp.maximum(n_ref[v], 0.0).astype(BF16))
    relu_b = jnp.concatenate(relus)
    scales = []
    for copy, c in zip(copies, columns):
        copy.wait()
        z = jnp.dot(relu_b, out_ref[:, c], preferred_element_type=F32)
        for v in range(2):
            z_ref[v, :, c], scale = batch_norm(z[v * clips : (v + 1) * clips])
            zn_ref[v, :, c] = z_ref[v, :, c].astype(BF16)
            scales.append(scale)
    z_s = [jnp.concatenate(scales[v::2], axis=1) for v in range(2)]
    first = view == 0
    own, other = zn_ref[view].astype(F32), zn_ref[1 - view].astype(F32)
    corr_diag = jnp.sum(own * other, axis=0, keepdims=True) / clips
    extra = -2.0 * (1.0 - corr_diag) - 2.0 * LAMBDA_OFF * corr_diag
    gram = across(zn_ref[1 - view], zn_ref[1 - view])
    spread = jnp.dot(gram, own, precision=HIGHEST, preferred_element_type=F32)
    dzn = spread * (2.0 * LAMBDA_OFF / (clips * clips)) + other * (extra / clips)
    dz_b = norm_back(dzn, z_ref[view], jnp.where(first, z_s[0], z_s[1])).astype(BF16)
    dxh = jnp.where(n_ref[view] > 0, across(dz_b, out_ref[...]), 0.0) * gain
    dhidden = norm_back(dxh, x_ref[view], jnp.where(first, hidden_s[0], hidden_s[1]))
    mine = lax.broadcasted_iota(jnp.int32, dhidden.shape, 0) == row
    own_row = jnp.sum(jnp.where(mine, dhidden, 0.0), axis=0, keepdims=True)
    rows = jnp.broadcast_to(own_row, (8, own_row.shape[1]))
    dpool_ref[...] = across(rows, in_ref[...], precision=HIGHEST)[:1] / cell_count


def projector_back(seen, proj_in, proj_gain, proj_out, place, cell_count):
    _, clips, channels = seen.shape
    width = proj_in.shape[1]
    wide = (2, clips, width)
    return pl.pallas_call(
        functools.partial(projector_kernel, cell_count=cell_count),
        out_shape=jax.ShapeDtypeStruct((1, channels), F32),
        in_specs=[pl.BlockSpec(memory_space=pltpu.SMEM)]
        + [pl.BlockSpec(memory_space=pltpu.VMEM)] * 3
        + [pl.BlockSpec(memory_space=pltpu.HBM)],
        scratch_shapes=[
            pltpu.VMEM(wide, F32),
            pltpu.VMEM(wide, F32),
            pltpu.VMEM(wide, F32),
            pltpu.VMEM(wide, BF16),
            pltpu.VMEM(proj_out.shape, BF16),
            pltpu.SemaphoreType.DMA((CHUNKS,)),
        ],
        cost_estimate=pl.CostEstimate(flops=6 * clips * width * width, transcendentals=0, bytes_accessed=2 * width * width),
        compiler_params=pltpu.CompilerParams(vmem_limit_bytes=26 << 20),
    )(place, seen, proj_in, proj_gain.reshape(1, width), in_hbm(proj_out))


def from_other_half(x):
    return lax.ppermute(x, PLANE, [(0, 3), (1, 2), (2, 1), (3, 0)])


def from_peer(x, axes, k):
    return lax.ppermute(x, axes, [(i, i ^ k) for i in range(4)])


def from_ring(x, axes):
    return [x] + [from_peer(x, axes, k) for k in (1, 2, 3)]


def total_of(arrays):
    return sum(a.astype(F32) for a in arrays)


def place_kernel(place_ref, *refs):
    view, core, ring = place_ref[1], place_ref[2], place_ref[3]
    outs = refs[8:]
    for shift, pieces in enumerate((refs[:4], refs[4:8])):
        for k, piece in enumerate(pieces):
            rows = piece.shape[2]
            start = pl.multiple_of((4 * (core ^ shift) + (ring ^ k)) * rows, rows)
            for n, out in enumerate(outs):
                for v in range(2):
                    out[view ^ v, pl.ds(start, rows)] = piece[n, v].astype(F32)


def summed(grads, place):
    taps, channels = grads[0].shape
    core, ring = lax.axis_index("core"), lax.axis_index("z")
    halves = jnp.stack(grads).reshape(len(grads), 2, 4, taps // 8, channels)
    mine = lax.dynamic_index_in_dim(halves, core, 1, False)
    given = lax.dynamic_index_in_dim(halves, 1 - core, 1, False)
    pieces = (mine + swapped(given)).astype(BF16)
    parts = [lax.dynamic_index_in_dim(pieces, ring, 1, False)]
    parts += [from_peer(lax.dynamic_index_in_dim(pieces, ring ^ k, 1, False), "z", k) for k in (1, 2, 3)]
    parts = from_ring(total_of(parts).astype(BF16), "y")
    parts = from_ring(total_of(parts).astype(BF16), PLANE)
    both = jnp.stack([total_of([parts[0], parts[3]]), total_of([parts[1], parts[2]])], axis=1).astype(BF16)
    mine = from_ring(both, "z")
    given = [swapped(a) for a in mine]
    whole = jax.ShapeDtypeStruct((2, taps, channels), F32)
    return tuple(
        pl.pallas_call(
            place_kernel,
            out_shape=[whole] * len(grads),
            in_specs=[pl.BlockSpec(memory_space=pltpu.SMEM)] + [pl.BlockSpec(memory_space=pltpu.VMEM)] * 8,
            compiler_params=pltpu.CompilerParams(vmem_limit_bytes=16 << 20),
        )(place, *mine, *given)
    )


def per_device(
    rgb_maps, flow_maps, in_weights, out_weights, decay, skip, proj_in, proj_gain, proj_out
):
    half = lax.axis_index("xh")
    view = lax.axis_index("xl") ^ half
    _, frames_here, side, _, channels = rgb_maps.shape
    place = jnp.stack([half, view, lax.axis_index("core"), lax.axis_index("z"), lax.axis_index(("y", "z", "core"))])
    place = place.astype(jnp.int32)
    got = clips_to_devices(rgb_maps, flow_maps, decay, place)
    senders, rows, _ = got.shape
    cell_count = 2 * senders * frames_here * side * side
    plan = Plan(senders, frames_here, side, channels)
    skips = skip.reshape(2, 1, channels)
    here = plan.frames
    inputs, decays, end = plan.call(
        inputs_step,
        False,
        [2, "view"],
        [plan.maps_of(BF16), plan.decays_of(), plan.carry_of()],
        [here, 2, None],
        [*plan.cols(), plan.both(), plan.carry()],
    )(place, got, in_weights)
    income = from_other_half(end)
    states_b, slope, pooled_part = plan.call(
        mixed_step,
        False,
        [here, 2, None, "view", "view"],
        [plan.maps_of(BF16), plan.maps_of(F32), jax.ShapeDtypeStruct((1, channels), F32)],
        [here, here, None],
        [*plan.cols(), plan.both(), plan.carry(), pltpu.VMEM((side, channels), F32)],
        kept=(0, 1),
    )(place, inputs, decays, income, skips, out_weights)

    seen = from_all(from_cores(pooled_part[0]), ("xh", "xl", "y", "z"))
    dpool = projector_back(seen.reshape(4, -1, channels), proj_in, proj_gain, proj_out, place, cell_count)

    dmix_b, source, end = plan.call(
        from_out_step,
        True,
        [here, 2, None, "view"],
        [plan.maps_of(BF16), plan.maps_of(F32), plan.carry_of()],
        [here, here, None],
        [*plan.cols(), plan.both(), plan.carry()],
    )(place, slope, decays, dpool, out_weights)
    income = from_other_half(end)
    (out_grad,) = plan.call(
        out_grad_step,
        False,
        [here, here],
        [plan.grad_of()],
        [None],
        [*plan.cols(), plan.acc()],
    )(place, states_b, dmix_b)
    (in_grad,) = plan.call(
        in_grad_step,
        True,
        [2, here, here, 2, None, None, "view"],
        [plan.grad_of()],
        [None],
        [*plan.cols(), plan.carry(), pltpu.VMEM((here, *plan.map), BF16), plan.acc()],
    )(place, got, slope, source, decays, income, dpool, skips)
    return summed([in_grad, out_grad], place)


def solution(mesh):
    finer = Mesh(mesh.devices.reshape(2, 2, 4, 4, 2), ("xh", "xl", "y", "z", "core"))
    frames = ("xh", "xl", "y")
    return jax.shard_map(
        per_device,
        mesh=finer,
        in_specs=(
            P(("z", "core"), frames, None, None, None),
            P(("z", "core"), frames, None, None, None),
            P(),
            P(),
            P(None, frames, None),
            P(),
            P(),
            P(),
            P(),
        ),
        out_specs=(P(), P()),
        check_vma=False,
    )
```

```python
import functools

import jax
import jax.numpy as jnp
from jax import lax
from jax.experimental import pallas as pl
from jax.experimental.pallas import tpu as pltpu
from jax.sharding import Mesh
from jax.sharding import PartitionSpec as P

TIME = ("xl", "y")
PLANE = ("xh", "xl")


LAMBDA_OFF = 0.0051
EPSILON = 1e-05
HIGHEST = lax.Precision.HIGHEST


BF16, F32 = jnp.bfloat16, jnp.float32
CHUNKS = 4


def pair_weights(weights_ref, both_ref):
    taps, channels = weights_ref.shape[1:]
    third = taps // 3
    both_ref[:taps, :channels] = weights_ref[0]
    both_ref[taps:, :channels] = jnp.zeros((third, channels), BF16)
    both_ref[:third, channels:] = jnp.zeros((third, channels), BF16)
    both_ref[third:, channels:] = weights_ref[0]


def flipped_pair_weights(weights_ref, both_ref):
    taps, channels = weights_ref.shape[1:]
    third = taps // 3
    both_ref[taps:, :channels] = jnp.zeros((third, channels), BF16)
    both_ref[:third, channels:] = jnp.zeros((third, channels), BF16)
    for k in range(taps // channels):
        block = weights_ref[0, taps - (k + 1) * channels : taps - k * channels].astype(F32).T.astype(BF16)
        both_ref[k * channels : (k + 1) * channels, :channels] = block
        both_ref[third + k * channels : third + (k + 1) * channels, channels:] = block


def take_carry(carry_ref, income_ref, has_income):
    @pl.when(has_income)
    def _():
        carry_ref[...] = income_ref[...]

    @pl.when(jnp.logical_not(has_income))
    def _():
        carry_ref[...] = jnp.zeros_like(carry_ref)


def clear_edges(cols_ref):
    frames, _, _, side, lanes = cols_ref.shape
    cols_ref[:, 0, 0] = jnp.zeros((frames, side, lanes), BF16)
    cols_ref[:, side // 2, 1] = jnp.zeros((frames, side, lanes), BF16)


def spread_columns(maps, cols_ref):
    frames, pairs, _, side, channels = maps.shape
    flat = maps.astype(F32).reshape(frames * side * side, channels)
    column = lax.broadcasted_iota(jnp.int32, flat.shape, 0) & (side - 1)
    left = jnp.where(column == 0, 0.0, pltpu.roll(flat, 1, 0))
    right = jnp.where(column == side - 1, 0.0, pltpu.roll(flat, flat.shape[0] - 1, 0))
    for k, shifted in enumerate((left, flat, right)):
        rows = shifted.astype(BF16).reshape(frames, pairs, 2, side, channels)
        lanes = slice(k * channels, (k + 1) * channels)
        cols_ref[:, 0:pairs, 1, :, lanes] = rows[:, :, 0]
        cols_ref[:, 1 : pairs + 1, 0, :, lanes] = rows[:, :, 1]


def pair_patches(cols_ref):
    frames, ends, _, side, lanes = cols_ref.shape
    pairs = ends - 1
    pieces = [cols_ref[:, a : a + pairs, b].reshape(frames * pairs * side, lanes) for a in (0, 1) for b in (0, 1)]
    return jnp.concatenate(pieces, axis=1)


def pair_convolve(cols_ref, weights_ref):
    frames, ends, _, side, lanes = cols_ref.shape
    channels = lanes // 3
    both = jnp.dot(pair_patches(cols_ref), weights_ref[...], preferred_element_type=F32)
    shape = (frames, ends - 1, side, channels)
    return both[:, :channels].reshape(shape), both[:, channels:].reshape(shape)


def add_weight_product(cols, grads, acc_ref):
    frames, pairs, _, side, channels = grads.shape
    rows = frames * pairs * side
    both = [grads[:, :, k].reshape(rows, channels) for k in range(2)]
    acc_ref[...] += lax.dot_general(
        jnp.concatenate(both, axis=1),
        jnp.concatenate([pair_patches(cols_ref) for cols_ref in cols]),
        (((0,), (0,)), ((), ())),
        preferred_element_type=F32,
    )


def folded(acc_ref):
    channels = acc_ref.shape[0] // 2
    width = acc_ref.shape[1] // 4
    total = acc_ref[:channels, : 3 * width] + acc_ref[channels:, width:]
    return total.T


def spread_groups(groups, cols):
    for maps, cols_ref in zip(groups, cols):
        spread_columns(maps, cols_ref)


def halves(ref):
    group = ref.shape[0] // 2
    return [ref[:group], ref[group:]]


def got_maps(got_ref, shape):
    cells = shape[0] * shape[1] * shape[2] * shape[3] // 2
    return [got_ref[h, :cells].reshape(shape[0] // 2, *shape[1:]) for h in range(2)]


def decay_of(decays_ref, t):
    group = decays_ref.shape[1]
    return decays_ref[t // group, t % group : t % group + 1]


def inputs_step(step, last, place_ref, got_ref, weights_ref, inputs_ref, decays_ref, end_ref, cols_a, cols_b, both_ref, carry_ref):
    cols = (cols_a, cols_b)
    frames, _, _, side, _ = inputs_ref.shape
    group = frames // 2
    cells = group * side * side

    @pl.when(step == 0)
    def _():
        clear_edges(cols_a)
        clear_edges(cols_b)
        pair_weights(weights_ref, both_ref)
        carry_ref[...] = jnp.zeros_like(carry_ref)

    spread_groups(got_maps(got_ref, inputs_ref.shape), cols)
    for h in range(2):
        parts = got_ref[h, cells:].astype(F32)
        decays_ref[h] = parts[:group] + parts[group : 2 * group] + parts[2 * group : 3 * group]
        for k, rows in enumerate(pair_convolve(cols[h], both_ref)):
            inputs_ref[h * group : (h + 1) * group, :, k] = rows.astype(BF16)
    carried = carry_ref[...]
    for t in range(frames):
        carried = decay_of(decays_ref, t) * carried + inputs_ref[t].astype(F32)
    carry_ref[...] = carried

    @pl.when(step == last)
    def _():
        end_ref[...] = carried


def mixed_step(step, last, place_ref, inputs_ref, decays_ref, income_ref, skip_ref, weights_ref, states_ref, slope_ref, pooled_ref, cols_a, cols_b, both_ref, carry_ref, sum_ref):
    cols = (cols_a, cols_b)
    frames = inputs_ref.shape[0]
    group = frames // 2

    @pl.when(step == 0)
    def _():
        clear_edges(cols_a)
        clear_edges(cols_b)
        pair_weights(weights_ref, both_ref)
        take_carry(carry_ref, income_ref, place_ref[0] == 1)
        sum_ref[...] = jnp.zeros_like(sum_ref)

    carried = carry_ref[...]
    for t in range(frames):
        carried = decay_of(decays_ref, t) * carried + inputs_ref[t].astype(F32)
        states_ref[t] = carried.astype(BF16)
    carry_ref[...] = carried
    spread_groups(halves(states_ref), cols)
    total = sum_ref[...]
    for h in range(2):
        here = slice(h * group, (h + 1) * group)
        for k, rows in enumerate(pair_convolve(cols[h], both_ref)):
            mixed = rows + skip_ref[0] * inputs_ref[here, :, k].astype(F32)
            sigma = jax.nn.sigmoid(mixed)
            slope_ref[here, :, k] = sigma * (1.0 + mixed * (1.0 - sigma))
            total = total + jnp.sum(mixed * sigma, axis=(0, 1))
    sum_ref[...] = total

    @pl.when(step == last)
    def _():
        pooled_ref[...] = jnp.sum(total, axis=0, keepdims=True)


def from_out_step(step, last, place_ref, slope_ref, decays_ref, dpool_ref, weights_ref, dmix_ref, source_ref, end_ref, cols_a, cols_b, both_ref, carry_ref):
    cols = (cols_a, cols_b)
    frames = slope_ref.shape[0]
    group = frames // 2

    @pl.when(step == 0)
    def _():
        clear_edges(cols_a)
        clear_edges(cols_b)
        flipped_pair_weights(weights_ref, both_ref)
        carry_ref[...] = jnp.zeros_like(carry_ref)

    dmix_ref[...] = (dpool_ref[...] * slope_ref[...]).astype(BF16)
    spread_groups(halves(dmix_ref), cols)
    for h in range(2):
        for k, rows in enumerate(pair_convolve(cols[h], both_ref)):
            source_ref[h * group : (h + 1) * group, :, k] = rows
    carried = carry_ref[...]
    for t in reversed(range(frames)):
        carried = decay_of(decays_ref, t) * (source_ref[t] + carried)
    carry_ref[...] = carried

    @pl.when(step == last)
    def _():
        end_ref[...] = carried


def out_grad_step(step, last, place_ref, states_ref, dmix_ref, grad_ref, cols_a, cols_b, acc_ref):

    @pl.when(step == 0)
    def _():
        clear_edges(cols_a)
        clear_edges(cols_b)
        acc_ref[...] = jnp.zeros_like(acc_ref)

    spread_groups(halves(states_ref), (cols_a, cols_b))
    add_weight_product((cols_a, cols_b), dmix_ref[...], acc_ref)

    @pl.when(step == last)
    def _():
        grad_ref[...] = folded(acc_ref)


def in_grad_step(step, last, place_ref, got_ref, slope_ref, source_ref, decays_ref, income_ref, dpool_ref, skip_ref, grad_ref, cols_a, cols_b, carry_ref, dinput_ref, acc_ref):
    frames = slope_ref.shape[0]

    @pl.when(step == 0)
    def _():
        clear_edges(cols_a)
        clear_edges(cols_b)
        take_carry(carry_ref, income_ref, place_ref[0] == 0)
        acc_ref[...] = jnp.zeros_like(acc_ref)

    spread_groups(got_maps(got_ref, slope_ref.shape), (cols_a, cols_b))
    carried = carry_ref[...]
    for t in reversed(range(frames)):
        carried = source_ref[t] + carried
        dmix = dpool_ref[...] * slope_ref[t]
        dinput_ref[t] = (carried + skip_ref[0] * dmix).astype(BF16)
        carried = decay_of(decays_ref, t) * carried
    carry_ref[...] = carried
    add_weight_product((cols_a, cols_b), dinput_ref[...], acc_ref)

    @pl.when(step == last)
    def _():
        grad_ref[...] = folded(acc_ref)


class Plan:
    def __init__(self, senders, group, side, channels):
        self.steps, self.frames, self.group, self.side, self.channels = senders // 2, 2 * group, group, side, channels
        self.map = (side // 2, 2, side, channels)

    def maps_of(self, dtype):
        return jax.ShapeDtypeStruct((self.steps * self.frames, *self.map), dtype)

    def carry_of(self):
        return jax.ShapeDtypeStruct(self.map, F32)

    def decays_of(self):
        return jax.ShapeDtypeStruct((2 * self.steps, self.group, self.channels), F32)

    def grad_of(self):
        return jax.ShapeDtypeStruct((9 * self.channels, self.channels), F32)

    def cols(self):
        return [pltpu.VMEM((self.group, self.side // 2 + 1, 2, self.side, 3 * self.channels), BF16)] * 2

    def carry(self):
        return pltpu.VMEM(self.map, F32)

    def acc(self):
        return pltpu.VMEM((2 * self.channels, 12 * self.channels), F32)

    def both(self):
        return pltpu.VMEM((12 * self.channels, 2 * self.channels), BF16)

    def call(self, run, back, takes, out_shape, gives, scratch, kept=()):
        cells = self.steps * self.frames * self.side * self.side
        work = 2 * 9 * cells * self.channels * self.channels
        blocks = [*takes, *gives]
        buffers = [pltpu.VMEM(out_shape[n].shape, out_shape[n].dtype) for n in kept]
        sems = [pltpu.SemaphoreType.DMA((len(kept), self.steps))] if kept else []
        first_out = len(takes)

        def kernel(place_ref, *refs):
            arrays, rest = list(refs[: len(blocks)]), refs[len(blocks) :]
            far = {}
            for k, n in enumerate(kept):
                far[k] = arrays[first_out + n]
                arrays[first_out + n] = rest[k]
            rest = rest[len(kept) :]
            if kept:
                sems_ref, rest = rest[-1], rest[:-1]

            def copy_of(k, i):
                rows = pl.ds(i * gives[kept[k]], gives[kept[k]])
                return pltpu.make_async_copy(arrays[first_out + kept[k]].at[rows], far[k].at[rows], sems_ref.at[k, i])

            def step(i, _):
                at = self.steps - 1 - i if back else i
                views = []
                for ref, block in zip(arrays, blocks):
                    if block == "view":
                        views.append(ref.at[pl.ds(place_ref[1], 1)])
                    else:
                        views.append(ref if block is None else ref.at[pl.ds(at * block, block)])
                run(i, self.steps - 1, place_ref, *views, *rest)
                for k in range(len(kept)):
                    copy_of(k, at).start()
                return 0

            lax.fori_loop(0, self.steps, step, 0)
            for k in range(len(kept)):
                for i in range(self.steps):
                    copy_of(k, i).wait()

        vmem, hbm = pl.BlockSpec(memory_space=pltpu.VMEM), pl.BlockSpec(memory_space=pltpu.HBM)
        return pl.pallas_call(
            kernel,
            out_shape=[pltpu.HBM(o.shape, o.dtype) if n in kept else o for n, o in enumerate(out_shape)],
            in_specs=[pl.BlockSpec(memory_space=pltpu.SMEM)] + [vmem] * len(takes),
            out_specs=[hbm if n in kept else vmem for n in range(len(out_shape))],
            scratch_shapes=[*buffers, *scratch, *sems],
            cost_estimate=pl.CostEstimate(flops=2 * work, transcendentals=0, bytes_accessed=4 * cells * self.channels),
            compiler_params=pltpu.CompilerParams(vmem_limit_bytes=24 << 20),
        )


def swapped(x):
    return lax.ppermute(x, "core", [(0, 1), (1, 0)])


def from_cores(x):
    here, there = x, swapped(x)
    first = lax.axis_index("core") == 0
    return jnp.stack([jnp.where(first, here, there), jnp.where(first, there, here)])


def from_all(x, axes):
    peers = lax.axis_size(axes)
    return lax.all_to_all(jnp.broadcast_to(x[None], (peers, *x.shape)), axes, 0, 0, tiled=True)


def in_hbm(x):
    return pltpu.with_memory_space_constraint(x, pltpu.HBM)


def pack_kernel(place_ref, rgb_ref, flow_ref, decay_ref, sent_ref, map_sems):
    half = place_ref[0]
    clips, cells, channels = rgb_ref.shape
    frames = decay_ref.shape[1]
    copies = []
    for v, maps_ref in enumerate((rgb_ref, flow_ref)):
        for c in range(clips):
            to = sent_ref.at[(v ^ half) * clips + c, :cells]
            copies.append(pltpu.make_async_copy(maps_ref.at[c], to, map_sems.at[v, c]))
    for copy in copies:
        copy.start()
    for v in range(2):
        decays = decay_ref[v]
        high = decays.astype(BF16).astype(F32)
        middle = (decays - high).astype(BF16).astype(F32)
        low = decays - high - middle
        rows = sent_ref.shape[1] - cells
        parts = [high, middle, low, jnp.zeros((rows - 3 * frames, channels), F32)]
        parts = jnp.concatenate(parts).astype(BF16)
        for c in range(clips):
            sent_ref[(v ^ half) * clips + c, cells:] = parts
    for copy in copies:
        copy.wait()


def clips_to_devices(rgb_maps, flow_maps, decay, place):
    clips, frames, side, _, channels = rgb_maps.shape
    cells = frames * side * side
    hbm = pl.BlockSpec(memory_space=pltpu.HBM)
    sent = pl.pallas_call(
        pack_kernel,
        out_shape=jax.ShapeDtypeStruct((2 * clips, cells + 16, channels), BF16),
        in_specs=[pl.BlockSpec(memory_space=pltpu.SMEM), hbm, hbm, pl.BlockSpec(memory_space=pltpu.VMEM)],
        out_specs=pl.BlockSpec(memory_space=pltpu.VMEM),
        scratch_shapes=[pltpu.SemaphoreType.DMA((2, clips))],
        compiler_params=pltpu.CompilerParams(vmem_limit_bytes=16 << 20),
    )(place, *(in_hbm(maps.reshape(clips, cells, channels)) for maps in (rgb_maps, flow_maps)), decay)
    return lax.all_to_all(sent, TIME, 0, 0, tiled=True)


def batch_norm(values):
    centered = values - jnp.mean(values, axis=0, keepdims=True)
    scale = lax.rsqrt(jnp.mean(centered * centered, axis=0, keepdims=True) + EPSILON)
    return centered * scale, scale


def norm_back(grad, normed, scale):
    mean = jnp.mean(grad, axis=0, keepdims=True)
    along = jnp.mean(grad * normed, axis=0, keepdims=True)
    return (grad - mean - normed * along) * scale


def across(a, b, **kinds):
    return lax.dot_general(a, b, (((1,), (1,)), ((), ())), preferred_element_type=F32, **kinds)


def projector_kernel(place_ref, seen_ref, in_ref, gain_ref, far_ref, dpool_ref, x_ref, n_ref, z_ref, zn_ref, out_ref, sems, *, cell_count):
    view, row = place_ref[1], place_ref[4]
    clips = seen_ref.shape[1]
    chunk = out_ref.shape[1] // CHUNKS
    columns = [slice(j * chunk, (j + 1) * chunk) for j in range(CHUNKS)]
    copies = [pltpu.make_async_copy(far_ref.at[:, c], out_ref.at[:, c], sems.at[j]) for j, c in enumerate(columns)]
    for copy in copies:
        copy.start()
    gain = gain_ref[...]
    pooled = jnp.concatenate([seen_ref[0] + seen_ref[3], seen_ref[1] + seen_ref[2]]) / cell_count
    hidden = jnp.dot(pooled, in_ref[...], precision=HIGHEST, preferred_element_type=F32)
    hidden_s, relus = [], []
    for v in range(2):
        x_ref[v], scale = batch_norm(hidden[v * clips : (v + 1) * clips])
        n_ref[v] = x_ref[v] * gain
        hidden_s.append(scale)
        relus.append(jnp.maximum(n_ref[v], 0.0).astype(BF16))
    relu_b = jnp.concatenate(relus)
    scales = []
    for copy, c in zip(copies, columns):
        copy.wait()
        z = jnp.dot(relu_b, out_ref[:, c], preferred_element_type=F32)
        for v in range(2):
            z_ref[v, :, c], scale = batch_norm(z[v * clips : (v + 1) * clips])
            zn_ref[v, :, c] = z_ref[v, :, c].astype(BF16)
            scales.append(scale)
    z_s = [jnp.concatenate(scales[v::2], axis=1) for v in range(2)]
    first = view == 0
    own, other = zn_ref[view].astype(F32), zn_ref[1 - view].astype(F32)
    corr_diag = jnp.sum(own * other, axis=0, keepdims=True) / clips
    extra = -2.0 * (1.0 - corr_diag) - 2.0 * LAMBDA_OFF * corr_diag
    gram = across(zn_ref[1 - view], zn_ref[1 - view])
    spread = jnp.dot(gram, own, precision=HIGHEST, preferred_element_type=F32)
    dzn = spread * (2.0 * LAMBDA_OFF / (clips * clips)) + other * (extra / clips)
    dz_b = norm_back(dzn, z_ref[view], jnp.where(first, z_s[0], z_s[1])).astype(BF16)
    dxh = jnp.where(n_ref[view] > 0, across(dz_b, out_ref[...]), 0.0) * gain
    dhidden = norm_back(dxh, x_ref[view], jnp.where(first, hidden_s[0], hidden_s[1]))
    mine = lax.broadcasted_iota(jnp.int32, dhidden.shape, 0) == row
    own_row = jnp.sum(jnp.where(mine, dhidden, 0.0), axis=0, keepdims=True)
    rows = jnp.broadcast_to(own_row, (8, own_row.shape[1]))
    dpool_ref[...] = across(rows, in_ref[...], precision=HIGHEST)[:1] / cell_count


def projector_back(seen, proj_in, proj_gain, proj_out, place, cell_count):
    _, clips, channels = seen.shape
    width = proj_in.shape[1]
    wide = (2, clips, width)
    return pl.pallas_call(
        functools.partial(projector_kernel, cell_count=cell_count),
        out_shape=jax.ShapeDtypeStruct((1, channels), F32),
        in_specs=[pl.BlockSpec(memory_space=pltpu.SMEM)]
        + [pl.BlockSpec(memory_space=pltpu.VMEM)] * 3
        + [pl.BlockSpec(memory_space=pltpu.HBM)],
        scratch_shapes=[
            pltpu.VMEM(wide, F32),
            pltpu.VMEM(wide, F32),
            pltpu.VMEM(wide, F32),
            pltpu.VMEM(wide, BF16),
            pltpu.VMEM(proj_out.shape, BF16),
            pltpu.SemaphoreType.DMA((CHUNKS,)),
        ],
        cost_estimate=pl.CostEstimate(flops=6 * clips * width * width, transcendentals=0, bytes_accessed=2 * width * width),
        compiler_params=pltpu.CompilerParams(vmem_limit_bytes=26 << 20),
    )(place, seen, proj_in, proj_gain.reshape(1, width), in_hbm(proj_out))


def from_other_half(x):
    return lax.ppermute(x, PLANE, [(0, 3), (1, 2), (2, 1), (3, 0)])


def from_peer(x, axes, k):
    return lax.ppermute(x, axes, [(i, i ^ k) for i in range(4)])


def from_ring(x, axes):
    return [x] + [from_peer(x, axes, k) for k in (1, 2, 3)]


def total_of(arrays):
    return sum(a.astype(F32) for a in arrays)


def place_kernel(place_ref, *refs):
    view, core, ring = place_ref[1], place_ref[2], place_ref[3]
    outs = refs[8:]
    for shift, pieces in enumerate((refs[:4], refs[4:8])):
        for k, piece in enumerate(pieces):
            rows = piece.shape[2]
            start = pl.multiple_of((4 * (core ^ shift) + (ring ^ k)) * rows, rows)
            for n, out in enumerate(outs):
                for v in range(2):
                    out[view ^ v, pl.ds(start, rows)] = piece[n, v].astype(F32)


def summed(grads, place):
    taps, channels = grads[0].shape
    core, ring = lax.axis_index("core"), lax.axis_index("z")
    halves = jnp.stack(grads).reshape(len(grads), 2, 4, taps // 8, channels)
    mine = lax.dynamic_index_in_dim(halves, core, 1, False)
    given = lax.dynamic_index_in_dim(halves, 1 - core, 1, False)
    pieces = (mine + swapped(given)).astype(BF16)
    parts = [lax.dynamic_index_in_dim(pieces, ring, 1, False)]
    parts += [from_peer(lax.dynamic_index_in_dim(pieces, ring ^ k, 1, False), "z", k) for k in (1, 2, 3)]
    parts = from_ring(total_of(parts).astype(BF16), "y")
    parts = from_ring(total_of(parts).astype(BF16), PLANE)
    both = jnp.stack([total_of([parts[0], parts[3]]), total_of([parts[1], parts[2]])], axis=1).astype(BF16)
    mine = from_ring(both, "z")
    given = [swapped(a) for a in mine]
    whole = jax.ShapeDtypeStruct((2, taps, channels), F32)
    return tuple(
        pl.pallas_call(
            place_kernel,
            out_shape=[whole] * len(grads),
            in_specs=[pl.BlockSpec(memory_space=pltpu.SMEM)] + [pl.BlockSpec(memory_space=pltpu.VMEM)] * 8,
            compiler_params=pltpu.CompilerParams(vmem_limit_bytes=16 << 20),
        )(place, *mine, *given)
    )


def per_device(
    rgb_maps, flow_maps, in_weights, out_weights, decay, skip, proj_in, proj_gain, proj_out
):
    half = lax.axis_index("xh")
    view = lax.axis_index("xl") ^ half
    _, frames_here, side, _, channels = rgb_maps.shape
    place = jnp.stack([half, view, lax.axis_index("core"), lax.axis_index("z"), lax.axis_index(("y", "z", "core"))])
    place = place.astype(jnp.int32)
    got = clips_to_devices(rgb_maps, flow_maps, decay, place)
    senders, rows, _ = got.shape
    cell_count = 2 * senders * frames_here * side * side
    plan = Plan(senders, frames_here, side, channels)
    skips = skip.reshape(2, 1, channels)
    here = plan.frames
    inputs, decays, end = plan.call(
        inputs_step,
        False,
        [2, "view"],
        [plan.maps_of(BF16), plan.decays_of(), plan.carry_of()],
        [here, 2, None],
        [*plan.cols(), plan.both(), plan.carry()],
    )(place, got, in_weights)
    income = from_other_half(end)
    states_b, slope, pooled_part = plan.call(
        mixed_step,
        False,
        [here, 2, None, "view", "view"],
        [plan.maps_of(BF16), plan.maps_of(F32), jax.ShapeDtypeStruct((1, channels), F32)],
        [here, here, None],
        [*plan.cols(), plan.both(), plan.carry(), pltpu.VMEM((side, channels), F32)],
        kept=(0, 1),
    )(place, inputs, decays, income, skips, out_weights)

    seen = from_all(from_cores(pooled_part[0]), ("xh", "xl", "y", "z"))
    dpool = projector_back(seen.reshape(4, -1, channels), proj_in, proj_gain, proj_out, place, cell_count)

    dmix_b, source, end = plan.call(
        from_out_step,
        True,
        [here, 2, None, "view"],
        [plan.maps_of(BF16), plan.maps_of(F32), plan.carry_of()],
        [here, here, None],
        [*plan.cols(), plan.both(), plan.carry()],
    )(place, slope, decays, dpool, out_weights)
    income = from_other_half(end)
    (out_grad,) = plan.call(
        out_grad_step,
        False,
        [here, here],
        [plan.grad_of()],
        [None],
        [*plan.cols(), plan.acc()],
    )(place, states_b, dmix_b)
    (in_grad,) = plan.call(
        in_grad_step,
        True,
        [2, here, here, 2, None, None, "view"],
        [plan.grad_of()],
        [None],
        [*plan.cols(), plan.carry(), pltpu.VMEM((here, *plan.map), BF16), plan.acc()],
    )(place, got, slope, source, decays, income, dpool, skips)
    return summed([in_grad, out_grad], place)


def solution(mesh):
    finer = Mesh(mesh.devices.reshape(2, 2, 4, 4, 2), ("xh", "xl", "y", "z", "core"))
    frames = ("xh", "xl", "y")
    return jax.shard_map(
        per_device,
        mesh=finer,
        in_specs=(
            P(("z", "core"), frames, None, None, None),
            P(("z", "core"), frames, None, None, None),
            P(),
            P(),
            P(None, frames, None),
            P(),
            P(),
            P(),
            P(),
        ),
        out_specs=(P(), P()),
        check_vma=False,
    )
```

```python
import functools

import jax
import jax.numpy as jnp
from jax import lax
from jax.experimental import pallas as pl
from jax.experimental.pallas import tpu as pltpu
from jax.sharding import Mesh
from jax.sharding import PartitionSpec as P

TIME = ("xl", "y")
PLANE = ("xh", "xl")


LAMBDA_OFF = 0.0051
EPSILON = 1e-05
HIGHEST = lax.Precision.HIGHEST


BF16, F32 = jnp.bfloat16, jnp.float32
CHUNKS = 4


def pair_weights(weights_ref, both_ref):
    taps, channels = weights_ref.shape[1:]
    third = taps // 3
    both_ref[:taps, :channels] = weights_ref[0]
    both_ref[taps:, :channels] = jnp.zeros((third, channels), BF16)
    both_ref[:third, channels:] = jnp.zeros((third, channels), BF16)
    both_ref[third:, channels:] = weights_ref[0]


def flipped_pair_weights(weights_ref, both_ref):
    taps, channels = weights_ref.shape[1:]
    third = taps // 3
    both_ref[taps:, :channels] = jnp.zeros((third, channels), BF16)
    both_ref[:third, channels:] = jnp.zeros((third, channels), BF16)
    for k in range(taps // channels):
        block = weights_ref[0, taps - (k + 1) * channels : taps - k * channels].astype(F32).T.astype(BF16)
        both_ref[k * channels : (k + 1) * channels, :channels] = block
        both_ref[third + k * channels : third + (k + 1) * channels, channels:] = block


def take_carry(carry_ref, income_ref, has_income):
    @pl.when(has_income)
    def _():
        carry_ref[...] = income_ref[...]

    @pl.when(jnp.logical_not(has_income))
    def _():
        carry_ref[...] = jnp.zeros_like(carry_ref)


def clear_edges(cols_ref):
    frames, _, _, side, lanes = cols_ref.shape
    cols_ref[:, 0, 0] = jnp.zeros((frames, side, lanes), BF16)
    cols_ref[:, side // 2, 1] = jnp.zeros((frames, side, lanes), BF16)


def spread_columns(maps, cols_ref):
    frames, pairs, _, side, channels = maps.shape
    flat = maps.astype(F32).reshape(frames * side * side, channels)
    column = lax.broadcasted_iota(jnp.int32, flat.shape, 0) & (side - 1)
    left = jnp.where(column == 0, 0.0, pltpu.roll(flat, 1, 0))
    right = jnp.where(column == side - 1, 0.0, pltpu.roll(flat, flat.shape[0] - 1, 0))
    for k, shifted in enumerate((left, flat, right)):
        rows = shifted.astype(BF16).reshape(frames, pairs, 2, side, channels)
        lanes = slice(k * channels, (k + 1) * channels)
        cols_ref[:, 0:pairs, 1, :, lanes] = rows[:, :, 0]
        cols_ref[:, 1 : pairs + 1, 0, :, lanes] = rows[:, :, 1]


def pair_patches(cols_ref):
    frames, ends, _, side, lanes = cols_ref.shape
    pairs = ends - 1
    pieces = [cols_ref[:, a : a + pairs, b].reshape(frames * pairs * side, lanes) for a in (0, 1) for b in (0, 1)]
    return jnp.concatenate(pieces, axis=1)


def pair_convolve(cols_ref, weights_ref):
    frames, ends, _, side, lanes = cols_ref.shape
    channels = lanes // 3
    both = jnp.dot(pair_patches(cols_ref), weights_ref[...], preferred_element_type=F32)
    shape = (frames, ends - 1, side, channels)
    return both[:, :channels].reshape(shape), both[:, channels:].reshape(shape)


def add_weight_product(cols, grads, acc_ref):
    frames, pairs, _, side, channels = grads.shape
    rows = frames * pairs * side
    both = [grads[:, :, k].reshape(rows, channels) for k in range(2)]
    acc_ref[...] += lax.dot_general(
        jnp.concatenate(both, axis=1),
        jnp.concatenate([pair_patches(cols_ref) for cols_ref in cols]),
        (((0,), (0,)), ((), ())),
        preferred_element_type=F32,
    )


def folded(acc_ref):
    channels = acc_ref.shape[0] // 2
    width = acc_ref.shape[1] // 4
    total = acc_ref[:channels, : 3 * width] + acc_ref[channels:, width:]
    return total.T


def spread_groups(groups, cols):
    for maps, cols_ref in zip(groups, cols):
        spread_columns(maps, cols_ref)


def halves(ref):
    group = ref.shape[0] // 2
    return [ref[:group], ref[group:]]


def got_maps(got_ref, shape):
    cells = shape[0] * shape[1] * shape[2] * shape[3] // 2
    return [got_ref[h, :cells].reshape(shape[0] // 2, *shape[1:]) for h in range(2)]


def decay_of(decays_ref, t):
    group = decays_ref.shape[1]
    return decays_ref[t // group, t % group : t % group + 1]


def pair_kernel(place_ref, weights_ref, both_ref):
    pair_weights(weights_ref.at[pl.ds(place_ref[1], 1)], both_ref)


def piece_kernel(piece_ref, both_ref, inputs_ref, cols_ref):
    frames, _, _, side, _ = inputs_ref.shape
    clear_edges(cols_ref)
    spread_columns(piece_ref[: frames * side * side].reshape(inputs_ref.shape), cols_ref)
    for k, rows in enumerate(pair_convolve(cols_ref, both_ref)):
        inputs_ref[:, :, k] = rows.astype(BF16)


def order_kernel(place_ref, *refs):
    for k in range(8):
        refs[8][place_ref[5] ^ k] = refs[k][...]


def gather_kernel(place_ref, *refs):
    pieces, convolved, (inputs_ref, decays_ref, end_ref) = refs[:8], refs[8:16], refs[16:]
    group = convolved[0].shape[0]
    cells = pieces[0].shape[0] - 16
    for k in range(8):
        sender = place_ref[5] ^ k
        inputs_ref[pl.ds(sender * group, group)] = convolved[k][...]
        parts = pieces[k][cells:].astype(F32)
        decays_ref[sender] = parts[:group] + parts[group : 2 * group] + parts[2 * group : 3 * group]

    def advance(t, carried):
        for n in range(group):
            carried = decays_ref[t, n : n + 1] * carried + inputs_ref[t * group + n].astype(F32)
        end_ref[...] = carried
        return carried

    lax.fori_loop(0, 8, advance, jnp.zeros(end_ref.shape, F32))


def mixed_step(step, last, place_ref, inputs_ref, decays_ref, income_ref, skip_ref, weights_ref, states_ref, slope_ref, pooled_ref, cols_a, cols_b, both_ref, carry_ref, sum_ref):
    cols = (cols_a, cols_b)
    frames = inputs_ref.shape[0]
    group = frames // 2

    @pl.when(step == 0)
    def _():
        clear_edges(cols_a)
        clear_edges(cols_b)
        pair_weights(weights_ref, both_ref)
        take_carry(carry_ref, income_ref, place_ref[0] == 1)
        sum_ref[...] = jnp.zeros_like(sum_ref)

    carried = carry_ref[...]
    for t in range(frames):
        carried = decay_of(decays_ref, t) * carried + inputs_ref[t].astype(F32)
        states_ref[t] = carried.astype(BF16)
    carry_ref[...] = carried
    spread_groups(halves(states_ref), cols)
    total = sum_ref[...]
    for h in range(2):
        here = slice(h * group, (h + 1) * group)
        for k, rows in enumerate(pair_convolve(cols[h], both_ref)):
            mixed = rows + skip_ref[0] * inputs_ref[here, :, k].astype(F32)
            sigma = jax.nn.sigmoid(mixed)
            slope_ref[here, :, k] = sigma * (1.0 + mixed * (1.0 - sigma))
            total = total + jnp.sum(mixed * sigma, axis=(0, 1))
    sum_ref[...] = total

    @pl.when(step == last)
    def _():
        pooled_ref[...] = jnp.sum(total, axis=0, keepdims=True)


def from_out_step(step, last, place_ref, slope_ref, decays_ref, dpool_ref, weights_ref, dmix_ref, source_ref, end_ref, cols_a, cols_b, both_ref, carry_ref):
    cols = (cols_a, cols_b)
    frames = slope_ref.shape[0]
    group = frames // 2

    @pl.when(step == 0)
    def _():
        clear_edges(cols_a)
        clear_edges(cols_b)
        flipped_pair_weights(weights_ref, both_ref)
        carry_ref[...] = jnp.zeros_like(carry_ref)

    dmix_ref[...] = (dpool_ref[...] * slope_ref[...]).astype(BF16)
    spread_groups(halves(dmix_ref), cols)
    for h in range(2):
        for k, rows in enumerate(pair_convolve(cols[h], both_ref)):
            source_ref[h * group : (h + 1) * group, :, k] = rows
    carried = carry_ref[...]
    for t in reversed(range(frames)):
        carried = decay_of(decays_ref, t) * (source_ref[t] + carried)
    carry_ref[...] = carried

    @pl.when(step == last)
    def _():
        end_ref[...] = carried


def out_grad_step(step, last, place_ref, states_ref, dmix_ref, grad_ref, cols_a, cols_b, acc_ref):

    @pl.when(step == 0)
    def _():
        clear_edges(cols_a)
        clear_edges(cols_b)
        acc_ref[...] = jnp.zeros_like(acc_ref)

    spread_groups(halves(states_ref), (cols_a, cols_b))
    add_weight_product((cols_a, cols_b), dmix_ref[...], acc_ref)

    @pl.when(step == last)
    def _():
        grad_ref[...] = folded(acc_ref)


def in_grad_step(step, last, place_ref, got_ref, slope_ref, source_ref, decays_ref, income_ref, dpool_ref, skip_ref, grad_ref, cols_a, cols_b, carry_ref, dinput_ref, acc_ref):
    frames = slope_ref.shape[0]

    @pl.when(step == 0)
    def _():
        clear_edges(cols_a)
        clear_edges(cols_b)
        take_carry(carry_ref, income_ref, place_ref[0] == 0)
        acc_ref[...] = jnp.zeros_like(acc_ref)

    spread_groups(got_maps(got_ref, slope_ref.shape), (cols_a, cols_b))
    carried = carry_ref[...]
    for t in reversed(range(frames)):
        carried = source_ref[t] + carried
        dmix = dpool_ref[...] * slope_ref[t]
        dinput_ref[t] = (carried + skip_ref[0] * dmix).astype(BF16)
        carried = decay_of(decays_ref, t) * carried
    carry_ref[...] = carried
    add_weight_product((cols_a, cols_b), dinput_ref[...], acc_ref)

    @pl.when(step == last)
    def _():
        grad_ref[...] = folded(acc_ref)


class Plan:
    def __init__(self, senders, group, side, channels):
        self.steps, self.frames, self.group, self.side, self.channels = senders // 2, 2 * group, group, side, channels
        self.map = (side // 2, 2, side, channels)

    def maps_of(self, dtype):
        return jax.ShapeDtypeStruct((self.steps * self.frames, *self.map), dtype)

    def carry_of(self):
        return jax.ShapeDtypeStruct(self.map, F32)

    def decays_of(self):
        return jax.ShapeDtypeStruct((2 * self.steps, self.group, self.channels), F32)

    def grad_of(self):
        return jax.ShapeDtypeStruct((9 * self.channels, self.channels), F32)

    def cols(self):
        return [pltpu.VMEM((self.group, self.side // 2 + 1, 2, self.side, 3 * self.channels), BF16)] * 2

    def carry(self):
        return pltpu.VMEM(self.map, F32)

    def acc(self):
        return pltpu.VMEM((2 * self.channels, 12 * self.channels), F32)

    def both(self):
        return pltpu.VMEM((12 * self.channels, 2 * self.channels), BF16)

    def small(self, kernel, arity, out_shape, scratch=(), placed=True):
        vmem = pl.BlockSpec(memory_space=pltpu.VMEM)
        return pl.pallas_call(
            kernel,
            out_shape=out_shape,
            in_specs=[pl.BlockSpec(memory_space=pltpu.SMEM) if placed else vmem] + [vmem] * (arity - 1),
            scratch_shapes=list(scratch),
            compiler_params=pltpu.CompilerParams(vmem_limit_bytes=16 << 20),
        )

    def call(self, run, back, takes, out_shape, gives, scratch, kept=()):
        cells = self.steps * self.frames * self.side * self.side
        work = 2 * 9 * cells * self.channels * self.channels
        blocks = [*takes, *gives]
        buffers = [pltpu.VMEM(out_shape[n].shape, out_shape[n].dtype) for n in kept]
        sems = [pltpu.SemaphoreType.DMA((len(kept), self.steps))] if kept else []
        first_out = len(takes)

        def kernel(place_ref, *refs):
            arrays, rest = list(refs[: len(blocks)]), refs[len(blocks) :]
            far = {}
            for k, n in enumerate(kept):
                far[k] = arrays[first_out + n]
                arrays[first_out + n] = rest[k]
            rest = rest[len(kept) :]
            if kept:
                sems_ref, rest = rest[-1], rest[:-1]

            def copy_of(k, i):
                rows = pl.ds(i * gives[kept[k]], gives[kept[k]])
                return pltpu.make_async_copy(arrays[first_out + kept[k]].at[rows], far[k].at[rows], sems_ref.at[k, i])

            def step(i, _):
                at = self.steps - 1 - i if back else i
                views = []
                for ref, block in zip(arrays, blocks):
                    if block == "view":
                        views.append(ref.at[pl.ds(place_ref[1], 1)])
                    else:
                        views.append(ref if block is None else ref.at[pl.ds(at * block, block)])
                run(i, self.steps - 1, place_ref, *views, *rest)
                for k in range(len(kept)):
                    copy_of(k, at).start()
                return 0

            if kept:
                lax.fori_loop(0, self.steps, step, 0)
            else:
                for i in range(self.steps):
                    step(i, 0)
            for k in range(len(kept)):
                for i in range(self.steps):
                    copy_of(k, i).wait()

        vmem, hbm = pl.BlockSpec(memory_space=pltpu.VMEM), pl.BlockSpec(memory_space=pltpu.HBM)
        return pl.pallas_call(
            kernel,
            out_shape=[pltpu.HBM(o.shape, o.dtype) if n in kept else o for n, o in enumerate(out_shape)],
            in_specs=[pl.BlockSpec(memory_space=pltpu.SMEM)] + [vmem] * len(takes),
            out_specs=[hbm if n in kept else vmem for n in range(len(out_shape))],
            scratch_shapes=[*buffers, *scratch, *sems],
            cost_estimate=pl.CostEstimate(flops=2 * work, transcendentals=0, bytes_accessed=4 * cells * self.channels),
            compiler_params=pltpu.CompilerParams(vmem_limit_bytes=24 << 20),
        )


def swapped(x):
    return lax.ppermute(x, "core", [(0, 1), (1, 0)])


def from_cores(x):
    here, there = x, swapped(x)
    first = lax.axis_index("core") == 0
    return jnp.stack([jnp.where(first, here, there), jnp.where(first, there, here)])


def from_all(x, axes):
    peers = lax.axis_size(axes)
    return lax.all_to_all(jnp.broadcast_to(x[None], (peers, *x.shape)), axes, 0, 0, tiled=True)


def in_hbm(x):
    return pltpu.with_memory_space_constraint(x, pltpu.HBM)


def pack_kernel(place_ref, rgb_ref, flow_ref, decay_ref, *refs):
    sent, (parts_ref, sems, part_sem) = refs[:8], refs[8:]
    view, clip = place_ref[1], place_ref[6]
    clips, cells, channels = rgb_ref.shape
    frames = decay_ref.shape[1]

    def copy_of(maps_ref, k):
        return pltpu.make_async_copy(maps_ref.at[clip ^ (k % clips)], sent[k].at[:cells], sems.at[k])

    decay_copy = pltpu.make_async_copy(decay_ref, parts_ref, part_sem)
    decay_copy.start()
    for second in range(2):
        for v, maps_ref in enumerate((rgb_ref, flow_ref)):

            @pl.when((view ^ second) == v)
            def _(second=second, maps_ref=maps_ref):
                for k in range(second * clips, (second + 1) * clips):
                    copy_of(maps_ref, k).start()

    decay_copy.wait()
    for second in range(2):
        decays = parts_ref[view ^ second]
        high = decays.astype(BF16).astype(F32)
        middle = (decays - high).astype(BF16).astype(F32)
        low = decays - high - middle
        rows = sent[0].shape[0] - cells
        parts = [high, middle, low, jnp.zeros((rows - 3 * frames, channels), F32)]
        parts = jnp.concatenate(parts).astype(BF16)
        for k in range(second * clips, (second + 1) * clips):
            sent[k][cells:] = parts
    for k in range(2 * clips):
        copy_of(rgb_ref, k).wait()


def clips_to_devices(rgb_maps, flow_maps, decay, place):
    clips, frames, side, _, channels = rgb_maps.shape
    cells = frames * side * side
    hbm = pl.BlockSpec(memory_space=pltpu.HBM)
    sent = pl.pallas_call(
        pack_kernel,
        out_shape=[jax.ShapeDtypeStruct((cells + 16, channels), BF16)] * (2 * clips),
        in_specs=[pl.BlockSpec(memory_space=pltpu.SMEM), hbm, hbm, hbm],
        out_specs=[pl.BlockSpec(memory_space=pltpu.VMEM)] * (2 * clips),
        scratch_shapes=[
            pltpu.VMEM(decay.shape, F32),
            pltpu.SemaphoreType.DMA((2 * clips,)),
            pltpu.SemaphoreType.DMA,
        ],
        compiler_params=pltpu.CompilerParams(vmem_limit_bytes=16 << 20),
    )(place, *(in_hbm(maps.reshape(clips, cells, channels)) for maps in (rgb_maps, flow_maps)), in_hbm(decay))
    peers = 2 * clips
    return [sent[0]] + [lax.ppermute(sent[k], TIME, [(i, i ^ k) for i in range(peers)]) for k in range(1, peers)]


def batch_norm(values):
    centered = values - jnp.mean(values, axis=0, keepdims=True)
    scale = lax.rsqrt(jnp.mean(centered * centered, axis=0, keepdims=True) + EPSILON)
    return centered * scale, scale


def norm_back(grad, normed, scale):
    mean = jnp.mean(grad, axis=0, keepdims=True)
    along = jnp.mean(grad * normed, axis=0, keepdims=True)
    return (grad - mean - normed * along) * scale


def across(a, b, **kinds):
    return lax.dot_general(a, b, (((1,), (1,)), ((), ())), preferred_element_type=F32, **kinds)


def projector_kernel(place_ref, seen_ref, in_ref, gain_ref, far_ref, dpool_ref, x_ref, n_ref, z_ref, zn_ref, out_ref, sems, *, cell_count):
    view, row = place_ref[1], place_ref[4]
    clips = seen_ref.shape[1]
    chunk = out_ref.shape[1] // CHUNKS
    columns = [slice(j * chunk, (j + 1) * chunk) for j in range(CHUNKS)]
    copies = [pltpu.make_async_copy(far_ref.at[:, c], out_ref.at[:, c], sems.at[j]) for j, c in enumerate(columns)]
    for copy in copies:
        copy.start()
    gain = gain_ref[...]
    pooled = jnp.concatenate([seen_ref[0] + seen_ref[3], seen_ref[1] + seen_ref[2]]) / cell_count
    hidden = jnp.dot(pooled, in_ref[...], precision=HIGHEST, preferred_element_type=F32)
    hidden_s, relus = [], []
    for v in range(2):
        x_ref[v], scale = batch_norm(hidden[v * clips : (v + 1) * clips])
        n_ref[v] = x_ref[v] * gain
        hidden_s.append(scale)
        relus.append(jnp.maximum(n_ref[v], 0.0).astype(BF16))
    relu_b = jnp.concatenate(relus)
    scales = []
    for copy, c in zip(copies, columns):
        copy.wait()
        z = jnp.dot(relu_b, out_ref[:, c], preferred_element_type=F32)
        for v in range(2):
            z_ref[v, :, c], scale = batch_norm(z[v * clips : (v + 1) * clips])
            zn_ref[v, :, c] = z_ref[v, :, c].astype(BF16)
            scales.append(scale)
    z_s = [jnp.concatenate(scales[v::2], axis=1) for v in range(2)]
    first = view == 0
    own, other = zn_ref[view].astype(F32), zn_ref[1 - view].astype(F32)
    corr_diag = jnp.sum(own * other, axis=0, keepdims=True) / clips
    extra = -2.0 * (1.0 - corr_diag) - 2.0 * LAMBDA_OFF * corr_diag
    gram = across(zn_ref[1 - view], zn_ref[1 - view])
    spread = jnp.dot(gram, own, precision=HIGHEST, preferred_element_type=F32)
    dzn = spread * (2.0 * LAMBDA_OFF / (clips * clips)) + other * (extra / clips)
    dz_b = norm_back(dzn, z_ref[view], jnp.where(first, z_s[0], z_s[1])).astype(BF16)
    dxh = jnp.where(n_ref[view] > 0, across(dz_b, out_ref[...]), 0.0) * gain
    dhidden = norm_back(dxh, x_ref[view], jnp.where(first, hidden_s[0], hidden_s[1]))
    mine = lax.broadcasted_iota(jnp.int32, dhidden.shape, 0) == row
    own_row = jnp.sum(jnp.where(mine, dhidden, 0.0), axis=0, keepdims=True)
    rows = jnp.broadcast_to(own_row, (8, own_row.shape[1]))
    dpool_ref[...] = across(rows, in_ref[...], precision=HIGHEST)[:1] / cell_count


def projector_back(seen, proj_in, proj_gain, proj_out, place, cell_count):
    _, clips, channels = seen.shape
    width = proj_in.shape[1]
    wide = (2, clips, width)
    return pl.pallas_call(
        functools.partial(projector_kernel, cell_count=cell_count),
        out_shape=jax.ShapeDtypeStruct((1, channels), F32),
        in_specs=[pl.BlockSpec(memory_space=pltpu.SMEM)]
        + [pl.BlockSpec(memory_space=pltpu.VMEM)] * 3
        + [pl.BlockSpec(memory_space=pltpu.HBM)],
        scratch_shapes=[
            pltpu.VMEM(wide, F32),
            pltpu.VMEM(wide, F32),
            pltpu.VMEM(wide, F32),
            pltpu.VMEM(wide, BF16),
            pltpu.VMEM(proj_out.shape, BF16),
            pltpu.SemaphoreType.DMA((CHUNKS,)),
        ],
        cost_estimate=pl.CostEstimate(flops=6 * clips * width * width, transcendentals=0, bytes_accessed=2 * width * width),
        compiler_params=pltpu.CompilerParams(vmem_limit_bytes=26 << 20),
    )(place, seen, proj_in, proj_gain.reshape(1, width), in_hbm(proj_out))


def from_other_half(x):
    return lax.ppermute(x, PLANE, [(0, 3), (1, 2), (2, 1), (3, 0)])


def from_peer(x, axes, k):
    return lax.ppermute(x, axes, [(i, i ^ k) for i in range(4)])


def from_ring(x, axes):
    return [x] + [from_peer(x, axes, k) for k in (1, 2, 3)]


def total_of(arrays):
    return sum(a.astype(F32) for a in arrays)


def place_kernel(place_ref, *refs):
    view, core, ring = place_ref[1], place_ref[2], place_ref[3]
    outs = refs[8:]
    for shift, pieces in enumerate((refs[:4], refs[4:8])):
        for k, piece in enumerate(pieces):
            rows = piece.shape[2]
            start = pl.multiple_of((4 * (core ^ shift) + (ring ^ k)) * rows, rows)
            for n, out in enumerate(outs):
                for v in range(2):
                    out[view ^ v, pl.ds(start, rows)] = piece[n, v].astype(F32)


def summed(grads, place):
    taps, channels = grads[0].shape
    core, ring = lax.axis_index("core"), lax.axis_index("z")
    halves = jnp.stack(grads).reshape(len(grads), 2, 4, taps // 8, channels)
    mine = lax.dynamic_index_in_dim(halves, core, 1, False)
    given = lax.dynamic_index_in_dim(halves, 1 - core, 1, False)
    pieces = (mine + swapped(given)).astype(BF16)
    parts = [lax.dynamic_index_in_dim(pieces, ring, 1, False)]
    parts += [from_peer(lax.dynamic_index_in_dim(pieces, ring ^ k, 1, False), "z", k) for k in (1, 2, 3)]
    parts = from_ring(total_of(parts).astype(BF16), "y")
    parts = from_ring(total_of(parts).astype(BF16), PLANE)
    both = jnp.stack([total_of([parts[0], parts[3]]), total_of([parts[1], parts[2]])], axis=1).astype(BF16)
    mine = from_ring(both, "z")
    given = [swapped(a) for a in mine]
    whole = jax.ShapeDtypeStruct((2, taps, channels), F32)
    return tuple(
        pl.pallas_call(
            place_kernel,
            out_shape=[whole] * len(grads),
            in_specs=[pl.BlockSpec(memory_space=pltpu.SMEM)] + [pl.BlockSpec(memory_space=pltpu.VMEM)] * 8,
            compiler_params=pltpu.CompilerParams(vmem_limit_bytes=16 << 20),
        )(place, *mine, *given)
    )


def per_device(
    rgb_maps, flow_maps, in_weights, out_weights, decay, skip, proj_in, proj_gain, proj_out
):
    half = lax.axis_index("xh")
    view = lax.axis_index("xl") ^ half
    _, frames_here, side, _, channels = rgb_maps.shape
    place = jnp.stack([half, view, lax.axis_index("core"), lax.axis_index("z"), lax.axis_index(("y", "z", "core")), lax.axis_index(TIME), lax.axis_index("y")])
    place = place.astype(jnp.int32)
    pieces = clips_to_devices(rgb_maps, flow_maps, decay, place)
    senders = len(pieces)
    cell_count = 2 * senders * frames_here * side * side
    plan = Plan(senders, frames_here, side, channels)
    skips = skip.reshape(2, 1, channels)
    here = plan.frames
    both = plan.small(pair_kernel, 2, jax.ShapeDtypeStruct((12 * channels, 2 * channels), BF16))(place, in_weights)
    piece_of = jax.ShapeDtypeStruct((frames_here, *plan.map), BF16)
    convolved = [plan.small(piece_kernel, 2, piece_of, plan.cols()[:1], False)(piece, both) for piece in pieces]
    inputs, decays, end = plan.small(gather_kernel, 17, [plan.maps_of(BF16), plan.decays_of(), plan.carry_of()])(
        place, *pieces, *convolved
    )
    got = plan.small(order_kernel, 9, jax.ShapeDtypeStruct((senders, *pieces[0].shape), BF16))(place, *pieces)
    income = from_other_half(end)
    states_b, slope, pooled_part = plan.call(
        mixed_step,
        False,
        [here, 2, None, "view", "view"],
        [plan.maps_of(BF16), plan.maps_of(F32), jax.ShapeDtypeStruct((1, channels), F32)],
        [here, here, None],
        [*plan.cols(), plan.both(), plan.carry(), pltpu.VMEM((side, channels), F32)],
        kept=(0, 1),
    )(place, inputs, decays, income, skips, out_weights)

    seen = from_all(from_cores(pooled_part[0]), ("xh", "xl", "y", "z"))
    dpool = projector_back(seen.reshape(4, -1, channels), proj_in, proj_gain, proj_out, place, cell_count)

    dmix_b, source, end = plan.call(
        from_out_step,
        True,
        [here, 2, None, "view"],
        [plan.maps_of(BF16), plan.maps_of(F32), plan.carry_of()],
        [here, here, None],
        [*plan.cols(), plan.both(), plan.carry()],
    )(place, slope, decays, dpool, out_weights)
    income = from_other_half(end)
    (out_grad,) = plan.call(
        out_grad_step,
        False,
        [here, here],
        [plan.grad_of()],
        [None],
        [*plan.cols(), plan.acc()],
    )(place, states_b, dmix_b)
    (in_grad,) = plan.call(
        in_grad_step,
        True,
        [2, here, here, 2, None, None, "view"],
        [plan.grad_of()],
        [None],
        [*plan.cols(), plan.carry(), pltpu.VMEM((here, *plan.map), BF16), plan.acc()],
    )(place, got, slope, source, decays, income, dpool, skips)
    return summed([in_grad, out_grad], place)


def solution(mesh):
    finer = Mesh(mesh.devices.reshape(2, 2, 4, 4, 2), ("xh", "xl", "y", "z", "core"))
    frames = ("xh", "xl", "y")
    return jax.shard_map(
        per_device,
        mesh=finer,
        in_specs=(
            P(("z", "core"), frames, None, None, None),
            P(("z", "core"), frames, None, None, None),
            P(),
            P(),
            P(None, frames, None),
            P(),
            P(),
            P(),
            P(),
        ),
        out_specs=(P(), P()),
        check_vma=False,
    )
```

```python
import functools

import jax
import jax.numpy as jnp
from jax import lax
from jax.experimental import pallas as pl
from jax.experimental.pallas import tpu as pltpu
from jax.sharding import Mesh
from jax.sharding import PartitionSpec as P

TIME = ("xl", "y")
PLANE = ("xh", "xl")


LAMBDA_OFF = 0.0051
EPSILON = 1e-05
HIGHEST = lax.Precision.HIGHEST


BF16, F32 = jnp.bfloat16, jnp.float32
CHUNKS = 4
PEERS = (0, 6, 1, 3, 2, 4, 5, 7)


def pair_weights(weights_ref, both_ref):
    taps, channels = weights_ref.shape[1:]
    third = taps // 3
    both_ref[:taps, :channels] = weights_ref[0]
    both_ref[taps:, :channels] = jnp.zeros((third, channels), BF16)
    both_ref[:third, channels:] = jnp.zeros((third, channels), BF16)
    both_ref[third:, channels:] = weights_ref[0]


def flipped_pair_weights(weights_ref, both_ref):
    taps, channels = weights_ref.shape[1:]
    third = taps // 3
    both_ref[taps:, :channels] = jnp.zeros((third, channels), BF16)
    both_ref[:third, channels:] = jnp.zeros((third, channels), BF16)
    for k in range(taps // channels):
        block = weights_ref[0, taps - (k + 1) * channels : taps - k * channels].astype(F32).T.astype(BF16)
        both_ref[k * channels : (k + 1) * channels, :channels] = block
        both_ref[third + k * channels : third + (k + 1) * channels, channels:] = block


def take_carry(carry_ref, income_ref, has_income):
    @pl.when(has_income)
    def _():
        carry_ref[...] = income_ref[...]

    @pl.when(jnp.logical_not(has_income))
    def _():
        carry_ref[...] = jnp.zeros_like(carry_ref)


def clear_edges(cols_ref):
    frames, _, _, side, lanes = cols_ref.shape
    cols_ref[:, 0, 0] = jnp.zeros((frames, side, lanes), BF16)
    cols_ref[:, side // 2, 1] = jnp.zeros((frames, side, lanes), BF16)


def spread_columns(maps, cols_ref):
    frames, pairs, _, side, channels = maps.shape
    flat = maps.astype(F32).reshape(frames * side * side, channels)
    column = lax.broadcasted_iota(jnp.int32, flat.shape, 0) & (side - 1)
    left = jnp.where(column == 0, 0.0, pltpu.roll(flat, 1, 0))
    right = jnp.where(column == side - 1, 0.0, pltpu.roll(flat, flat.shape[0] - 1, 0))
    for k, shifted in enumerate((left, flat, right)):
        rows = shifted.astype(BF16).reshape(frames, pairs, 2, side, channels)
        lanes = slice(k * channels, (k + 1) * channels)
        cols_ref[:, 0:pairs, 1, :, lanes] = rows[:, :, 0]
        cols_ref[:, 1 : pairs + 1, 0, :, lanes] = rows[:, :, 1]


def pair_patches(cols_ref):
    frames, ends, _, side, lanes = cols_ref.shape
    pairs = ends - 1
    pieces = [cols_ref[:, a : a + pairs, b].reshape(frames * pairs * side, lanes) for a in (0, 1) for b in (0, 1)]
    return jnp.concatenate(pieces, axis=1)


def pair_convolve(cols_ref, weights_ref):
    frames, ends, _, side, lanes = cols_ref.shape
    channels = lanes // 3
    both = jnp.dot(pair_patches(cols_ref), weights_ref[...], preferred_element_type=F32)
    shape = (frames, ends - 1, side, channels)
    return both[:, :channels].reshape(shape), both[:, channels:].reshape(shape)


def add_weight_product(cols, grads, acc_ref):
    frames, pairs, _, side, channels = grads.shape
    rows = frames * pairs * side
    both = [grads[:, :, k].reshape(rows, channels) for k in range(2)]
    acc_ref[...] += lax.dot_general(
        jnp.concatenate(both, axis=1),
        jnp.concatenate([pair_patches(cols_ref) for cols_ref in cols]),
        (((0,), (0,)), ((), ())),
        preferred_element_type=F32,
    )


def folded(acc_ref):
    channels = acc_ref.shape[0] // 2
    width = acc_ref.shape[1] // 4
    total = acc_ref[:channels, : 3 * width] + acc_ref[channels:, width:]
    return total.T


def spread_groups(groups, cols):
    for maps, cols_ref in zip(groups, cols):
        spread_columns(maps, cols_ref)


def halves(ref):
    group = ref.shape[0] // 2
    return [ref[:group], ref[group:]]


def got_maps(got_ref, shape):
    cells = shape[0] * shape[1] * shape[2] * shape[3] // 2
    return [got_ref[h, :cells].reshape(shape[0] // 2, *shape[1:]) for h in range(2)]


def decay_of(decays_ref, t):
    group = decays_ref.shape[1]
    return decays_ref[t // group, t % group : t % group + 1]


def pair_kernel(place_ref, weights_ref, both_ref):
    pair_weights(weights_ref.at[pl.ds(place_ref[1], 1)], both_ref)


def piece_kernel(piece_ref, both_ref, inputs_ref, cols_ref):
    frames, _, _, side, _ = inputs_ref.shape
    clear_edges(cols_ref)
    spread_columns(piece_ref[: frames * side * side].reshape(inputs_ref.shape), cols_ref)
    for k, rows in enumerate(pair_convolve(cols_ref, both_ref)):
        inputs_ref[:, :, k] = rows.astype(BF16)


def order_kernel(place_ref, *refs):
    for k in range(8):
        refs[8][place_ref[5] ^ PEERS[k]] = refs[k][...]


def gather_kernel(place_ref, *refs):
    pieces, convolved, (inputs_ref, decays_ref, end_ref) = refs[:8], refs[8:16], refs[16:]
    group = convolved[0].shape[0]
    cells = pieces[0].shape[0] - 16
    for k in range(8):
        sender = place_ref[5] ^ PEERS[k]
        inputs_ref[pl.ds(sender * group, group)] = convolved[k][...]
        parts = pieces[k][cells:].astype(F32)
        decays_ref[sender] = parts[:group] + parts[group : 2 * group] + parts[2 * group : 3 * group]

    def advance(t, carried):
        for n in range(group):
            carried = decays_ref[t, n : n + 1] * carried + inputs_ref[t * group + n].astype(F32)
        end_ref[...] = carried
        return carried

    lax.fori_loop(0, 8, advance, jnp.zeros(end_ref.shape, F32))


def mixed_step(first, final, place_ref, inputs_ref, decays_ref, income_ref, skip_ref, weights_ref, states_ref, slope_ref, pooled_ref, cols_a, cols_b, both_ref, carry_ref, sum_ref):
    cols = (cols_a, cols_b)
    frames = inputs_ref.shape[0]
    group = frames // 2

    @pl.when(first)
    def _():
        clear_edges(cols_a)
        clear_edges(cols_b)
        pair_weights(weights_ref, both_ref)
        take_carry(carry_ref, income_ref, place_ref[0] == 1)
        sum_ref[...] = jnp.zeros_like(sum_ref)

    carried = carry_ref[...]
    for t in range(frames):
        carried = decay_of(decays_ref, t) * carried + inputs_ref[t].astype(F32)
        states_ref[t] = carried.astype(BF16)
    carry_ref[...] = carried
    spread_groups(halves(states_ref), cols)
    total = sum_ref[...]
    for h in range(2):
        here = slice(h * group, (h + 1) * group)
        for k, rows in enumerate(pair_convolve(cols[h], both_ref)):
            mixed = rows + skip_ref[0] * inputs_ref[here, :, k].astype(F32)
            sigma = jax.nn.sigmoid(mixed)
            slope_ref[here, :, k] = sigma * (1.0 + mixed * (1.0 - sigma))
            total = total + jnp.sum(mixed * sigma, axis=(0, 1))
    sum_ref[...] = total

    @pl.when(final)
    def _():
        pooled_ref[...] = jnp.sum(total, axis=0, keepdims=True)


def from_out_step(first, final, place_ref, slope_ref, decays_ref, dpool_ref, weights_ref, dmix_ref, source_ref, end_ref, cols_a, cols_b, both_ref, carry_ref):
    cols = (cols_a, cols_b)
    frames = slope_ref.shape[0]
    group = frames // 2

    @pl.when(first)
    def _():
        clear_edges(cols_a)
        clear_edges(cols_b)
        flipped_pair_weights(weights_ref, both_ref)
        carry_ref[...] = jnp.zeros_like(carry_ref)

    dmix_ref[...] = (dpool_ref[...] * slope_ref[...]).astype(BF16)
    spread_groups(halves(dmix_ref), cols)
    for h in range(2):
        for k, rows in enumerate(pair_convolve(cols[h], both_ref)):
            source_ref[h * group : (h + 1) * group, :, k] = rows
    carried = carry_ref[...]
    for t in reversed(range(frames)):
        carried = decay_of(decays_ref, t) * (source_ref[t] + carried)
    carry_ref[...] = carried

    @pl.when(final)
    def _():
        end_ref[...] = carried


def out_grad_step(first, final, place_ref, states_ref, dmix_ref, grad_ref, cols_a, cols_b, acc_ref):

    @pl.when(first)
    def _():
        clear_edges(cols_a)
        clear_edges(cols_b)
        acc_ref[...] = jnp.zeros_like(acc_ref)

    spread_groups(halves(states_ref), (cols_a, cols_b))
    add_weight_product((cols_a, cols_b), dmix_ref[...], acc_ref)

    @pl.when(final)
    def _():
        grad_ref[...] = folded(acc_ref)


def in_grad_step(first, final, place_ref, got_ref, slope_ref, source_ref, decays_ref, income_ref, dpool_ref, skip_ref, grad_ref, cols_a, cols_b, carry_ref, dinput_ref, acc_ref):
    frames = slope_ref.shape[0]

    @pl.when(first)
    def _():
        clear_edges(cols_a)
        clear_edges(cols_b)
        take_carry(carry_ref, income_ref, place_ref[0] == 0)
        acc_ref[...] = jnp.zeros_like(acc_ref)

    spread_groups(got_maps(got_ref, slope_ref.shape), (cols_a, cols_b))
    carried = carry_ref[...]
    for t in reversed(range(frames)):
        carried = source_ref[t] + carried
        dmix = dpool_ref[...] * slope_ref[t]
        dinput_ref[t] = (carried + skip_ref[0] * dmix).astype(BF16)
        carried = decay_of(decays_ref, t) * carried
    carry_ref[...] = carried
    add_weight_product((cols_a, cols_b), dinput_ref[...], acc_ref)

    @pl.when(final)
    def _():
        grad_ref[...] = folded(acc_ref)


class Plan:
    def __init__(self, senders, group, side, channels):
        self.steps, self.frames, self.group, self.side, self.channels = senders // 2, 2 * group, group, side, channels
        self.map = (side // 2, 2, side, channels)

    def maps_of(self, dtype):
        return jax.ShapeDtypeStruct((self.steps * self.frames, *self.map), dtype)

    def carry_of(self):
        return jax.ShapeDtypeStruct(self.map, F32)

    def decays_of(self):
        return jax.ShapeDtypeStruct((2 * self.steps, self.group, self.channels), F32)

    def grad_of(self):
        return jax.ShapeDtypeStruct((9 * self.channels, self.channels), F32)

    def cols(self):
        return [pltpu.VMEM((self.group, self.side // 2 + 1, 2, self.side, 3 * self.channels), BF16)] * 2

    def carry(self):
        return pltpu.VMEM(self.map, F32)

    def acc(self):
        return pltpu.VMEM((2 * self.channels, 12 * self.channels), F32)

    def both(self):
        return pltpu.VMEM((12 * self.channels, 2 * self.channels), BF16)

    def small(self, kernel, arity, out_shape, scratch=(), placed=True):
        vmem = pl.BlockSpec(memory_space=pltpu.VMEM)
        return pl.pallas_call(
            kernel,
            out_shape=out_shape,
            in_specs=[pl.BlockSpec(memory_space=pltpu.SMEM) if placed else vmem] + [vmem] * (arity - 1),
            scratch_shapes=list(scratch),
            compiler_params=pltpu.CompilerParams(vmem_limit_bytes=16 << 20),
        )

    def call(self, run, back, takes, out_shape, gives, scratch, kept=()):
        cells = self.steps * self.frames * self.side * self.side
        work = 2 * 9 * cells * self.channels * self.channels
        blocks = [*takes, *gives]
        buffers = [pltpu.VMEM(out_shape[n].shape, out_shape[n].dtype) for n in kept]
        sems = [pltpu.SemaphoreType.DMA((len(kept), self.steps))] if kept else []
        first_out = len(takes)

        def kernel(place_ref, *refs):
            arrays, rest = list(refs[: len(blocks)]), refs[len(blocks) :]
            far = {}
            for k, n in enumerate(kept):
                far[k] = arrays[first_out + n]
                arrays[first_out + n] = rest[k]
            rest = rest[len(kept) :]
            if kept:
                sems_ref, rest = rest[-1], rest[:-1]

            def copy_of(k, i):
                rows = pl.ds(i * gives[kept[k]], gives[kept[k]])
                return pltpu.make_async_copy(arrays[first_out + kept[k]].at[rows], far[k].at[rows], sems_ref.at[k, i])

            def step(i, first, final):
                at = self.steps - 1 - i if back else i
                views = []
                for ref, block in zip(arrays, blocks):
                    if block == "view":
                        views.append(ref.at[pl.ds(place_ref[1], 1)])
                    else:
                        views.append(ref if block is None else ref.at[pl.ds(at * block, block)])
                run(first, final, place_ref, *views, *rest)
                for k in range(len(kept)):
                    copy_of(k, at).start()

            def two_steps(i, _):
                step(2 * i, i == 0, False)
                step(2 * i + 1, False, i == self.steps // 2 - 1)
                return 0

            if kept:
                lax.fori_loop(0, self.steps // 2, two_steps, 0)
            else:
                for i in range(self.steps):
                    step(i, i == 0, i == self.steps - 1)
            for k in range(len(kept)):
                for i in range(self.steps):
                    copy_of(k, i).wait()

        vmem, hbm = pl.BlockSpec(memory_space=pltpu.VMEM), pl.BlockSpec(memory_space=pltpu.HBM)
        return pl.pallas_call(
            kernel,
            out_shape=[pltpu.HBM(o.shape, o.dtype) if n in kept else o for n, o in enumerate(out_shape)],
            in_specs=[pl.BlockSpec(memory_space=pltpu.SMEM)] + [vmem] * len(takes),
            out_specs=[hbm if n in kept else vmem for n in range(len(out_shape))],
            scratch_shapes=[*buffers, *scratch, *sems],
            cost_estimate=pl.CostEstimate(flops=2 * work, transcendentals=0, bytes_accessed=4 * cells * self.channels),
            compiler_params=pltpu.CompilerParams(vmem_limit_bytes=24 << 20),
        )


def swapped(x):
    return lax.ppermute(x, "core", [(0, 1), (1, 0)])


def from_cores(x):
    here, there = x, swapped(x)
    first = lax.axis_index("core") == 0
    return jnp.stack([jnp.where(first, here, there), jnp.where(first, there, here)])


def from_all(x, axes):
    peers = lax.axis_size(axes)
    return lax.all_to_all(jnp.broadcast_to(x[None], (peers, *x.shape)), axes, 0, 0, tiled=True)


def in_hbm(x):
    return pltpu.with_memory_space_constraint(x, pltpu.HBM)


def pack_kernel(place_ref, rgb_ref, flow_ref, decay_ref, *refs):
    sent, (parts_ref, sems, part_sem) = refs[:8], refs[8:]
    view, clip = place_ref[1], place_ref[6]
    clips, cells, channels = rgb_ref.shape
    frames = decay_ref.shape[1]

    def copy_of(maps_ref, k):
        return pltpu.make_async_copy(maps_ref.at[clip ^ (PEERS[k] % clips)], sent[k].at[:cells], sems.at[k])

    decay_copy = pltpu.make_async_copy(decay_ref, parts_ref, part_sem)
    decay_copy.start()
    for second in range(2):
        for v, maps_ref in enumerate((rgb_ref, flow_ref)):

            @pl.when((view ^ second) == v)
            def _(second=second, maps_ref=maps_ref):
                for k in range(2 * clips):
                    if PEERS[k] // clips == second:
                        copy_of(maps_ref, k).start()

    decay_copy.wait()
    for second in range(2):
        decays = parts_ref[view ^ second]
        high = decays.astype(BF16).astype(F32)
        middle = (decays - high).astype(BF16).astype(F32)
        low = decays - high - middle
        rows = sent[0].shape[0] - cells
        parts = [high, middle, low, jnp.zeros((rows - 3 * frames, channels), F32)]
        parts = jnp.concatenate(parts).astype(BF16)
        for k in range(2 * clips):
            if PEERS[k] // clips == second:
                sent[k][cells:] = parts
    for k in range(2 * clips):
        copy_of(rgb_ref, k).wait()


def clips_to_devices(rgb_maps, flow_maps, decay, place):
    clips, frames, side, _, channels = rgb_maps.shape
    cells = frames * side * side
    hbm = pl.BlockSpec(memory_space=pltpu.HBM)
    sent = pl.pallas_call(
        pack_kernel,
        out_shape=[jax.ShapeDtypeStruct((cells + 16, channels), BF16)] * (2 * clips),
        in_specs=[pl.BlockSpec(memory_space=pltpu.SMEM), hbm, hbm, hbm],
        out_specs=[pl.BlockSpec(memory_space=pltpu.VMEM)] * (2 * clips),
        scratch_shapes=[
            pltpu.VMEM(decay.shape, F32),
            pltpu.SemaphoreType.DMA((2 * clips,)),
            pltpu.SemaphoreType.DMA,
        ],
        compiler_params=pltpu.CompilerParams(vmem_limit_bytes=16 << 20),
    )(place, *(in_hbm(maps.reshape(clips, cells, channels)) for maps in (rgb_maps, flow_maps)), in_hbm(decay))
    peers = 2 * clips
    return [sent[0]] + [lax.ppermute(sent[k], TIME, [(i, i ^ PEERS[k]) for i in range(peers)]) for k in range(1, peers)]


def batch_norm(values):
    centered = values - jnp.mean(values, axis=0, keepdims=True)
    scale = lax.rsqrt(jnp.mean(centered * centered, axis=0, keepdims=True) + EPSILON)
    return centered * scale, scale


def norm_back(grad, normed, scale):
    mean = jnp.mean(grad, axis=0, keepdims=True)
    along = jnp.mean(grad * normed, axis=0, keepdims=True)
    return (grad - mean - normed * along) * scale


def across(a, b, **kinds):
    return lax.dot_general(a, b, (((1,), (1,)), ((), ())), preferred_element_type=F32, **kinds)


def projector_kernel(place_ref, seen_ref, in_ref, gain_ref, far_ref, dpool_ref, x_ref, n_ref, z_ref, zn_ref, out_ref, sems, *, cell_count):
    view, row = place_ref[1], place_ref[4]
    clips = seen_ref.shape[1]
    chunk = out_ref.shape[1] // CHUNKS
    columns = [slice(j * chunk, (j + 1) * chunk) for j in range(CHUNKS)]
    copies = [pltpu.make_async_copy(far_ref.at[:, c], out_ref.at[:, c], sems.at[j]) for j, c in enumerate(columns)]
    for copy in copies:
        copy.start()
    gain = gain_ref[...]
    pooled = jnp.concatenate([seen_ref[0] + seen_ref[3], seen_ref[1] + seen_ref[2]]) / cell_count
    hidden = jnp.dot(pooled, in_ref[...], precision=HIGHEST, preferred_element_type=F32)
    hidden_s, relus = [], []
    for v in range(2):
        x_ref[v], scale = batch_norm(hidden[v * clips : (v + 1) * clips])
        n_ref[v] = x_ref[v] * gain
        hidden_s.append(scale)
        relus.append(jnp.maximum(n_ref[v], 0.0).astype(BF16))
    relu_b = jnp.concatenate(relus)
    scales = []
    for copy, c in zip(copies, columns):
        copy.wait()
        z = jnp.dot(relu_b, out_ref[:, c], preferred_element_type=F32)
        for v in range(2):
            z_ref[v, :, c], scale = batch_norm(z[v * clips : (v + 1) * clips])
            zn_ref[v, :, c] = z_ref[v, :, c].astype(BF16)
            scales.append(scale)
    z_s = [jnp.concatenate(scales[v::2], axis=1) for v in range(2)]
    first = view == 0
    own, other = zn_ref[view].astype(F32), zn_ref[1 - view].astype(F32)
    corr_diag = jnp.sum(own * other, axis=0, keepdims=True) / clips
    extra = -2.0 * (1.0 - corr_diag) - 2.0 * LAMBDA_OFF * corr_diag
    gram = across(zn_ref[1 - view], zn_ref[1 - view])
    spread = jnp.dot(gram, own, precision=HIGHEST, preferred_element_type=F32)
    dzn = spread * (2.0 * LAMBDA_OFF / (clips * clips)) + other * (extra / clips)
    dz_b = norm_back(dzn, z_ref[view], jnp.where(first, z_s[0], z_s[1])).astype(BF16)
    dxh = jnp.where(n_ref[view] > 0, across(dz_b, out_ref[...]), 0.0) * gain
    dhidden = norm_back(dxh, x_ref[view], jnp.where(first, hidden_s[0], hidden_s[1]))
    mine = lax.broadcasted_iota(jnp.int32, dhidden.shape, 0) == row
    own_row = jnp.sum(jnp.where(mine, dhidden, 0.0), axis=0, keepdims=True)
    rows = jnp.broadcast_to(own_row, (8, own_row.shape[1]))
    dpool_ref[...] = across(rows, in_ref[...], precision=HIGHEST)[:1] / cell_count


def projector_back(seen, proj_in, proj_gain, proj_out, place, cell_count):
    _, clips, channels = seen.shape
    width = proj_in.shape[1]
    wide = (2, clips, width)
    return pl.pallas_call(
        functools.partial(projector_kernel, cell_count=cell_count),
        out_shape=jax.ShapeDtypeStruct((1, channels), F32),
        in_specs=[pl.BlockSpec(memory_space=pltpu.SMEM)]
        + [pl.BlockSpec(memory_space=pltpu.VMEM)] * 3
        + [pl.BlockSpec(memory_space=pltpu.HBM)],
        scratch_shapes=[
            pltpu.VMEM(wide, F32),
            pltpu.VMEM(wide, F32),
            pltpu.VMEM(wide, F32),
            pltpu.VMEM(wide, BF16),
            pltpu.VMEM(proj_out.shape, BF16),
            pltpu.SemaphoreType.DMA((CHUNKS,)),
        ],
        cost_estimate=pl.CostEstimate(flops=6 * clips * width * width, transcendentals=0, bytes_accessed=2 * width * width),
        compiler_params=pltpu.CompilerParams(vmem_limit_bytes=26 << 20),
    )(place, seen, proj_in, proj_gain.reshape(1, width), in_hbm(proj_out))


def from_other_half(x):
    return lax.ppermute(x, PLANE, [(0, 3), (1, 2), (2, 1), (3, 0)])


def from_peer(x, axes, k):
    return lax.ppermute(x, axes, [(i, i ^ k) for i in range(4)])


def from_ring(x, axes):
    return [x] + [from_peer(x, axes, k) for k in (1, 2, 3)]


def total_of(arrays):
    return sum(a.astype(F32) for a in arrays)


def place_kernel(place_ref, *refs):
    view, core, ring = place_ref[1], place_ref[2], place_ref[3]
    outs = refs[8:]
    for shift, pieces in enumerate((refs[:4], refs[4:8])):
        for k, piece in enumerate(pieces):
            rows = piece.shape[2]
            start = pl.multiple_of((4 * (core ^ shift) + (ring ^ k)) * rows, rows)
            for n, out in enumerate(outs):
                for v in range(2):
                    out[view ^ v, pl.ds(start, rows)] = piece[n, v].astype(F32)


def summed(grads, place):
    taps, channels = grads[0].shape
    core, ring = lax.axis_index("core"), lax.axis_index("z")
    halves = jnp.stack(grads).reshape(len(grads), 2, 4, taps // 8, channels)
    mine = lax.dynamic_index_in_dim(halves, core, 1, False)
    given = lax.dynamic_index_in_dim(halves, 1 - core, 1, False)
    pieces = (mine + swapped(given)).astype(BF16)
    parts = [lax.dynamic_index_in_dim(pieces, ring, 1, False)]
    parts += [from_peer(lax.dynamic_index_in_dim(pieces, ring ^ k, 1, False), "z", k) for k in (1, 2, 3)]
    parts = from_ring(total_of(parts).astype(BF16), "y")
    parts = from_ring(total_of(parts).astype(BF16), PLANE)
    both = jnp.stack([total_of([parts[0], parts[3]]), total_of([parts[1], parts[2]])], axis=1).astype(BF16)
    mine = from_ring(both, "z")
    given = [swapped(a) for a in mine]
    whole = jax.ShapeDtypeStruct((2, taps, channels), F32)
    return tuple(
        pl.pallas_call(
            place_kernel,
            out_shape=[whole] * len(grads),
            in_specs=[pl.BlockSpec(memory_space=pltpu.SMEM)] + [pl.BlockSpec(memory_space=pltpu.VMEM)] * 8,
            compiler_params=pltpu.CompilerParams(vmem_limit_bytes=16 << 20),
        )(place, *mine, *given)
    )


def per_device(
    rgb_maps, flow_maps, in_weights, out_weights, decay, skip, proj_in, proj_gain, proj_out
):
    half = lax.axis_index("xh")
    view = lax.axis_index("xl") ^ half
    _, frames_here, side, _, channels = rgb_maps.shape
    place = jnp.stack([half, view, lax.axis_index("core"), lax.axis_index("z"), lax.axis_index(("y", "z", "core")), lax.axis_index(TIME), lax.axis_index("y")])
    place = place.astype(jnp.int32)
    pieces = clips_to_devices(rgb_maps, flow_maps, decay, place)
    senders = len(pieces)
    cell_count = 2 * senders * frames_here * side * side
    plan = Plan(senders, frames_here, side, channels)
    skips = skip.reshape(2, 1, channels)
    here = plan.frames
    both = plan.small(pair_kernel, 2, jax.ShapeDtypeStruct((12 * channels, 2 * channels), BF16))(place, in_weights)
    piece_of = jax.ShapeDtypeStruct((frames_here, *plan.map), BF16)
    convolved = [plan.small(piece_kernel, 2, piece_of, plan.cols()[:1], False)(piece, both) for piece in pieces]
    inputs, decays, end = plan.small(gather_kernel, 17, [plan.maps_of(BF16), plan.decays_of(), plan.carry_of()])(
        place, *pieces, *convolved
    )
    got = plan.small(order_kernel, 9, jax.ShapeDtypeStruct((senders, *pieces[0].shape), BF16))(place, *pieces)
    income = from_other_half(end)
    states_b, slope, pooled_part = plan.call(
        mixed_step,
        False,
        [here, 2, None, "view", "view"],
        [plan.maps_of(BF16), plan.maps_of(F32), jax.ShapeDtypeStruct((1, channels), F32)],
        [here, here, None],
        [*plan.cols(), plan.both(), plan.carry(), pltpu.VMEM((side, channels), F32)],
        kept=(0, 1),
    )(place, inputs, decays, income, skips, out_weights)

    seen = from_all(from_cores(pooled_part[0]), ("xh", "xl", "y", "z"))
    dpool = projector_back(seen.reshape(4, -1, channels), proj_in, proj_gain, proj_out, place, cell_count)

    dmix_b, source, end = plan.call(
        from_out_step,
        True,
        [here, 2, None, "view"],
        [plan.maps_of(BF16), plan.maps_of(F32), plan.carry_of()],
        [here, here, None],
        [*plan.cols(), plan.both(), plan.carry()],
    )(place, slope, decays, dpool, out_weights)
    income = from_other_half(end)
    (out_grad,) = plan.call(
        out_grad_step,
        False,
        [here, here],
        [plan.grad_of()],
        [None],
        [*plan.cols(), plan.acc()],
    )(place, states_b, dmix_b)
    (in_grad,) = plan.call(
        in_grad_step,
        True,
        [2, here, here, 2, None, None, "view"],
        [plan.grad_of()],
        [None],
        [*plan.cols(), plan.carry(), pltpu.VMEM((here, *plan.map), BF16), plan.acc()],
    )(place, got, slope, source, decays, income, dpool, skips)
    return summed([in_grad, out_grad], place)


def solution(mesh):
    finer = Mesh(mesh.devices.reshape(2, 2, 4, 4, 2), ("xh", "xl", "y", "z", "core"))
    frames = ("xh", "xl", "y")
    return jax.shard_map(
        per_device,
        mesh=finer,
        in_specs=(
            P(("z", "core"), frames, None, None, None),
            P(("z", "core"), frames, None, None, None),
            P(),
            P(),
            P(None, frames, None),
            P(),
            P(),
            P(),
            P(),
        ),
        out_specs=(P(), P()),
        check_vma=False,
    )
```

```python
import functools

import jax
import jax.numpy as jnp
from jax import lax
from jax.experimental import pallas as pl
from jax.experimental.pallas import tpu as pltpu
from jax.sharding import Mesh
from jax.sharding import PartitionSpec as P

TIME = ("xl", "y")
PLANE = ("xh", "xl")


LAMBDA_OFF = 0.0051
EPSILON = 1e-05
HIGHEST = lax.Precision.HIGHEST


BF16, F32 = jnp.bfloat16, jnp.float32
CHUNKS = 4
PEERS = (0, 6, 1, 3, 2, 4, 5, 7)


def pair_weights(weights_ref, both_ref):
    taps, channels = weights_ref.shape[1:]
    third = taps // 3
    both_ref[:taps, :channels] = weights_ref[0]
    both_ref[taps:, :channels] = jnp.zeros((third, channels), BF16)
    both_ref[:third, channels:] = jnp.zeros((third, channels), BF16)
    both_ref[third:, channels:] = weights_ref[0]


def flipped_pair_weights(weights_ref, both_ref):
    taps, channels = weights_ref.shape[1:]
    third = taps // 3
    both_ref[taps:, :channels] = jnp.zeros((third, channels), BF16)
    both_ref[:third, channels:] = jnp.zeros((third, channels), BF16)
    for k in range(taps // channels):
        block = weights_ref[0, taps - (k + 1) * channels : taps - k * channels].astype(F32).T.astype(BF16)
        both_ref[k * channels : (k + 1) * channels, :channels] = block
        both_ref[third + k * channels : third + (k + 1) * channels, channels:] = block


def take_carry(carry_ref, income_ref, has_income):
    @pl.when(has_income)
    def _():
        carry_ref[...] = income_ref[...]

    @pl.when(jnp.logical_not(has_income))
    def _():
        carry_ref[...] = jnp.zeros_like(carry_ref)


def clear_edges(cols_ref):
    frames, _, _, side, lanes = cols_ref.shape
    cols_ref[:, 0, 0] = jnp.zeros((frames, side, lanes), BF16)
    cols_ref[:, side // 2, 1] = jnp.zeros((frames, side, lanes), BF16)


def spread_columns(maps, cols_ref):
    frames, pairs, _, side, channels = maps.shape
    flat = maps.astype(F32).reshape(frames * side * side, channels)
    column = lax.broadcasted_iota(jnp.int32, flat.shape, 0) & (side - 1)
    left = jnp.where(column == 0, 0.0, pltpu.roll(flat, 1, 0))
    right = jnp.where(column == side - 1, 0.0, pltpu.roll(flat, flat.shape[0] - 1, 0))
    for k, shifted in enumerate((left, flat, right)):
        rows = shifted.astype(BF16).reshape(frames, pairs, 2, side, channels)
        lanes = slice(k * channels, (k + 1) * channels)
        cols_ref[:, 0:pairs, 1, :, lanes] = rows[:, :, 0]
        cols_ref[:, 1 : pairs + 1, 0, :, lanes] = rows[:, :, 1]


def pair_patches(cols_ref):
    frames, ends, _, side, lanes = cols_ref.shape
    pairs = ends - 1
    pieces = [cols_ref[:, a : a + pairs, b].reshape(frames * pairs * side, lanes) for a in (0, 1) for b in (0, 1)]
    return jnp.concatenate(pieces, axis=1)


def pair_convolve(cols_ref, weights_ref):
    frames, ends, _, side, lanes = cols_ref.shape
    channels = lanes // 3
    both = jnp.dot(pair_patches(cols_ref), weights_ref[...], preferred_element_type=F32)
    shape = (frames, ends - 1, side, channels)
    return both[:, :channels].reshape(shape), both[:, channels:].reshape(shape)


def add_weight_product(cols, grads, acc_ref):
    frames, pairs, _, side, channels = grads.shape
    rows = frames * pairs * side
    both = [grads[:, :, k].reshape(rows, channels) for k in range(2)]
    acc_ref[...] += lax.dot_general(
        jnp.concatenate(both, axis=1),
        jnp.concatenate([pair_patches(cols_ref) for cols_ref in cols]),
        (((0,), (0,)), ((), ())),
        preferred_element_type=F32,
    )


def folded(acc_ref):
    channels = acc_ref.shape[0] // 2
    width = acc_ref.shape[1] // 4
    total = acc_ref[:channels, : 3 * width] + acc_ref[channels:, width:]
    return total.T


def spread_groups(groups, cols):
    for maps, cols_ref in zip(groups, cols):
        spread_columns(maps, cols_ref)


def halves(ref):
    group = ref.shape[0] // 2
    return [ref[:group], ref[group:]]


def got_maps(got_ref, shape):
    cells = shape[0] * shape[1] * shape[2] * shape[3] // 2
    return [got_ref[h, :cells].reshape(shape[0] // 2, *shape[1:]) for h in range(2)]


def decay_of(decays_ref, t):
    group = decays_ref.shape[1]
    return decays_ref[t // group, t % group : t % group + 1]


def pair_kernel(place_ref, weights_ref, both_ref):
    pair_weights(weights_ref.at[pl.ds(place_ref[1], 1)], both_ref)


def piece_kernel(piece_ref, both_ref, inputs_ref, cols_ref):
    frames, _, _, side, _ = inputs_ref.shape
    clear_edges(cols_ref)
    spread_columns(piece_ref[: frames * side * side].reshape(inputs_ref.shape), cols_ref)
    for k, rows in enumerate(pair_convolve(cols_ref, both_ref)):
        inputs_ref[:, :, k] = rows.astype(BF16)


def order_kernel(place_ref, *refs):
    for k in range(8):
        refs[8][place_ref[5] ^ PEERS[k]] = refs[k][...]


def gather_kernel(place_ref, *refs):
    pieces, convolved, (inputs_ref, decays_ref, end_ref) = refs[:8], refs[8:16], refs[16:]
    group = convolved[0].shape[0]
    cells = pieces[0].shape[0] - 16
    for k in range(8):
        sender = place_ref[5] ^ PEERS[k]
        inputs_ref[pl.ds(sender * group, group)] = convolved[k][...]
        parts = pieces[k][cells:].astype(F32)
        decays_ref[sender] = parts[:group] + parts[group : 2 * group] + parts[2 * group : 3 * group]

    def advance(t, carried):
        for n in range(group):
            carried = decays_ref[t, n : n + 1] * carried + inputs_ref[t * group + n].astype(F32)
        end_ref[...] = carried
        return carried

    lax.fori_loop(0, 8, advance, jnp.zeros(end_ref.shape, F32))


def mixed_step(first, final, place_ref, inputs_ref, decays_ref, income_ref, skip_ref, weights_ref, states_ref, slope_ref, pooled_ref, cols_a, cols_b, both_ref, carry_ref, sum_ref):
    cols = (cols_a, cols_b)
    frames = inputs_ref.shape[0]
    group = frames // 2

    @pl.when(first)
    def _():
        clear_edges(cols_a)
        clear_edges(cols_b)
        pair_weights(weights_ref, both_ref)
        take_carry(carry_ref, income_ref, place_ref[0] == 1)
        sum_ref[...] = jnp.zeros_like(sum_ref)

    carried = carry_ref[...]
    for t in range(frames):
        carried = decay_of(decays_ref, t) * carried + inputs_ref[t].astype(F32)
        states_ref[t] = carried.astype(BF16)
    carry_ref[...] = carried
    spread_groups(halves(states_ref), cols)
    total = sum_ref[...]
    for h in range(2):
        here = slice(h * group, (h + 1) * group)
        for k, rows in enumerate(pair_convolve(cols[h], both_ref)):
            mixed = rows + skip_ref[0] * inputs_ref[here, :, k].astype(F32)
            sigma = jax.nn.sigmoid(mixed)
            silu = mixed * sigma
            slope_ref[here, :, k] = sigma + silu * (1.0 - sigma)
            total = total + jnp.sum(silu, axis=(0, 1))
    sum_ref[...] = total

    @pl.when(final)
    def _():
        pooled_ref[...] = jnp.sum(total, axis=0, keepdims=True)


def from_out_step(first, final, place_ref, slope_ref, decays_ref, dpool_ref, weights_ref, dmix_ref, source_ref, end_ref, cols_a, cols_b, both_ref, carry_ref):
    cols = (cols_a, cols_b)
    frames = slope_ref.shape[0]
    group = frames // 2

    @pl.when(first)
    def _():
        clear_edges(cols_a)
        clear_edges(cols_b)
        flipped_pair_weights(weights_ref, both_ref)
        carry_ref[...] = jnp.zeros_like(carry_ref)

    dmix_ref[...] = (dpool_ref[...] * slope_ref[...]).astype(BF16)
    spread_groups(halves(dmix_ref), cols)
    for h in range(2):
        for k, rows in enumerate(pair_convolve(cols[h], both_ref)):
            source_ref[h * group : (h + 1) * group, :, k] = rows
    carried = carry_ref[...]
    for t in reversed(range(frames)):
        carried = decay_of(decays_ref, t) * (source_ref[t] + carried)
    carry_ref[...] = carried

    @pl.when(final)
    def _():
        end_ref[...] = carried


def out_grad_step(first, final, place_ref, states_ref, dmix_ref, grad_ref, cols_a, cols_b, acc_ref):

    @pl.when(first)
    def _():
        clear_edges(cols_a)
        clear_edges(cols_b)
        acc_ref[...] = jnp.zeros_like(acc_ref)

    spread_groups(halves(states_ref), (cols_a, cols_b))
    add_weight_product((cols_a, cols_b), dmix_ref[...], acc_ref)

    @pl.when(final)
    def _():
        grad_ref[...] = folded(acc_ref)


def in_grad_step(first, final, place_ref, got_ref, slope_ref, source_ref, decays_ref, income_ref, dpool_ref, skip_ref, grad_ref, cols_a, cols_b, carry_ref, dinput_ref, acc_ref):
    frames = slope_ref.shape[0]

    @pl.when(first)
    def _():
        clear_edges(cols_a)
        clear_edges(cols_b)
        take_carry(carry_ref, income_ref, place_ref[0] == 0)
        acc_ref[...] = jnp.zeros_like(acc_ref)

    spread_groups(got_maps(got_ref, slope_ref.shape), (cols_a, cols_b))
    carried = carry_ref[...]
    for t in reversed(range(frames)):
        carried = source_ref[t] + carried
        dmix = dpool_ref[...] * slope_ref[t]
        dinput_ref[t] = (carried + skip_ref[0] * dmix).astype(BF16)
        carried = decay_of(decays_ref, t) * carried
    carry_ref[...] = carried
    add_weight_product((cols_a, cols_b), dinput_ref[...], acc_ref)

    @pl.when(final)
    def _():
        grad_ref[...] = folded(acc_ref)


class Plan:
    def __init__(self, senders, group, side, channels):
        self.steps, self.frames, self.group, self.side, self.channels = senders // 2, 2 * group, group, side, channels
        self.map = (side // 2, 2, side, channels)

    def maps_of(self, dtype):
        return jax.ShapeDtypeStruct((self.steps * self.frames, *self.map), dtype)

    def carry_of(self):
        return jax.ShapeDtypeStruct(self.map, F32)

    def decays_of(self):
        return jax.ShapeDtypeStruct((2 * self.steps, self.group, self.channels), F32)

    def grad_of(self):
        return jax.ShapeDtypeStruct((9 * self.channels, self.channels), F32)

    def cols(self):
        return [pltpu.VMEM((self.group, self.side // 2 + 1, 2, self.side, 3 * self.channels), BF16)] * 2

    def carry(self):
        return pltpu.VMEM(self.map, F32)

    def acc(self):
        return pltpu.VMEM((2 * self.channels, 12 * self.channels), F32)

    def both(self):
        return pltpu.VMEM((12 * self.channels, 2 * self.channels), BF16)

    def small(self, kernel, arity, out_shape, scratch=(), placed=True):
        vmem = pl.BlockSpec(memory_space=pltpu.VMEM)
        return pl.pallas_call(
            kernel,
            out_shape=out_shape,
            in_specs=[pl.BlockSpec(memory_space=pltpu.SMEM) if placed else vmem] + [vmem] * (arity - 1),
            scratch_shapes=list(scratch),
            compiler_params=pltpu.CompilerParams(vmem_limit_bytes=16 << 20),
        )

    def call(self, run, back, takes, out_shape, gives, scratch, kept=()):
        cells = self.steps * self.frames * self.side * self.side
        work = 2 * 9 * cells * self.channels * self.channels
        blocks = [*takes, *gives]
        buffers = [pltpu.VMEM(out_shape[n].shape, out_shape[n].dtype) for n in kept]
        sems = [pltpu.SemaphoreType.DMA((len(kept), self.steps))] if kept else []
        first_out = len(takes)

        def kernel(place_ref, *refs):
            arrays, rest = list(refs[: len(blocks)]), refs[len(blocks) :]
            far = {}
            for k, n in enumerate(kept):
                far[k] = arrays[first_out + n]
                arrays[first_out + n] = rest[k]
            rest = rest[len(kept) :]
            if kept:
                sems_ref, rest = rest[-1], rest[:-1]

            def copy_of(k, i):
                rows = pl.ds(i * gives[kept[k]], gives[kept[k]])
                return pltpu.make_async_copy(arrays[first_out + kept[k]].at[rows], far[k].at[rows], sems_ref.at[k, i])

            def step(i, first, final):
                at = self.steps - 1 - i if back else i
                views = []
                for ref, block in zip(arrays, blocks):
                    if block == "view":
                        views.append(ref.at[pl.ds(place_ref[1], 1)])
                    else:
                        views.append(ref if block is None else ref.at[pl.ds(at * block, block)])
                run(first, final, place_ref, *views, *rest)
                for k in range(len(kept)):
                    copy_of(k, at).start()

            def two_steps(i, _):
                step(2 * i, i == 0, False)
                step(2 * i + 1, False, i == self.steps // 2 - 1)
                return 0

            if kept:
                lax.fori_loop(0, self.steps // 2, two_steps, 0)
            else:
                for i in range(self.steps):
                    step(i, i == 0, i == self.steps - 1)
            for k in range(len(kept)):
                for i in range(self.steps):
                    copy_of(k, i).wait()

        vmem, hbm = pl.BlockSpec(memory_space=pltpu.VMEM), pl.BlockSpec(memory_space=pltpu.HBM)
        return pl.pallas_call(
            kernel,
            out_shape=[pltpu.HBM(o.shape, o.dtype) if n in kept else o for n, o in enumerate(out_shape)],
            in_specs=[pl.BlockSpec(memory_space=pltpu.SMEM)] + [vmem] * len(takes),
            out_specs=[hbm if n in kept else vmem for n in range(len(out_shape))],
            scratch_shapes=[*buffers, *scratch, *sems],
            cost_estimate=pl.CostEstimate(flops=2 * work, transcendentals=0, bytes_accessed=4 * cells * self.channels),
            compiler_params=pltpu.CompilerParams(vmem_limit_bytes=24 << 20),
        )


def swapped(x):
    return lax.ppermute(x, "core", [(0, 1), (1, 0)])


def from_cores(x):
    here, there = x, swapped(x)
    first = lax.axis_index("core") == 0
    return jnp.stack([jnp.where(first, here, there), jnp.where(first, there, here)])


def from_all(x, axes):
    peers = lax.axis_size(axes)
    return lax.all_to_all(jnp.broadcast_to(x[None], (peers, *x.shape)), axes, 0, 0, tiled=True)


def in_hbm(x):
    return pltpu.with_memory_space_constraint(x, pltpu.HBM)


def pack_kernel(place_ref, rgb_ref, flow_ref, decay_ref, *refs):
    sent, (parts_ref, sems, part_sem) = refs[:8], refs[8:]
    view, clip = place_ref[1], place_ref[6]
    clips, cells, channels = rgb_ref.shape
    frames = decay_ref.shape[1]

    def copy_of(maps_ref, k):
        return pltpu.make_async_copy(maps_ref.at[clip ^ (PEERS[k] % clips)], sent[k].at[:cells], sems.at[k])

    decay_copy = pltpu.make_async_copy(decay_ref, parts_ref, part_sem)
    decay_copy.start()
    for second in range(2):
        for v, maps_ref in enumerate((rgb_ref, flow_ref)):

            @pl.when((view ^ second) == v)
            def _(second=second, maps_ref=maps_ref):
                for k in range(2 * clips):
                    if PEERS[k] // clips == second:
                        copy_of(maps_ref, k).start()

    decay_copy.wait()
    for second in range(2):
        decays = parts_ref[view ^ second]
        high = decays.astype(BF16).astype(F32)
        middle = (decays - high).astype(BF16).astype(F32)
        low = decays - high - middle
        rows = sent[0].shape[0] - cells
        parts = [high, middle, low, jnp.zeros((rows - 3 * frames, channels), F32)]
        parts = jnp.concatenate(parts).astype(BF16)
        for k in range(2 * clips):
            if PEERS[k] // clips == second:
                sent[k][cells:] = parts
    for k in range(2 * clips):
        copy_of(rgb_ref, k).wait()


def clips_to_devices(rgb_maps, flow_maps, decay, place):
    clips, frames, side, _, channels = rgb_maps.shape
    cells = frames * side * side
    hbm = pl.BlockSpec(memory_space=pltpu.HBM)
    sent = pl.pallas_call(
        pack_kernel,
        out_shape=[jax.ShapeDtypeStruct((cells + 16, channels), BF16)] * (2 * clips),
        in_specs=[pl.BlockSpec(memory_space=pltpu.SMEM), hbm, hbm, hbm],
        out_specs=[pl.BlockSpec(memory_space=pltpu.VMEM)] * (2 * clips),
        scratch_shapes=[
            pltpu.VMEM(decay.shape, F32),
            pltpu.SemaphoreType.DMA((2 * clips,)),
            pltpu.SemaphoreType.DMA,
        ],
        compiler_params=pltpu.CompilerParams(vmem_limit_bytes=16 << 20),
    )(place, *(in_hbm(maps.reshape(clips, cells, channels)) for maps in (rgb_maps, flow_maps)), in_hbm(decay))
    peers = 2 * clips
    return [sent[0]] + [lax.ppermute(sent[k], TIME, [(i, i ^ PEERS[k]) for i in range(peers)]) for k in range(1, peers)]


def batch_norm(values):
    centered = values - jnp.mean(values, axis=0, keepdims=True)
    scale = lax.rsqrt(jnp.mean(centered * centered, axis=0, keepdims=True) + EPSILON)
    return centered * scale, scale


def norm_back(grad, normed, scale):
    mean = jnp.mean(grad, axis=0, keepdims=True)
    along = jnp.mean(grad * normed, axis=0, keepdims=True)
    return (grad - mean - normed * along) * scale


def across(a, b, **kinds):
    return lax.dot_general(a, b, (((1,), (1,)), ((), ())), preferred_element_type=F32, **kinds)


def projector_kernel(place_ref, seen_ref, in_ref, gain_ref, far_ref, dpool_ref, x_ref, n_ref, z_ref, zn_ref, out_ref, sems, *, cell_count):
    view, row = place_ref[1], place_ref[4]
    clips = seen_ref.shape[1]
    chunk = out_ref.shape[1] // CHUNKS
    columns = [slice(j * chunk, (j + 1) * chunk) for j in range(CHUNKS)]
    copies = [pltpu.make_async_copy(far_ref.at[:, c], out_ref.at[:, c], sems.at[j]) for j, c in enumerate(columns)]
    for copy in copies:
        copy.start()
    gain = gain_ref[...]
    pooled = jnp.concatenate([seen_ref[0] + seen_ref[3], seen_ref[1] + seen_ref[2]]) / cell_count
    hidden = jnp.dot(pooled, in_ref[...], precision=HIGHEST, preferred_element_type=F32)
    hidden_s, relus = [], []
    for v in range(2):
        x_ref[v], scale = batch_norm(hidden[v * clips : (v + 1) * clips])
        n_ref[v] = x_ref[v] * gain
        hidden_s.append(scale)
        relus.append(jnp.maximum(n_ref[v], 0.0).astype(BF16))
    relu_b = jnp.concatenate(relus)
    scales = []
    for copy, c in zip(copies, columns):
        copy.wait()
        z = jnp.dot(relu_b, out_ref[:, c], preferred_element_type=F32)
        for v in range(2):
            z_ref[v, :, c], scale = batch_norm(z[v * clips : (v + 1) * clips])
            zn_ref[v, :, c] = z_ref[v, :, c].astype(BF16)
            scales.append(scale)
    z_s = [jnp.concatenate(scales[v::2], axis=1) for v in range(2)]
    first = view == 0
    own, other = zn_ref[view].astype(F32), zn_ref[1 - view].astype(F32)
    corr_diag = jnp.sum(own * other, axis=0, keepdims=True) / clips
    extra = -2.0 * (1.0 - corr_diag) - 2.0 * LAMBDA_OFF * corr_diag
    gram = across(zn_ref[1 - view], zn_ref[1 - view])
    spread = jnp.dot(gram, own, precision=HIGHEST, preferred_element_type=F32)
    dzn = spread * (2.0 * LAMBDA_OFF / (clips * clips)) + other * (extra / clips)
    dz_b = norm_back(dzn, z_ref[view], jnp.where(first, z_s[0], z_s[1])).astype(BF16)
    dxh = jnp.where(n_ref[view] > 0, across(dz_b, out_ref[...]), 0.0) * gain
    dhidden = norm_back(dxh, x_ref[view], jnp.where(first, hidden_s[0], hidden_s[1]))
    mine = lax.broadcasted_iota(jnp.int32, dhidden.shape, 0) == row
    own_row = jnp.sum(jnp.where(mine, dhidden, 0.0), axis=0, keepdims=True)
    channels, width = in_ref.shape
    part = in_ref[:, :channels] * own_row[:, :channels]
    for k in range(channels, width, channels):
        part = part + in_ref[:, k : k + channels] * own_row[:, k : k + channels]
    dpool_ref[...] = jnp.sum(part.T, axis=0, keepdims=True) / cell_count


def projector_back(seen, proj_in, proj_gain, proj_out, place, cell_count):
    _, clips, channels = seen.shape
    width = proj_in.shape[1]
    wide = (2, clips, width)
    return pl.pallas_call(
        functools.partial(projector_kernel, cell_count=cell_count),
        out_shape=jax.ShapeDtypeStruct((1, channels), F32),
        in_specs=[pl.BlockSpec(memory_space=pltpu.SMEM)]
        + [pl.BlockSpec(memory_space=pltpu.VMEM)] * 3
        + [pl.BlockSpec(memory_space=pltpu.HBM)],
        scratch_shapes=[
            pltpu.VMEM(wide, F32),
            pltpu.VMEM(wide, F32),
            pltpu.VMEM(wide, F32),
            pltpu.VMEM(wide, BF16),
            pltpu.VMEM(proj_out.shape, BF16),
            pltpu.SemaphoreType.DMA((CHUNKS,)),
        ],
        cost_estimate=pl.CostEstimate(flops=6 * clips * width * width, transcendentals=0, bytes_accessed=2 * width * width),
        compiler_params=pltpu.CompilerParams(vmem_limit_bytes=26 << 20),
    )(place, seen, proj_in, proj_gain.reshape(1, width), in_hbm(proj_out))


def from_other_half(x):
    return lax.ppermute(x, PLANE, [(0, 3), (1, 2), (2, 1), (3, 0)])


def from_peer(x, axes, k):
    return lax.ppermute(x, axes, [(i, i ^ k) for i in range(4)])


def from_ring(x, axes):
    return [x] + [from_peer(x, axes, k) for k in (1, 2, 3)]


def total_of(arrays):
    return sum(a.astype(F32) for a in arrays)


def place_kernel(place_ref, *refs):
    view, core, ring = place_ref[1], place_ref[2], place_ref[3]
    outs, (whole_ref, sems) = refs[8:10], refs[10:]
    copies = []
    for n, out in enumerate(outs):
        for v in range(2):
            for shift, pieces in enumerate((refs[:4], refs[4:8])):
                for k, piece in enumerate(pieces):
                    rows = piece.shape[2]
                    start = pl.multiple_of((4 * (core ^ shift) + (ring ^ k)) * rows, rows)
                    whole_ref[n, v, pl.ds(start, rows)] = piece[n, v].astype(F32)
            copies.append(pltpu.make_async_copy(whole_ref.at[n, v], out.at[view ^ v], sems.at[n, v]))
            copies[-1].start()
    for copy in copies:
        copy.wait()


def summed(grads, place):
    taps, channels = grads[0].shape
    core, ring = lax.axis_index("core"), lax.axis_index("z")
    halves = jnp.stack(grads).reshape(len(grads), 2, 4, taps // 8, channels)
    mine = lax.dynamic_index_in_dim(halves, core, 1, False)
    given = lax.dynamic_index_in_dim(halves, 1 - core, 1, False)
    pieces = (mine + swapped(given)).astype(BF16)
    parts = [lax.dynamic_index_in_dim(pieces, ring, 1, False)]
    parts += [from_peer(lax.dynamic_index_in_dim(pieces, ring ^ k, 1, False), "z", k) for k in (1, 2, 3)]
    parts = from_ring(total_of(parts).astype(BF16), "y")
    parts = from_ring(total_of(parts).astype(BF16), PLANE)
    both = jnp.stack([total_of([parts[0], parts[3]]), total_of([parts[1], parts[2]])], axis=1).astype(BF16)
    mine = from_ring(both, "z")
    given = [swapped(a) for a in mine]
    whole = pltpu.HBM((2, taps, channels), F32)
    return tuple(
        pl.pallas_call(
            place_kernel,
            out_shape=[whole] * len(grads),
            in_specs=[pl.BlockSpec(memory_space=pltpu.SMEM)] + [pl.BlockSpec(memory_space=pltpu.VMEM)] * 8,
            out_specs=[pl.BlockSpec(memory_space=pltpu.HBM)] * len(grads),
            scratch_shapes=[pltpu.VMEM((len(grads), 2, taps, channels), F32), pltpu.SemaphoreType.DMA((len(grads), 2))],
            compiler_params=pltpu.CompilerParams(vmem_limit_bytes=16 << 20),
        )(place, *mine, *given)
    )


def per_device(
    rgb_maps, flow_maps, in_weights, out_weights, decay, skip, proj_in, proj_gain, proj_out
):
    half = lax.axis_index("xh")
    view = lax.axis_index("xl") ^ half
    _, frames_here, side, _, channels = rgb_maps.shape
    place = jnp.stack([half, view, lax.axis_index("core"), lax.axis_index("z"), lax.axis_index(("y", "z", "core")), lax.axis_index(TIME), lax.axis_index("y")])
    place = place.astype(jnp.int32)
    pieces = clips_to_devices(rgb_maps, flow_maps, decay, place)
    senders = len(pieces)
    cell_count = 2 * senders * frames_here * side * side
    plan = Plan(senders, frames_here, side, channels)
    skips = skip.reshape(2, 1, channels)
    here = plan.frames
    both = plan.small(pair_kernel, 2, jax.ShapeDtypeStruct((12 * channels, 2 * channels), BF16))(place, in_weights)
    piece_of = jax.ShapeDtypeStruct((frames_here, *plan.map), BF16)
    convolved = [plan.small(piece_kernel, 2, piece_of, plan.cols()[:1], False)(piece, both) for piece in pieces]
    inputs, decays, end = plan.small(gather_kernel, 17, [plan.maps_of(BF16), plan.decays_of(), plan.carry_of()])(
        place, *pieces, *convolved
    )
    got = plan.small(order_kernel, 9, jax.ShapeDtypeStruct((senders, *pieces[0].shape), BF16))(place, *pieces)
    income = from_other_half(end)
    states_b, slope, pooled_part = plan.call(
        mixed_step,
        False,
        [here, 2, None, "view", "view"],
        [plan.maps_of(BF16), plan.maps_of(F32), jax.ShapeDtypeStruct((1, channels), F32)],
        [here, here, None],
        [*plan.cols(), plan.both(), plan.carry(), pltpu.VMEM((side, channels), F32)],
        kept=(0, 1),
    )(place, inputs, decays, income, skips, out_weights)

    seen = from_all(from_cores(pooled_part[0]), ("xh", "xl", "y", "z"))
    dpool = projector_back(seen.reshape(4, -1, channels), proj_in, proj_gain, proj_out, place, cell_count)

    dmix_b, source, end = plan.call(
        from_out_step,
        True,
        [here, 2, None, "view"],
        [plan.maps_of(BF16), plan.maps_of(F32), plan.carry_of()],
        [here, here, None],
        [*plan.cols(), plan.both(), plan.carry()],
    )(place, slope, decays, dpool, out_weights)
    income = from_other_half(end)
    (out_grad,) = plan.call(
        out_grad_step,
        False,
        [here, here],
        [plan.grad_of()],
        [None],
        [*plan.cols(), plan.acc()],
    )(place, states_b, dmix_b)
    (in_grad,) = plan.call(
        in_grad_step,
        True,
        [2, here, here, 2, None, None, "view"],
        [plan.grad_of()],
        [None],
        [*plan.cols(), plan.carry(), pltpu.VMEM((here, *plan.map), BF16), plan.acc()],
    )(place, got, slope, source, decays, income, dpool, skips)
    return summed([in_grad, out_grad], place)


def solution(mesh):
    finer = Mesh(mesh.devices.reshape(2, 2, 4, 4, 2), ("xh", "xl", "y", "z", "core"))
    frames = ("xh", "xl", "y")
    return jax.shard_map(
        per_device,
        mesh=finer,
        in_specs=(
            P(("z", "core"), frames, None, None, None),
            P(("z", "core"), frames, None, None, None),
            P(),
            P(),
            P(None, frames, None),
            P(),
            P(),
            P(),
            P(),
        ),
        out_specs=(P(), P()),
        check_vma=False,
    )
```

```python
import functools

import jax
import jax.numpy as jnp
from jax import lax
from jax.experimental import pallas as pl
from jax.experimental.pallas import tpu as pltpu
from jax.sharding import Mesh
from jax.sharding import PartitionSpec as P

TIME = ("xl", "y")
PLANE = ("xh", "xl")


LAMBDA_OFF = 0.0051
EPSILON = 1e-05
HIGHEST = lax.Precision.HIGHEST


BF16, F32 = jnp.bfloat16, jnp.float32
CHUNKS = 8
PEERS = (0, 6, 1, 3, 2, 4, 5, 7)


def pair_weights(weights_ref, both_ref):
    taps, channels = weights_ref.shape[1:]
    third = taps // 3
    both_ref[:taps, :channels] = weights_ref[0]
    both_ref[taps:, :channels] = jnp.zeros((third, channels), BF16)
    both_ref[:third, channels:] = jnp.zeros((third, channels), BF16)
    both_ref[third:, channels:] = weights_ref[0]


def flipped_pair_weights(weights_ref, both_ref):
    taps, channels = weights_ref.shape[1:]
    third = taps // 3
    both_ref[taps:, :channels] = jnp.zeros((third, channels), BF16)
    both_ref[:third, channels:] = jnp.zeros((third, channels), BF16)
    for k in range(taps // channels):
        block = weights_ref[0, taps - (k + 1) * channels : taps - k * channels].astype(F32).T.astype(BF16)
        both_ref[k * channels : (k + 1) * channels, :channels] = block
        both_ref[third + k * channels : third + (k + 1) * channels, channels:] = block


def take_carry(carry_ref, income_ref, has_income):
    @pl.when(has_income)
    def _():
        carry_ref[...] = income_ref[...]

    @pl.when(jnp.logical_not(has_income))
    def _():
        carry_ref[...] = jnp.zeros_like(carry_ref)


def clear_edges(cols_ref):
    frames, _, _, side, lanes = cols_ref.shape
    cols_ref[:, 0, 0] = jnp.zeros((frames, side, lanes), BF16)
    cols_ref[:, side // 2, 1] = jnp.zeros((frames, side, lanes), BF16)


def spread_columns(maps, cols_ref):
    frames, pairs, _, side, channels = maps.shape
    flat = maps.astype(F32).reshape(frames * side * side, channels)
    column = lax.broadcasted_iota(jnp.int32, flat.shape, 0) & (side - 1)
    left = jnp.where(column == 0, 0.0, pltpu.roll(flat, 1, 0))
    right = jnp.where(column == side - 1, 0.0, pltpu.roll(flat, flat.shape[0] - 1, 0))
    for k, shifted in enumerate((left, flat, right)):
        rows = shifted.astype(BF16).reshape(frames, pairs, 2, side, channels)
        lanes = slice(k * channels, (k + 1) * channels)
        cols_ref[:, 0:pairs, 1, :, lanes] = rows[:, :, 0]
        cols_ref[:, 1 : pairs + 1, 0, :, lanes] = rows[:, :, 1]


def pair_patches(cols_ref):
    frames, ends, _, side, lanes = cols_ref.shape
    pairs = ends - 1
    pieces = [cols_ref[:, a : a + pairs, b].reshape(frames * pairs * side, lanes) for a in (0, 1) for b in (0, 1)]
    return jnp.concatenate(pieces, axis=1)


def pair_convolve(cols_ref, weights_ref):
    frames, ends, _, side, lanes = cols_ref.shape
    channels = lanes // 3
    both = jnp.dot(pair_patches(cols_ref), weights_ref[...], preferred_element_type=F32)
    shape = (frames, ends - 1, side, channels)
    return both[:, :channels].reshape(shape), both[:, channels:].reshape(shape)


def add_weight_product(cols, grads, acc_ref):
    frames, pairs, _, side, channels = grads.shape
    rows = frames * pairs * side
    both = [grads[:, :, k].reshape(rows, channels) for k in range(2)]
    acc_ref[...] += lax.dot_general(
        jnp.concatenate(both, axis=1),
        jnp.concatenate([pair_patches(cols_ref) for cols_ref in cols]),
        (((0,), (0,)), ((), ())),
        preferred_element_type=F32,
    )


def folded(acc_ref):
    channels = acc_ref.shape[0] // 2
    width = acc_ref.shape[1] // 4
    total = acc_ref[:channels, : 3 * width] + acc_ref[channels:, width:]
    return total.T


def spread_groups(groups, cols):
    for maps, cols_ref in zip(groups, cols):
        spread_columns(maps, cols_ref)


def halves(ref):
    group = ref.shape[0] // 2
    return [ref[:group], ref[group:]]


def got_maps(got_ref, shape):
    cells = shape[0] * shape[1] * shape[2] * shape[3] // 2
    return [got_ref[h, :cells].reshape(shape[0] // 2, *shape[1:]) for h in range(2)]


def decay_of(decays_ref, t):
    group = decays_ref.shape[1]
    return decays_ref[t // group, t % group : t % group + 1]


def pair_kernel(place_ref, weights_ref, both_ref):
    pair_weights(weights_ref.at[pl.ds(place_ref[1], 1)], both_ref)


def piece_kernel(piece_ref, both_ref, inputs_ref, cols_ref):
    frames, _, _, side, _ = inputs_ref.shape
    clear_edges(cols_ref)
    spread_columns(piece_ref[: frames * side * side].reshape(inputs_ref.shape), cols_ref)
    for k, rows in enumerate(pair_convolve(cols_ref, both_ref)):
        inputs_ref[:, :, k] = rows.astype(BF16)


def order_kernel(place_ref, *refs):
    for k in range(8):
        refs[8][place_ref[5] ^ PEERS[k]] = refs[k][...]


def gather_kernel(place_ref, *refs):
    pieces, convolved, (inputs_ref, decays_ref, end_ref) = refs[:8], refs[8:16], refs[16:]
    group = convolved[0].shape[0]
    cells = pieces[0].shape[0] - 16
    for k in range(8):
        sender = place_ref[5] ^ PEERS[k]
        inputs_ref[pl.ds(sender * group, group)] = convolved[k][...]
        parts = pieces[k][cells:].astype(F32)
        decays_ref[sender] = parts[:group] + parts[group : 2 * group] + parts[2 * group : 3 * group]

    def advance(t, carried):
        for n in range(group):
            carried = decays_ref[t, n : n + 1] * carried + inputs_ref[t * group + n].astype(F32)
        end_ref[...] = carried
        return carried

    lax.fori_loop(0, 8, advance, jnp.zeros(end_ref.shape, F32))


def mixed_step(first, final, place_ref, inputs_ref, decays_ref, income_ref, skip_ref, weights_ref, states_ref, slope_ref, pooled_ref, cols_a, cols_b, both_ref, carry_ref, sum_ref):
    cols = (cols_a, cols_b)
    frames = inputs_ref.shape[0]
    group = frames // 2

    @pl.when(first)
    def _():
        clear_edges(cols_a)
        clear_edges(cols_b)
        pair_weights(weights_ref, both_ref)
        take_carry(carry_ref, income_ref, place_ref[0] == 1)
        sum_ref[...] = jnp.zeros_like(sum_ref)

    carried = carry_ref[...]
    for t in range(frames):
        carried = decay_of(decays_ref, t) * carried + inputs_ref[t].astype(F32)
        states_ref[t] = carried.astype(BF16)
    carry_ref[...] = carried
    spread_groups(halves(states_ref), cols)
    total = sum_ref[...]
    for h in range(2):
        here = slice(h * group, (h + 1) * group)
        for k, rows in enumerate(pair_convolve(cols[h], both_ref)):
            mixed = rows + skip_ref[0] * inputs_ref[here, :, k].astype(F32)
            sigma = jax.nn.sigmoid(mixed)
            silu = mixed * sigma
            slope_ref[here, :, k] = sigma + silu * (1.0 - sigma)
            total = total + jnp.sum(silu, axis=(0, 1))
    sum_ref[...] = total

    @pl.when(final)
    def _():
        pooled_ref[...] = jnp.sum(total, axis=0, keepdims=True)


def from_out_step(first, final, place_ref, slope_ref, decays_ref, dpool_ref, weights_ref, dmix_ref, source_ref, end_ref, cols_a, cols_b, both_ref, carry_ref):
    cols = (cols_a, cols_b)
    frames = slope_ref.shape[0]
    group = frames // 2

    @pl.when(first)
    def _():
        clear_edges(cols_a)
        clear_edges(cols_b)
        flipped_pair_weights(weights_ref, both_ref)
        carry_ref[...] = jnp.zeros_like(carry_ref)

    dmix_ref[...] = (dpool_ref[...] * slope_ref[...]).astype(BF16)
    spread_groups(halves(dmix_ref), cols)
    for h in range(2):
        for k, rows in enumerate(pair_convolve(cols[h], both_ref)):
            source_ref[h * group : (h + 1) * group, :, k] = rows
    carried = carry_ref[...]
    for t in reversed(range(frames)):
        carried = decay_of(decays_ref, t) * (source_ref[t] + carried)
    carry_ref[...] = carried

    @pl.when(final)
    def _():
        end_ref[...] = carried


def out_grad_step(first, final, place_ref, states_ref, dmix_ref, grad_ref, cols_a, cols_b, acc_ref):

    @pl.when(first)
    def _():
        clear_edges(cols_a)
        clear_edges(cols_b)
        acc_ref[...] = jnp.zeros_like(acc_ref)

    spread_groups(halves(states_ref), (cols_a, cols_b))
    add_weight_product((cols_a, cols_b), dmix_ref[...], acc_ref)

    @pl.when(final)
    def _():
        grad_ref[...] = folded(acc_ref)


def in_grad_step(first, final, place_ref, got_ref, slope_ref, source_ref, decays_ref, income_ref, dpool_ref, skip_ref, grad_ref, cols_a, cols_b, carry_ref, dinput_ref, acc_ref):
    frames = slope_ref.shape[0]

    @pl.when(first)
    def _():
        clear_edges(cols_a)
        clear_edges(cols_b)
        take_carry(carry_ref, income_ref, place_ref[0] == 0)
        acc_ref[...] = jnp.zeros_like(acc_ref)

    spread_groups(got_maps(got_ref, slope_ref.shape), (cols_a, cols_b))
    carried = carry_ref[...]
    for t in reversed(range(frames)):
        carried = source_ref[t] + carried
        dmix = dpool_ref[...] * slope_ref[t]
        dinput_ref[t] = (carried + skip_ref[0] * dmix).astype(BF16)
        carried = decay_of(decays_ref, t) * carried
    carry_ref[...] = carried
    add_weight_product((cols_a, cols_b), dinput_ref[...], acc_ref)

    @pl.when(final)
    def _():
        grad_ref[...] = folded(acc_ref)


class Plan:
    def __init__(self, senders, group, side, channels):
        self.steps, self.frames, self.group, self.side, self.channels = senders // 2, 2 * group, group, side, channels
        self.map = (side // 2, 2, side, channels)

    def maps_of(self, dtype):
        return jax.ShapeDtypeStruct((self.steps * self.frames, *self.map), dtype)

    def carry_of(self):
        return jax.ShapeDtypeStruct(self.map, F32)

    def decays_of(self):
        return jax.ShapeDtypeStruct((2 * self.steps, self.group, self.channels), F32)

    def grad_of(self):
        return jax.ShapeDtypeStruct((9 * self.channels, self.channels), F32)

    def cols(self):
        return [pltpu.VMEM((self.group, self.side // 2 + 1, 2, self.side, 3 * self.channels), BF16)] * 2

    def carry(self):
        return pltpu.VMEM(self.map, F32)

    def acc(self):
        return pltpu.VMEM((2 * self.channels, 12 * self.channels), F32)

    def both(self):
        return pltpu.VMEM((12 * self.channels, 2 * self.channels), BF16)

    def small(self, kernel, arity, out_shape, scratch=(), placed=True):
        vmem = pl.BlockSpec(memory_space=pltpu.VMEM)
        return pl.pallas_call(
            kernel,
            out_shape=out_shape,
            in_specs=[pl.BlockSpec(memory_space=pltpu.SMEM) if placed else vmem] + [vmem] * (arity - 1),
            scratch_shapes=list(scratch),
            compiler_params=pltpu.CompilerParams(vmem_limit_bytes=16 << 20),
        )

    def call(self, run, back, takes, out_shape, gives, scratch, kept=()):
        cells = self.steps * self.frames * self.side * self.side
        work = 2 * 9 * cells * self.channels * self.channels
        blocks = [*takes, *gives]
        buffers = [pltpu.VMEM(out_shape[n].shape, out_shape[n].dtype) for n in kept]
        sems = [pltpu.SemaphoreType.DMA((len(kept), self.steps))] if kept else []
        first_out = len(takes)

        def kernel(place_ref, *refs):
            arrays, rest = list(refs[: len(blocks)]), refs[len(blocks) :]
            far = {}
            for k, n in enumerate(kept):
                far[k] = arrays[first_out + n]
                arrays[first_out + n] = rest[k]
            rest = rest[len(kept) :]
            if kept:
                sems_ref, rest = rest[-1], rest[:-1]

            def copy_of(k, i):
                rows = pl.ds(i * gives[kept[k]], gives[kept[k]])
                return pltpu.make_async_copy(arrays[first_out + kept[k]].at[rows], far[k].at[rows], sems_ref.at[k, i])

            def step(i, first, final):
                at = self.steps - 1 - i if back else i
                views = []
                for ref, block in zip(arrays, blocks):
                    if block == "view":
                        views.append(ref.at[pl.ds(place_ref[1], 1)])
                    else:
                        views.append(ref if block is None else ref.at[pl.ds(at * block, block)])
                run(first, final, place_ref, *views, *rest)
                for k in range(len(kept)):
                    copy_of(k, at).start()

            def two_steps(i, _):
                step(2 * i, i == 0, False)
                step(2 * i + 1, False, i == self.steps // 2 - 1)
                return 0

            if kept:
                lax.fori_loop(0, self.steps // 2, two_steps, 0)
            else:
                for i in range(self.steps):
                    step(i, i == 0, i == self.steps - 1)
            for k in range(len(kept)):
                for i in range(self.steps):
                    copy_of(k, i).wait()

        vmem, hbm = pl.BlockSpec(memory_space=pltpu.VMEM), pl.BlockSpec(memory_space=pltpu.HBM)
        return pl.pallas_call(
            kernel,
            out_shape=[pltpu.HBM(o.shape, o.dtype) if n in kept else o for n, o in enumerate(out_shape)],
            in_specs=[pl.BlockSpec(memory_space=pltpu.SMEM)] + [vmem] * len(takes),
            out_specs=[hbm if n in kept else vmem for n in range(len(out_shape))],
            scratch_shapes=[*buffers, *scratch, *sems],
            cost_estimate=pl.CostEstimate(flops=2 * work, transcendentals=0, bytes_accessed=4 * cells * self.channels),
            compiler_params=pltpu.CompilerParams(vmem_limit_bytes=24 << 20),
        )


def swapped(x):
    return lax.ppermute(x, "core", [(0, 1), (1, 0)])


def from_cores(x):
    here, there = x, swapped(x)
    first = lax.axis_index("core") == 0
    return jnp.stack([jnp.where(first, here, there), jnp.where(first, there, here)])


def from_all(x, axes):
    peers = lax.axis_size(axes)
    return lax.all_to_all(jnp.broadcast_to(x[None], (peers, *x.shape)), axes, 0, 0, tiled=True)


def in_hbm(x):
    return pltpu.with_memory_space_constraint(x, pltpu.HBM)


def pack_kernel(place_ref, rgb_ref, flow_ref, decay_ref, *refs):
    sent, (parts_ref, sems, part_sem) = refs[:8], refs[8:]
    view, clip = place_ref[1], place_ref[6]
    clips, cells, channels = rgb_ref.shape
    frames = decay_ref.shape[1]

    def copy_of(maps_ref, k):
        return pltpu.make_async_copy(maps_ref.at[clip ^ (PEERS[k] % clips)], sent[k].at[:cells], sems.at[k])

    decay_copy = pltpu.make_async_copy(decay_ref, parts_ref, part_sem)
    decay_copy.start()
    for second in range(2):
        for v, maps_ref in enumerate((rgb_ref, flow_ref)):

            @pl.when((view ^ second) == v)
            def _(second=second, maps_ref=maps_ref):
                for k in range(2 * clips):
                    if PEERS[k] // clips == second:
                        copy_of(maps_ref, k).start()

    decay_copy.wait()
    for second in range(2):
        decays = parts_ref[view ^ second]
        high = decays.astype(BF16).astype(F32)
        middle = (decays - high).astype(BF16).astype(F32)
        low = decays - high - middle
        rows = sent[0].shape[0] - cells
        parts = [high, middle, low, jnp.zeros((rows - 3 * frames, channels), F32)]
        parts = jnp.concatenate(parts).astype(BF16)
        for k in range(2 * clips):
            if PEERS[k] // clips == second:
                sent[k][cells:] = parts
    for k in range(2 * clips):
        copy_of(rgb_ref, k).wait()


def clips_to_devices(rgb_maps, flow_maps, decay, place):
    clips, frames, side, _, channels = rgb_maps.shape
    cells = frames * side * side
    hbm = pl.BlockSpec(memory_space=pltpu.HBM)
    sent = pl.pallas_call(
        pack_kernel,
        out_shape=[jax.ShapeDtypeStruct((cells + 16, channels), BF16)] * (2 * clips),
        in_specs=[pl.BlockSpec(memory_space=pltpu.SMEM), hbm, hbm, hbm],
        out_specs=[pl.BlockSpec(memory_space=pltpu.VMEM)] * (2 * clips),
        scratch_shapes=[
            pltpu.VMEM(decay.shape, F32),
            pltpu.SemaphoreType.DMA((2 * clips,)),
            pltpu.SemaphoreType.DMA,
        ],
        compiler_params=pltpu.CompilerParams(vmem_limit_bytes=16 << 20),
    )(place, *(in_hbm(maps.reshape(clips, cells, channels)) for maps in (rgb_maps, flow_maps)), in_hbm(decay))
    peers = 2 * clips
    return [sent[0]] + [lax.ppermute(sent[k], TIME, [(i, i ^ PEERS[k]) for i in range(peers)]) for k in range(1, peers)]


def batch_norm(values):
    centered = values - jnp.mean(values, axis=0, keepdims=True)
    scale = lax.rsqrt(jnp.mean(centered * centered, axis=0, keepdims=True) + EPSILON)
    return centered * scale, scale


def norm_back(grad, normed, scale):
    mean = jnp.mean(grad, axis=0, keepdims=True)
    along = jnp.mean(grad * normed, axis=0, keepdims=True)
    return (grad - mean - normed * along) * scale


def across(a, b, **kinds):
    return lax.dot_general(a, b, (((1,), (1,)), ((), ())), preferred_element_type=F32, **kinds)


def projector_kernel(place_ref, seen_ref, in_ref, gain_ref, far_ref, dpool_ref, x_ref, n_ref, z_ref, zn_ref, out_ref, sems, *, cell_count):
    view, row = place_ref[1], place_ref[4]
    clips = seen_ref.shape[1]
    chunk = out_ref.shape[1] // CHUNKS
    columns = [slice(j * chunk, (j + 1) * chunk) for j in range(CHUNKS)]
    copies = [pltpu.make_async_copy(far_ref.at[:, c], out_ref.at[:, c], sems.at[j]) for j, c in enumerate(columns)]
    for copy in copies:
        copy.start()
    gain = gain_ref[...]
    pooled = jnp.concatenate([seen_ref[0] + seen_ref[3], seen_ref[1] + seen_ref[2]]) / cell_count
    hidden = jnp.dot(pooled, in_ref[...], precision=HIGHEST, preferred_element_type=F32)
    hidden_s, relus = [], []
    for v in range(2):
        x_ref[v], scale = batch_norm(hidden[v * clips : (v + 1) * clips])
        n_ref[v] = x_ref[v] * gain
        hidden_s.append(scale)
        relus.append(jnp.maximum(n_ref[v], 0.0).astype(BF16))
    relu_b = jnp.concatenate(relus)
    scales = []
    for copy, c in zip(copies, columns):
        copy.wait()
        z = jnp.dot(relu_b, out_ref[:, c], preferred_element_type=F32)
        for v in range(2):
            z_ref[v, :, c], scale = batch_norm(z[v * clips : (v + 1) * clips])
            zn_ref[v, :, c] = z_ref[v, :, c].astype(BF16)
            scales.append(scale)
    z_s = [jnp.concatenate(scales[v::2], axis=1) for v in range(2)]
    first = view == 0
    own, other = zn_ref[view].astype(F32), zn_ref[1 - view].astype(F32)
    corr_diag = jnp.sum(own * other, axis=0, keepdims=True) / clips
    extra = -2.0 * (1.0 - corr_diag) - 2.0 * LAMBDA_OFF * corr_diag
    gram = across(zn_ref[1 - view], zn_ref[1 - view])
    spread = jnp.dot(gram, own, precision=HIGHEST, preferred_element_type=F32)
    dzn = spread * (2.0 * LAMBDA_OFF / (clips * clips)) + other * (extra / clips)
    dz_b = norm_back(dzn, z_ref[view], jnp.where(first, z_s[0], z_s[1])).astype(BF16)
    dxh = jnp.where(n_ref[view] > 0, across(dz_b, out_ref[...]), 0.0) * gain
    dhidden = norm_back(dxh, x_ref[view], jnp.where(first, hidden_s[0], hidden_s[1]))
    mine = lax.broadcasted_iota(jnp.int32, dhidden.shape, 0) == row
    own_row = jnp.sum(jnp.where(mine, dhidden, 0.0), axis=0, keepdims=True)
    channels, width = in_ref.shape
    part = in_ref[:, :channels] * own_row[:, :channels]
    for k in range(channels, width, channels):
        part = part + in_ref[:, k : k + channels] * own_row[:, k : k + channels]
    dpool_ref[...] = jnp.sum(part.T, axis=0, keepdims=True) / cell_count


def projector_back(seen, proj_in, proj_gain, proj_out, place, cell_count):
    _, clips, channels = seen.shape
    width = proj_in.shape[1]
    wide = (2, clips, width)
    return pl.pallas_call(
        functools.partial(projector_kernel, cell_count=cell_count),
        out_shape=jax.ShapeDtypeStruct((1, channels), F32),
        in_specs=[pl.BlockSpec(memory_space=pltpu.SMEM)]
        + [pl.BlockSpec(memory_space=pltpu.VMEM)] * 3
        + [pl.BlockSpec(memory_space=pltpu.HBM)],
        scratch_shapes=[
            pltpu.VMEM(wide, F32),
            pltpu.VMEM(wide, F32),
            pltpu.VMEM(wide, F32),
            pltpu.VMEM(wide, BF16),
            pltpu.VMEM(proj_out.shape, BF16),
            pltpu.SemaphoreType.DMA((CHUNKS,)),
        ],
        cost_estimate=pl.CostEstimate(flops=6 * clips * width * width, transcendentals=0, bytes_accessed=2 * width * width),
        compiler_params=pltpu.CompilerParams(vmem_limit_bytes=26 << 20),
    )(place, seen, proj_in, proj_gain.reshape(1, width), in_hbm(proj_out))


def from_other_half(x):
    return lax.ppermute(x, PLANE, [(0, 3), (1, 2), (2, 1), (3, 0)])


def from_peer(x, axes, k):
    return lax.ppermute(x, axes, [(i, i ^ k) for i in range(4)])


def from_ring(x, axes):
    return [x] + [from_peer(x, axes, k) for k in (1, 2, 3)]


def total_of(arrays):
    return sum(a.astype(F32) for a in arrays)


def place_kernel(place_ref, *refs):
    view, core, ring = place_ref[1], place_ref[2], place_ref[3]
    outs, (whole_ref, sems) = refs[8:10], refs[10:]
    copies = []
    for n, out in enumerate(outs):
        for v in range(2):
            for shift, pieces in enumerate((refs[:4], refs[4:8])):
                for k, piece in enumerate(pieces):
                    rows = piece.shape[2]
                    start = pl.multiple_of((4 * (core ^ shift) + (ring ^ k)) * rows, rows)
                    whole_ref[n, v, pl.ds(start, rows)] = piece[n, v].astype(F32)
            copies.append(pltpu.make_async_copy(whole_ref.at[n, v], out.at[view ^ v], sems.at[n, v]))
            copies[-1].start()
    for copy in copies:
        copy.wait()


def summed(grads, place):
    taps, channels = grads[0].shape
    core, ring = lax.axis_index("core"), lax.axis_index("z")
    halves = jnp.stack(grads).reshape(len(grads), 2, 4, taps // 8, channels)
    mine = lax.dynamic_index_in_dim(halves, core, 1, False)
    given = lax.dynamic_index_in_dim(halves, 1 - core, 1, False)
    pieces = (mine + swapped(given.astype(BF16)).astype(F32)).astype(BF16)
    parts = [lax.dynamic_index_in_dim(pieces, ring, 1, False)]
    parts += [from_peer(lax.dynamic_index_in_dim(pieces, ring ^ k, 1, False), "z", k) for k in (1, 2, 3)]
    parts = from_ring(total_of(parts).astype(BF16), "y")
    parts = from_ring(total_of(parts).astype(BF16), PLANE)
    both = jnp.stack([total_of([parts[0], parts[3]]), total_of([parts[1], parts[2]])], axis=1).astype(BF16)
    mine = from_ring(both, "z")
    given = [swapped(a) for a in mine]
    whole = pltpu.HBM((2, taps, channels), F32)
    return tuple(
        pl.pallas_call(
            place_kernel,
            out_shape=[whole] * len(grads),
            in_specs=[pl.BlockSpec(memory_space=pltpu.SMEM)] + [pl.BlockSpec(memory_space=pltpu.VMEM)] * 8,
            out_specs=[pl.BlockSpec(memory_space=pltpu.HBM)] * len(grads),
            scratch_shapes=[pltpu.VMEM((len(grads), 2, taps, channels), F32), pltpu.SemaphoreType.DMA((len(grads), 2))],
            compiler_params=pltpu.CompilerParams(vmem_limit_bytes=16 << 20),
        )(place, *mine, *given)
    )


def per_device(
    rgb_maps, flow_maps, in_weights, out_weights, decay, skip, proj_in, proj_gain, proj_out
):
    half = lax.axis_index("xh")
    view = lax.axis_index("xl") ^ half
    _, frames_here, side, _, channels = rgb_maps.shape
    place = jnp.stack([half, view, lax.axis_index("core"), lax.axis_index("z"), lax.axis_index(("y", "z", "core")), lax.axis_index(TIME), lax.axis_index("y")])
    place = place.astype(jnp.int32)
    pieces = clips_to_devices(rgb_maps, flow_maps, decay, place)
    senders = len(pieces)
    cell_count = 2 * senders * frames_here * side * side
    plan = Plan(senders, frames_here, side, channels)
    skips = skip.reshape(2, 1, channels)
    here = plan.frames
    both = plan.small(pair_kernel, 2, jax.ShapeDtypeStruct((12 * channels, 2 * channels), BF16))(place, in_weights)
    piece_of = jax.ShapeDtypeStruct((frames_here, *plan.map), BF16)
    convolved = [plan.small(piece_kernel, 2, piece_of, plan.cols()[:1], False)(piece, both) for piece in pieces]
    inputs, decays, end = plan.small(gather_kernel, 17, [plan.maps_of(BF16), plan.decays_of(), plan.carry_of()])(
        place, *pieces, *convolved
    )
    got = plan.small(order_kernel, 9, jax.ShapeDtypeStruct((senders, *pieces[0].shape), BF16))(place, *pieces)
    income = from_other_half(end)
    states_b, slope, pooled_part = plan.call(
        mixed_step,
        False,
        [here, 2, None, "view", "view"],
        [plan.maps_of(BF16), plan.maps_of(F32), jax.ShapeDtypeStruct((1, channels), F32)],
        [here, here, None],
        [*plan.cols(), plan.both(), plan.carry(), pltpu.VMEM((side, channels), F32)],
        kept=(0, 1),
    )(place, inputs, decays, income, skips, out_weights)

    seen = from_all(from_cores(pooled_part[0]), ("xh", "xl", "y", "z"))
    dpool = projector_back(seen.reshape(4, -1, channels), proj_in, proj_gain, proj_out, place, cell_count)

    dmix_b, source, end = plan.call(
        from_out_step,
        True,
        [here, 2, None, "view"],
        [plan.maps_of(BF16), plan.maps_of(F32), plan.carry_of()],
        [here, here, None],
        [*plan.cols(), plan.both(), plan.carry()],
    )(place, slope, decays, dpool, out_weights)
    income = from_other_half(end)
    (out_grad,) = plan.call(
        out_grad_step,
        False,
        [here, here],
        [plan.grad_of()],
        [None],
        [*plan.cols(), plan.acc()],
    )(place, states_b, dmix_b)
    (in_grad,) = plan.call(
        in_grad_step,
        True,
        [2, here, here, 2, None, None, "view"],
        [plan.grad_of()],
        [None],
        [*plan.cols(), plan.carry(), pltpu.VMEM((here, *plan.map), BF16), plan.acc()],
    )(place, got, slope, source, decays, income, dpool, skips)
    return summed([in_grad, out_grad], place)


def solution(mesh):
    finer = Mesh(mesh.devices.reshape(2, 2, 4, 4, 2), ("xh", "xl", "y", "z", "core"))
    frames = ("xh", "xl", "y")
    return jax.shard_map(
        per_device,
        mesh=finer,
        in_specs=(
            P(("z", "core"), frames, None, None, None),
            P(("z", "core"), frames, None, None, None),
            P(),
            P(),
            P(None, frames, None),
            P(),
            P(),
            P(),
            P(),
        ),
        out_specs=(P(), P()),
        check_vma=False,
    )
```

```python
import functools

import jax
import jax.numpy as jnp
from jax import lax
from jax.experimental import pallas as pl
from jax.experimental.pallas import tpu as pltpu
from jax.sharding import Mesh
from jax.sharding import PartitionSpec as P

TIME = ("xl", "y")
PLANE = ("xh", "xl")


LAMBDA_OFF = 0.0051
EPSILON = 1e-05
HIGHEST = lax.Precision.HIGHEST


BF16, F32 = jnp.bfloat16, jnp.float32
CHUNKS = 2
PEERS = (0, 6, 1, 3, 2, 4, 5, 7)


def pair_weights(weights_ref, both_ref):
    taps, channels = weights_ref.shape[1:]
    third = taps // 3
    both_ref[:taps, :channels] = weights_ref[0]
    both_ref[taps:, :channels] = jnp.zeros((third, channels), BF16)
    both_ref[:third, channels:] = jnp.zeros((third, channels), BF16)
    both_ref[third:, channels:] = weights_ref[0]


def flipped_pair_weights(weights_ref, both_ref):
    taps, channels = weights_ref.shape[1:]
    third = taps // 3
    both_ref[taps:, :channels] = jnp.zeros((third, channels), BF16)
    both_ref[:third, channels:] = jnp.zeros((third, channels), BF16)
    for k in range(taps // channels):
        block = weights_ref[0, taps - (k + 1) * channels : taps - k * channels].astype(F32).T.astype(BF16)
        both_ref[k * channels : (k + 1) * channels, :channels] = block
        both_ref[third + k * channels : third + (k + 1) * channels, channels:] = block


def take_carry(carry_ref, income_ref, has_income):
    @pl.when(has_income)
    def _():
        carry_ref[...] = income_ref[...]

    @pl.when(jnp.logical_not(has_income))
    def _():
        carry_ref[...] = jnp.zeros_like(carry_ref)


def clear_edges(cols_ref):
    frames, _, _, side, lanes = cols_ref.shape
    cols_ref[:, 0, 0] = jnp.zeros((frames, side, lanes), BF16)
    cols_ref[:, side // 2, 1] = jnp.zeros((frames, side, lanes), BF16)


def spread_columns(maps, cols_ref):
    frames, pairs, _, side, channels = maps.shape
    flat = maps.astype(F32).reshape(frames * side * side, channels)
    column = lax.broadcasted_iota(jnp.int32, flat.shape, 0) & (side - 1)
    left = jnp.where(column == 0, 0.0, pltpu.roll(flat, 1, 0))
    right = jnp.where(column == side - 1, 0.0, pltpu.roll(flat, flat.shape[0] - 1, 0))
    for k, shifted in enumerate((left, flat, right)):
        rows = shifted.astype(BF16).reshape(frames, pairs, 2, side, channels)
        lanes = slice(k * channels, (k + 1) * channels)
        cols_ref[:, 0:pairs, 1, :, lanes] = rows[:, :, 0]
        cols_ref[:, 1 : pairs + 1, 0, :, lanes] = rows[:, :, 1]


def pair_patches(cols_ref):
    frames, ends, _, side, lanes = cols_ref.shape
    pairs = ends - 1
    pieces = [cols_ref[:, a : a + pairs, b].reshape(frames * pairs * side, lanes) for a in (0, 1) for b in (0, 1)]
    return jnp.concatenate(pieces, axis=1)


def pair_convolve(cols_ref, weights_ref):
    frames, ends, _, side, lanes = cols_ref.shape
    channels = lanes // 3
    both = jnp.dot(pair_patches(cols_ref), weights_ref[...], preferred_element_type=F32)
    shape = (frames, ends - 1, side, channels)
    return both[:, :channels].reshape(shape), both[:, channels:].reshape(shape)


def add_weight_product(cols, grads, acc_ref):
    frames, pairs, _, side, channels = grads.shape
    rows = frames * pairs * side
    both = [grads[:, :, k].reshape(rows, channels) for k in range(2)]
    acc_ref[...] += lax.dot_general(
        jnp.concatenate(both, axis=1),
        jnp.concatenate([pair_patches(cols_ref) for cols_ref in cols]),
        (((0,), (0,)), ((), ())),
        preferred_element_type=F32,
    )


def folded(acc_ref):
    channels = acc_ref.shape[0] // 2
    width = acc_ref.shape[1] // 4
    total = acc_ref[:channels, : 3 * width] + acc_ref[channels:, width:]
    return total.T


def spread_groups(groups, cols):
    for maps, cols_ref in zip(groups, cols):
        spread_columns(maps, cols_ref)


def halves(ref):
    group = ref.shape[0] // 2
    return [ref[:group], ref[group:]]


def got_maps(got_ref, shape):
    cells = shape[0] * shape[1] * shape[2] * shape[3] // 2
    return [got_ref[h, :cells].reshape(shape[0] // 2, *shape[1:]) for h in range(2)]


def decay_of(decays_ref, t):
    group = decays_ref.shape[1]
    return decays_ref[t // group, t % group : t % group + 1]


def pair_kernel(place_ref, weights_ref, both_ref):
    pair_weights(weights_ref.at[pl.ds(place_ref[1], 1)], both_ref)


def piece_kernel(piece_ref, both_ref, inputs_ref, cols_ref):
    frames, _, _, side, _ = inputs_ref.shape
    clear_edges(cols_ref)
    spread_columns(piece_ref[: frames * side * side].reshape(inputs_ref.shape), cols_ref)
    for k, rows in enumerate(pair_convolve(cols_ref, both_ref)):
        inputs_ref[:, :, k] = rows.astype(BF16)


def order_kernel(place_ref, *refs):
    for k in range(8):
        refs[8][place_ref[5] ^ PEERS[k]] = refs[k][...]


def gather_kernel(place_ref, *refs):
    pieces, convolved, (inputs_ref, decays_ref, end_ref) = refs[:8], refs[8:16], refs[16:]
    group = convolved[0].shape[0]
    cells = pieces[0].shape[0] - 16
    for k in range(8):
        sender = place_ref[5] ^ PEERS[k]
        inputs_ref[pl.ds(sender * group, group)] = convolved[k][...]
        parts = pieces[k][cells:].astype(F32)
        decays_ref[sender] = parts[:group] + parts[group : 2 * group] + parts[2 * group : 3 * group]

    def advance(t, carried):
        for n in range(group):
            carried = decays_ref[t, n : n + 1] * carried + inputs_ref[t * group + n].astype(F32)
        end_ref[...] = carried
        return carried

    lax.fori_loop(0, 8, advance, jnp.zeros(end_ref.shape, F32))


def mixed_step(first, final, place_ref, inputs_ref, decays_ref, income_ref, skip_ref, weights_ref, states_ref, slope_ref, pooled_ref, cols_a, cols_b, both_ref, carry_ref, sum_ref):
    cols = (cols_a, cols_b)
    frames = inputs_ref.shape[0]
    group = frames // 2

    @pl.when(first)
    def _():
        clear_edges(cols_a)
        clear_edges(cols_b)
        pair_weights(weights_ref, both_ref)
        take_carry(carry_ref, income_ref, place_ref[0] == 1)
        sum_ref[...] = jnp.zeros_like(sum_ref)

    carried = carry_ref[...]
    for t in range(frames):
        carried = decay_of(decays_ref, t) * carried + inputs_ref[t].astype(F32)
        states_ref[t] = carried.astype(BF16)
    carry_ref[...] = carried
    spread_groups(halves(states_ref), cols)
    total = sum_ref[...]
    for h in range(2):
        here = slice(h * group, (h + 1) * group)
        for k, rows in enumerate(pair_convolve(cols[h], both_ref)):
            mixed = rows + skip_ref[0] * inputs_ref[here, :, k].astype(F32)
            sigma = jax.nn.sigmoid(mixed)
            silu = mixed * sigma
            slope_ref[here, :, k] = sigma + silu * (1.0 - sigma)
            total = total + jnp.sum(silu, axis=(0, 1))
    sum_ref[...] = total

    @pl.when(final)
    def _():
        pooled_ref[...] = jnp.sum(total, axis=0, keepdims=True)


def from_out_step(first, final, place_ref, slope_ref, decays_ref, dpool_ref, weights_ref, dmix_ref, source_ref, end_ref, cols_a, cols_b, both_ref, carry_ref):
    cols = (cols_a, cols_b)
    frames = slope_ref.shape[0]
    group = frames // 2

    @pl.when(first)
    def _():
        clear_edges(cols_a)
        clear_edges(cols_b)
        flipped_pair_weights(weights_ref, both_ref)
        carry_ref[...] = jnp.zeros_like(carry_ref)

    dmix_ref[...] = (dpool_ref[...] * slope_ref[...]).astype(BF16)
    spread_groups(halves(dmix_ref), cols)
    for h in range(2):
        for k, rows in enumerate(pair_convolve(cols[h], both_ref)):
            source_ref[h * group : (h + 1) * group, :, k] = rows
    carried = carry_ref[...]
    for t in reversed(range(frames)):
        carried = decay_of(decays_ref, t) * (source_ref[t] + carried)
    carry_ref[...] = carried

    @pl.when(final)
    def _():
        end_ref[...] = carried


def out_grad_step(first, final, place_ref, states_ref, dmix_ref, grad_ref, cols_a, cols_b, acc_ref):

    @pl.when(first)
    def _():
        clear_edges(cols_a)
        clear_edges(cols_b)
        acc_ref[...] = jnp.zeros_like(acc_ref)

    spread_groups(halves(states_ref), (cols_a, cols_b))
    add_weight_product((cols_a, cols_b), dmix_ref[...], acc_ref)

    @pl.when(final)
    def _():
        grad_ref[...] = folded(acc_ref)


def in_grad_step(first, final, place_ref, got_ref, slope_ref, source_ref, decays_ref, income_ref, dpool_ref, skip_ref, grad_ref, cols_a, cols_b, carry_ref, dinput_ref, acc_ref):
    frames = slope_ref.shape[0]

    @pl.when(first)
    def _():
        clear_edges(cols_a)
        clear_edges(cols_b)
        take_carry(carry_ref, income_ref, place_ref[0] == 0)
        acc_ref[...] = jnp.zeros_like(acc_ref)

    spread_groups(got_maps(got_ref, slope_ref.shape), (cols_a, cols_b))
    carried = carry_ref[...]
    for t in reversed(range(frames)):
        carried = source_ref[t] + carried
        dmix = dpool_ref[...] * slope_ref[t]
        dinput_ref[t] = (carried + skip_ref[0] * dmix).astype(BF16)
        carried = decay_of(decays_ref, t) * carried
    carry_ref[...] = carried
    add_weight_product((cols_a, cols_b), dinput_ref[...], acc_ref)

    @pl.when(final)
    def _():
        grad_ref[...] = folded(acc_ref)


class Plan:
    def __init__(self, senders, group, side, channels):
        self.steps, self.frames, self.group, self.side, self.channels = senders // 2, 2 * group, group, side, channels
        self.map = (side // 2, 2, side, channels)

    def maps_of(self, dtype):
        return jax.ShapeDtypeStruct((self.steps * self.frames, *self.map), dtype)

    def carry_of(self):
        return jax.ShapeDtypeStruct(self.map, F32)

    def decays_of(self):
        return jax.ShapeDtypeStruct((2 * self.steps, self.group, self.channels), F32)

    def grad_of(self):
        return jax.ShapeDtypeStruct((9 * self.channels, self.channels), F32)

    def cols(self):
        return [pltpu.VMEM((self.group, self.side // 2 + 1, 2, self.side, 3 * self.channels), BF16)] * 2

    def carry(self):
        return pltpu.VMEM(self.map, F32)

    def acc(self):
        return pltpu.VMEM((2 * self.channels, 12 * self.channels), F32)

    def both(self):
        return pltpu.VMEM((12 * self.channels, 2 * self.channels), BF16)

    def small(self, kernel, arity, out_shape, scratch=(), placed=True):
        vmem = pl.BlockSpec(memory_space=pltpu.VMEM)
        return pl.pallas_call(
            kernel,
            out_shape=out_shape,
            in_specs=[pl.BlockSpec(memory_space=pltpu.SMEM) if placed else vmem] + [vmem] * (arity - 1),
            scratch_shapes=list(scratch),
            compiler_params=pltpu.CompilerParams(vmem_limit_bytes=16 << 20),
        )

    def call(self, run, back, takes, out_shape, gives, scratch, kept=()):
        cells = self.steps * self.frames * self.side * self.side
        work = 2 * 9 * cells * self.channels * self.channels
        blocks = [*takes, *gives]
        buffers = [pltpu.VMEM(out_shape[n].shape, out_shape[n].dtype) for n in kept]
        sems = [pltpu.SemaphoreType.DMA((len(kept), self.steps))] if kept else []
        first_out = len(takes)

        def kernel(place_ref, *refs):
            arrays, rest = list(refs[: len(blocks)]), refs[len(blocks) :]
            far = {}
            for k, n in enumerate(kept):
                far[k] = arrays[first_out + n]
                arrays[first_out + n] = rest[k]
            rest = rest[len(kept) :]
            if kept:
                sems_ref, rest = rest[-1], rest[:-1]

            def copy_of(k, i):
                rows = pl.ds(i * gives[kept[k]], gives[kept[k]])
                return pltpu.make_async_copy(arrays[first_out + kept[k]].at[rows], far[k].at[rows], sems_ref.at[k, i])

            def step(i, first, final):
                at = self.steps - 1 - i if back else i
                views = []
                for ref, block in zip(arrays, blocks):
                    if block == "view":
                        views.append(ref.at[pl.ds(place_ref[1], 1)])
                    else:
                        views.append(ref if block is None else ref.at[pl.ds(at * block, block)])
                run(first, final, place_ref, *views, *rest)
                for k in range(len(kept)):
                    copy_of(k, at).start()

            def two_steps(i, _):
                step(2 * i, i == 0, False)
                step(2 * i + 1, False, i == self.steps // 2 - 1)
                return 0

            if kept:
                lax.fori_loop(0, self.steps // 2, two_steps, 0)
            else:
                for i in range(self.steps):
                    step(i, i == 0, i == self.steps - 1)
            for k in range(len(kept)):
                for i in range(self.steps):
                    copy_of(k, i).wait()

        vmem, hbm = pl.BlockSpec(memory_space=pltpu.VMEM), pl.BlockSpec(memory_space=pltpu.HBM)
        return pl.pallas_call(
            kernel,
            out_shape=[pltpu.HBM(o.shape, o.dtype) if n in kept else o for n, o in enumerate(out_shape)],
            in_specs=[pl.BlockSpec(memory_space=pltpu.SMEM)] + [vmem] * len(takes),
            out_specs=[hbm if n in kept else vmem for n in range(len(out_shape))],
            scratch_shapes=[*buffers, *scratch, *sems],
            cost_estimate=pl.CostEstimate(flops=2 * work, transcendentals=0, bytes_accessed=4 * cells * self.channels),
            compiler_params=pltpu.CompilerParams(vmem_limit_bytes=24 << 20),
        )


def swapped(x):
    return lax.ppermute(x, "core", [(0, 1), (1, 0)])


def from_cores(x):
    here, there = x, swapped(x)
    first = lax.axis_index("core") == 0
    return jnp.stack([jnp.where(first, here, there), jnp.where(first, there, here)])


def from_all(x, axes):
    peers = lax.axis_size(axes)
    return lax.all_to_all(jnp.broadcast_to(x[None], (peers, *x.shape)), axes, 0, 0, tiled=True)


def in_hbm(x):
    return pltpu.with_memory_space_constraint(x, pltpu.HBM)


def pack_kernel(place_ref, rgb_ref, flow_ref, decay_ref, *refs):
    sent, (parts_ref, sems, part_sem) = refs[:8], refs[8:]
    view, clip = place_ref[1], place_ref[6]
    clips, cells, channels = rgb_ref.shape
    frames = decay_ref.shape[1]

    def copy_of(maps_ref, k):
        return pltpu.make_async_copy(maps_ref.at[clip ^ (PEERS[k] % clips)], sent[k].at[:cells], sems.at[k])

    decay_copy = pltpu.make_async_copy(decay_ref, parts_ref, part_sem)
    decay_copy.start()
    for second in range(2):
        for v, maps_ref in enumerate((rgb_ref, flow_ref)):

            @pl.when((view ^ second) == v)
            def _(second=second, maps_ref=maps_ref):
                for k in range(2 * clips):
                    if PEERS[k] // clips == second:
                        copy_of(maps_ref, k).start()

    decay_copy.wait()
    for second in range(2):
        decays = parts_ref[view ^ second]
        high = decays.astype(BF16).astype(F32)
        middle = (decays - high).astype(BF16).astype(F32)
        low = decays - high - middle
        rows = sent[0].shape[0] - cells
        parts = [high, middle, low, jnp.zeros((rows - 3 * frames, channels), F32)]
        parts = jnp.concatenate(parts).astype(BF16)
        for k in range(2 * clips):
            if PEERS[k] // clips == second:
                sent[k][cells:] = parts
    for k in range(2 * clips):
        copy_of(rgb_ref, k).wait()


def clips_to_devices(rgb_maps, flow_maps, decay, place):
    clips, frames, side, _, channels = rgb_maps.shape
    cells = frames * side * side
    hbm = pl.BlockSpec(memory_space=pltpu.HBM)
    sent = pl.pallas_call(
        pack_kernel,
        out_shape=[jax.ShapeDtypeStruct((cells + 16, channels), BF16)] * (2 * clips),
        in_specs=[pl.BlockSpec(memory_space=pltpu.SMEM), hbm, hbm, hbm],
        out_specs=[pl.BlockSpec(memory_space=pltpu.VMEM)] * (2 * clips),
        scratch_shapes=[
            pltpu.VMEM(decay.shape, F32),
            pltpu.SemaphoreType.DMA((2 * clips,)),
            pltpu.SemaphoreType.DMA,
        ],
        compiler_params=pltpu.CompilerParams(vmem_limit_bytes=16 << 20),
    )(place, *(in_hbm(maps.reshape(clips, cells, channels)) for maps in (rgb_maps, flow_maps)), in_hbm(decay))
    peers = 2 * clips
    return [sent[0]] + [lax.ppermute(sent[k], TIME, [(i, i ^ PEERS[k]) for i in range(peers)]) for k in range(1, peers)]


def batch_norm(values):
    centered = values - jnp.mean(values, axis=0, keepdims=True)
    scale = lax.rsqrt(jnp.mean(centered * centered, axis=0, keepdims=True) + EPSILON)
    return centered * scale, scale


def norm_back(grad, normed, scale):
    mean = jnp.mean(grad, axis=0, keepdims=True)
    along = jnp.mean(grad * normed, axis=0, keepdims=True)
    return (grad - mean - normed * along) * scale


def across(a, b, **kinds):
    return lax.dot_general(a, b, (((1,), (1,)), ((), ())), preferred_element_type=F32, **kinds)


def projector_kernel(place_ref, seen_ref, in_ref, gain_ref, far_ref, dpool_ref, x_ref, n_ref, z_ref, zn_ref, out_ref, sems, *, cell_count):
    view, row = place_ref[1], place_ref[4]
    clips = seen_ref.shape[1]
    chunk = out_ref.shape[1] // CHUNKS
    columns = [slice(j * chunk, (j + 1) * chunk) for j in range(CHUNKS)]
    copies = [pltpu.make_async_copy(far_ref.at[:, c], out_ref.at[:, c], sems.at[j]) for j, c in enumerate(columns)]
    for copy in copies:
        copy.start()
    gain = gain_ref[...]
    pooled = jnp.concatenate([seen_ref[0] + seen_ref[3], seen_ref[1] + seen_ref[2]]) / cell_count
    hidden = jnp.dot(pooled, in_ref[...], precision=HIGHEST, preferred_element_type=F32)
    hidden_s, relus = [], []
    for v in range(2):
        x_ref[v], scale = batch_norm(hidden[v * clips : (v + 1) * clips])
        n_ref[v] = x_ref[v] * gain
        hidden_s.append(scale)
        relus.append(jnp.maximum(n_ref[v], 0.0).astype(BF16))
    relu_b = jnp.concatenate(relus)
    scales = []
    for copy, c in zip(copies, columns):
        copy.wait()
        z = jnp.dot(relu_b, out_ref[:, c], preferred_element_type=F32)
        for v in range(2):
            z_ref[v, :, c], scale = batch_norm(z[v * clips : (v + 1) * clips])
            zn_ref[v, :, c] = z_ref[v, :, c].astype(BF16)
            scales.append(scale)
    z_s = [jnp.concatenate(scales[v::2], axis=1) for v in range(2)]
    first = view == 0
    own, other = zn_ref[view].astype(F32), zn_ref[1 - view].astype(F32)
    corr_diag = jnp.sum(own * other, axis=0, keepdims=True) / clips
    extra = -2.0 * (1.0 - corr_diag) - 2.0 * LAMBDA_OFF * corr_diag
    gram = across(zn_ref[1 - view], zn_ref[1 - view])
    spread = jnp.dot(gram, own, precision=HIGHEST, preferred_element_type=F32)
    dzn = spread * (2.0 * LAMBDA_OFF / (clips * clips)) + other * (extra / clips)
    dz_b = norm_back(dzn, z_ref[view], jnp.where(first, z_s[0], z_s[1])).astype(BF16)
    dxh = jnp.where(n_ref[view] > 0, across(dz_b, out_ref[...]), 0.0) * gain
    dhidden = norm_back(dxh, x_ref[view], jnp.where(first, hidden_s[0], hidden_s[1]))
    mine = lax.broadcasted_iota(jnp.int32, dhidden.shape, 0) == row
    own_row = jnp.sum(jnp.where(mine, dhidden, 0.0), axis=0, keepdims=True)
    channels, width = in_ref.shape
    part = in_ref[:, :channels] * own_row[:, :channels]
    for k in range(channels, width, channels):
        part = part + in_ref[:, k : k + channels] * own_row[:, k : k + channels]
    dpool_ref[...] = jnp.sum(part.T, axis=0, keepdims=True) / cell_count


def projector_back(seen, proj_in, proj_gain, proj_out, place, cell_count):
    _, clips, channels = seen.shape
    width = proj_in.shape[1]
    wide = (2, clips, width)
    return pl.pallas_call(
        functools.partial(projector_kernel, cell_count=cell_count),
        out_shape=jax.ShapeDtypeStruct((1, channels), F32),
        in_specs=[pl.BlockSpec(memory_space=pltpu.SMEM)]
        + [pl.BlockSpec(memory_space=pltpu.VMEM)] * 3
        + [pl.BlockSpec(memory_space=pltpu.HBM)],
        scratch_shapes=[
            pltpu.VMEM(wide, F32),
            pltpu.VMEM(wide, F32),
            pltpu.VMEM(wide, F32),
            pltpu.VMEM(wide, BF16),
            pltpu.VMEM(proj_out.shape, BF16),
            pltpu.SemaphoreType.DMA((CHUNKS,)),
        ],
        cost_estimate=pl.CostEstimate(flops=6 * clips * width * width, transcendentals=0, bytes_accessed=2 * width * width),
        compiler_params=pltpu.CompilerParams(vmem_limit_bytes=26 << 20),
    )(place, seen, proj_in, proj_gain.reshape(1, width), in_hbm(proj_out))


def from_other_half(x):
    return lax.ppermute(x, PLANE, [(0, 3), (1, 2), (2, 1), (3, 0)])


def from_peer(x, axes, k):
    return lax.ppermute(x, axes, [(i, i ^ k) for i in range(4)])


def from_ring(x, axes):
    return [x] + [from_peer(x, axes, k) for k in (1, 2, 3)]


def total_of(arrays):
    return sum(a.astype(F32) for a in arrays)


def place_kernel(place_ref, *refs):
    view, core, ring = place_ref[1], place_ref[2], place_ref[3]
    outs, (whole_ref, sems) = refs[8:10], refs[10:]
    copies = []
    for n, out in enumerate(outs):
        for v in range(2):
            for shift, pieces in enumerate((refs[:4], refs[4:8])):
                for k, piece in enumerate(pieces):
                    rows = piece.shape[2]
                    start = pl.multiple_of((4 * (core ^ shift) + (ring ^ k)) * rows, rows)
                    whole_ref[n, v, pl.ds(start, rows)] = piece[n, v].astype(F32)
            copies.append(pltpu.make_async_copy(whole_ref.at[n, v], out.at[view ^ v], sems.at[n, v]))
            copies[-1].start()
    for copy in copies:
        copy.wait()


def summed(grads, place):
    taps, channels = grads[0].shape
    core, ring = lax.axis_index("core"), lax.axis_index("z")
    halves = jnp.stack(grads).reshape(len(grads), 2, 4, taps // 8, channels)
    mine = lax.dynamic_index_in_dim(halves, core, 1, False)
    given = lax.dynamic_index_in_dim(halves, 1 - core, 1, False)
    pieces = (mine + swapped(given)).astype(BF16)
    parts = [lax.dynamic_index_in_dim(pieces, ring, 1, False)]
    parts += [from_peer(lax.dynamic_index_in_dim(pieces, ring ^ k, 1, False), "z", k) for k in (1, 2, 3)]
    parts = from_ring(total_of(parts).astype(BF16), "y")
    parts = from_ring(total_of(parts).astype(BF16), PLANE)
    both = jnp.stack([total_of([parts[0], parts[3]]), total_of([parts[1], parts[2]])], axis=1).astype(BF16)
    mine = from_ring(both, "z")
    given = [swapped(a) for a in mine]
    whole = pltpu.HBM((2, taps, channels), F32)
    return tuple(
        pl.pallas_call(
            place_kernel,
            out_shape=[whole] * len(grads),
            in_specs=[pl.BlockSpec(memory_space=pltpu.SMEM)] + [pl.BlockSpec(memory_space=pltpu.VMEM)] * 8,
            out_specs=[pl.BlockSpec(memory_space=pltpu.HBM)] * len(grads),
            scratch_shapes=[pltpu.VMEM((len(grads), 2, taps, channels), F32), pltpu.SemaphoreType.DMA((len(grads), 2))],
            compiler_params=pltpu.CompilerParams(vmem_limit_bytes=16 << 20),
        )(place, *mine, *given)
    )


def per_device(
    rgb_maps, flow_maps, in_weights, out_weights, decay, skip, proj_in, proj_gain, proj_out
):
    half = lax.axis_index("xh")
    view = lax.axis_index("xl") ^ half
    _, frames_here, side, _, channels = rgb_maps.shape
    place = jnp.stack([half, view, lax.axis_index("core"), lax.axis_index("z"), lax.axis_index(("y", "z", "core")), lax.axis_index(TIME), lax.axis_index("y")])
    place = place.astype(jnp.int32)
    pieces = clips_to_devices(rgb_maps, flow_maps, decay, place)
    senders = len(pieces)
    cell_count = 2 * senders * frames_here * side * side
    plan = Plan(senders, frames_here, side, channels)
    skips = skip.reshape(2, 1, channels)
    here = plan.frames
    both = plan.small(pair_kernel, 2, jax.ShapeDtypeStruct((12 * channels, 2 * channels), BF16))(place, in_weights)
    piece_of = jax.ShapeDtypeStruct((frames_here, *plan.map), BF16)
    convolved = [plan.small(piece_kernel, 2, piece_of, plan.cols()[:1], False)(piece, both) for piece in pieces]
    inputs, decays, end = plan.small(gather_kernel, 17, [plan.maps_of(BF16), plan.decays_of(), plan.carry_of()])(
        place, *pieces, *convolved
    )
    got = plan.small(order_kernel, 9, jax.ShapeDtypeStruct((senders, *pieces[0].shape), BF16))(place, *pieces)
    income = from_other_half(end)
    states_b, slope, pooled_part = plan.call(
        mixed_step,
        False,
        [here, 2, None, "view", "view"],
        [plan.maps_of(BF16), plan.maps_of(F32), jax.ShapeDtypeStruct((1, channels), F32)],
        [here, here, None],
        [*plan.cols(), plan.both(), plan.carry(), pltpu.VMEM((side, channels), F32)],
        kept=(0, 1),
    )(place, inputs, decays, income, skips, out_weights)

    seen = from_all(from_cores(pooled_part[0]), ("xh", "xl", "y", "z"))
    dpool = projector_back(seen.reshape(4, -1, channels), proj_in, proj_gain, proj_out, place, cell_count)

    dmix_b, source, end = plan.call(
        from_out_step,
        True,
        [here, 2, None, "view"],
        [plan.maps_of(BF16), plan.maps_of(F32), plan.carry_of()],
        [here, here, None],
        [*plan.cols(), plan.both(), plan.carry()],
    )(place, slope, decays, dpool, out_weights)
    income = from_other_half(end)
    (out_grad,) = plan.call(
        out_grad_step,
        False,
        [here, here],
        [plan.grad_of()],
        [None],
        [*plan.cols(), plan.acc()],
    )(place, states_b, dmix_b)
    (in_grad,) = plan.call(
        in_grad_step,
        True,
        [2, here, here, 2, None, None, "view"],
        [plan.grad_of()],
        [None],
        [*plan.cols(), plan.carry(), pltpu.VMEM((here, *plan.map), BF16), plan.acc()],
    )(place, got, slope, source, decays, income, dpool, skips)
    return summed([in_grad, out_grad], place)


def solution(mesh):
    finer = Mesh(mesh.devices.reshape(2, 2, 4, 4, 2), ("xh", "xl", "y", "z", "core"))
    frames = ("xh", "xl", "y")
    return jax.shard_map(
        per_device,
        mesh=finer,
        in_specs=(
            P(("z", "core"), frames, None, None, None),
            P(("z", "core"), frames, None, None, None),
            P(),
            P(),
            P(None, frames, None),
            P(),
            P(),
            P(),
            P(),
        ),
        out_specs=(P(), P()),
        check_vma=False,
    )
```
